32 devices in a mesh: fsdp: 8 (over y, x, core), seq: 4 (over z).
Axes of the slice: x: 2, y: 2, z: 4, core: 2. Of those that a mesh axis runs over, the one named last changes fastest.
Arguments:
- inputs: bfloat16 [24, 320, 1024], P('fsdp', 'seq'), may hold values from -6 to 6
- lengths: int32 [24], P('fsdp'), may hold values from 256 to 320, as said below
- cotangent: bfloat16 [24, 320, 1024], P('fsdp', 'seq'), may hold values from -6 to 6
- attn_gain: bfloat16 [1024], P('fsdp'), may hold values from 0.25 to 1.75
- attn_shift: bfloat16 [1024], P('fsdp'), may hold values from -1 to 1
- qkv_weight: bfloat16 [1024, 3072], P('fsdp'), may hold values from -0.1875 to 0.1875
- qv_bias: bfloat16 [2048], P('fsdp'), may hold values from -0.5 to 0.5
- proj_weight: bfloat16 [1024, 1024], P('fsdp'), may hold values from -1.5 to 1.5
- proj_bias: bfloat16 [1024], P('fsdp'), may hold values from -1 to 1
- mlp_gain: bfloat16 [1024], P('fsdp'), may hold values from 0.25 to 1.75
- mlp_shift: bfloat16 [1024], P('fsdp'), may hold values from -1 to 1
- up_weight: bfloat16 [1024, 4096], P('fsdp'), may hold values from -0.1875 to 0.1875
- up_bias: bfloat16 [4096], P('fsdp'), may hold values from -1 to 1
- down_weight: bfloat16 [4096, 1024], P('fsdp'), may hold values from -0.09375 to 0.09375
- down_bias: bfloat16 [1024], P('fsdp'), may hold values from -1 to 1
Outputs:
- output: bfloat16 [24, 320, 1024], P('fsdp', 'seq')
- input_grad: bfloat16 [24, 320, 1024], P('fsdp', 'seq')
- attn_gain_grad: float32 [1024], P('fsdp')
- attn_shift_grad: float32 [1024], P('fsdp')
- query_key_value_weight_gradient: float32 [1024, 3072], P('fsdp')
- qv_bias_grad: float32 [2048], P('fsdp')
- proj_weight_grad: float32 [1024, 1024], P('fsdp')
- proj_bias_grad: float32 [1024], P('fsdp')
- mlp_gain_grad: float32 [1024], P('fsdp')
- mlp_shift_grad: float32 [1024], P('fsdp')
- up_weight_grad: float32 [1024, 4096], P('fsdp')
- up_bias_grad: float32 [4096], P('fsdp')
- down_weight_grad: float32 [4096, 1024], P('fsdp')
- down_bias_grad: float32 [1024], P('fsdp')
The draws below stay inside these ranges and needn't reach their ends.
Inputs may be any that keep to these rules, and one draw needn't show every extreme that they name: `lengths`: valid slots of each sequence; slots at or past it are padding; some sequence is full and some has the fewest.
All inputs are finite; a program needn't handle non-finite values.
Results may differ from the reference program's by a relative error of at most 0.015.
Values may be sent and summed in bfloat16 or wider, within the bound.
No kernel may reach another device: no remote copies, remote signals or barrier semaphores. Data moves between devices by JAX's collectives and lax.ppermute only.
A program may use at most 192 MiB of HBM per device.

```python
import jax
import jax.numpy as jnp
from jax import lax

D = 1024
HEADS = 16
HEAD = 64
FF = 4096
SLOTS = 320
SEQ_DEV = 3
SEQS = 24


def draw_lengths(key, part):
    folded = jax.random.fold_in(key, 7)
    key_rest, key_full, key_short = jax.random.split(folded, 3)
    shortest = SLOTS - SLOTS // 5
    chosen = jax.random.randint(key_rest, (SEQS,), shortest, SLOTS + 1)
    full_at = jax.random.randint(key_full, (), 0, SEQS)
    short_at = (full_at + 1 + jax.random.randint(key_short, (), 0, SEQS - 1)) % SEQS
    places = jnp.arange(SEQS)
    chosen = jnp.where(places == short_at, shortest, chosen)
    chosen = jnp.where(places == full_at, SLOTS, chosen)
    return chosen.astype(jnp.int32)


def strengthened(result, key, source, target, blocks, factor):
    owner, partner = [(jnp.arange(result.shape[position]) // (result.shape[position] // blocks)).reshape([-1 if axis == position else 1 for axis in range(result.ndim)]) for position in (source, target)]
    chosen = jax.random.permutation(key, blocks)[partner]
    strong = (owner == chosen) | (owner == (partner + blocks // 2) % blocks)
    return jnp.where(strong, factor * result, result)


def block_levels(own_key, shape, cuts, low, top_value):
    level = 1.0
    for position, shards_of in cuts:
        steps = jax.random.uniform(jax.random.fold_in(jax.random.fold_in(own_key, 6), position), (shards_of,), jnp.float32, low / len(cuts), top_value / len(cuts))
        level = level * jnp.repeat(jnp.exp(steps), shape[position] // shards_of).reshape((-1,) + (1,) * (len(shape) - 1 - position))
    return level


def bell_draw(key, extent, scale, bound, pieces=(), kind=jnp.bfloat16):
    level = block_levels(key, extent, pieces, -0.22, 0.18) if pieces else 1.0
    array = jax.random.normal(key, extent, jnp.float32) * scale * level
    return jnp.minimum(jnp.maximum(array, -bound), bound).astype(kind)


def noise_with(key, extent, width, bound, cuts, heavy, held_as=jnp.bfloat16):
    result = width * jax.random.normal(key, extent, jnp.float32)
    if cuts:
        result = result * block_levels(key, extent, cuts, -0.22, 0.18)
    return jnp.clip(strengthened(result, jax.random.fold_in(key, 3), *heavy), -bound, bound).astype(held_as)


def setup_inputs(seed: int = 0) -> dict:
    keys = jax.random.split(jax.random.key(seed), 16)
    inputs = bell_draw(keys[0], (SEQS, SLOTS, D), 1.0, 6.0, ((0, 8), (1, 4)))
    lengths = draw_lengths(jax.random.fold_in(keys[15], 71), 0)
    cotangent = noise_with(keys[2], (SEQS, SLOTS, D), 1.0, 6.0, ((0, 8), (1, 4)), (0, 2, 8, 2.0))
    attn_gain = jnp.clip(1.0 + 0.15 * jax.random.normal(keys[3], (D,), jnp.float32), 0.25, 1.75).astype(jnp.bfloat16)
    attn_shift = bell_draw(keys[4], (D,), 0.2, 1.0, ((0, 8),))
    qkv_weight = bell_draw(keys[5], (D, 3 * D), D ** -0.5, 0.1875, ((0, 8),))
    qv_bias = bell_draw(keys[6], (2 * D,), 0.1, 0.5, ((0, 8),))
    proj_weight = bell_draw(keys[7], (D, D), (D // 64) ** -0.5, 1.5, ((0, 8),))
    proj_bias = bell_draw(keys[8], (D,), 0.2, 1.0, ((0, 8),))
    mlp_gain = jnp.clip(1.0 + 0.15 * jax.random.normal(keys[9], (D,), jnp.float32), 0.25, 1.75).astype(jnp.bfloat16)
    mlp_shift = bell_draw(keys[10], (D,), 0.2, 1.0, ((0, 8),))
    up_weight = bell_draw(keys[11], (D, FF), D ** -0.5, 0.1875, ((0, 8),))
    up_bias = bell_draw(keys[12], (FF,), 0.2, 1.0, ((0, 8),))
    down_weight = bell_draw(keys[13], (FF, D), FF ** -0.5, 0.09375, ((0, 8),))
    down_bias = bell_draw(keys[14], (D,), 0.2, 1.0, ((0, 8),))
    return {"inputs": inputs, "lengths": lengths, "cotangent": cotangent, "attn_gain": attn_gain, "attn_shift": attn_shift, "qkv_weight": qkv_weight, "qv_bias": qv_bias, "proj_weight": proj_weight, "proj_bias": proj_bias, "mlp_gain": mlp_gain, "mlp_shift": mlp_shift, "up_weight": up_weight, "up_bias": up_bias, "down_weight": down_weight, "down_bias": down_bias}


EPSILON = 1e-06
MASKED = -1e+30

@jax.custom_vjp
def low(v):
    return lax.optimization_barrier(v.astype(jnp.bfloat16)).astype(jnp.float32)

@jax.custom_vjp
def low_back(v):
    return v

def low_keep(v):
    return (low(v), None)

def low_pass(kept, grad):
    return (grad,)

def back_keep(v):
    return (v, None)

def back_low(kept, grad):
    return (low(grad),)
low.defvjp(low_keep, low_pass)
low_back.defvjp(back_keep, back_low)

def normalize(value_entries):
    center = value_entries - lax.optimization_barrier(jnp.mean(value_entries, axis=-1, keepdims=True))
    return center * lax.rsqrt(lax.optimization_barrier(jnp.mean(center * center, axis=-1, keepdims=True)) + EPSILON)

def matmul_high(form, left, right):
    return jnp.einsum(form, left, right, precision=lax.Precision.HIGHEST)

def forward(value_entries, seq_lengths, params):
    attn_gain, attn_shift, qkv_weight, qv_bias, proj_weight, proj_bias, mlp_gain, mlp_shift, up_weight, up_bias, down_weight, down_bias = params
    group_size = value_entries.shape[0]
    slot_valid = jnp.arange(SLOTS, dtype=jnp.int32)[None, :] < seq_lengths[:, None]
    row_valid_mask = slot_valid.astype(value_entries.dtype)[:, :, None]
    normed_attn = low(normalize(value_entries) * attn_gain + attn_shift)
    complete_bias = jnp.concatenate([qv_bias[:D], jnp.zeros((D,), value_entries.dtype), qv_bias[D:]])
    query_key_value_rows = low(low_back(matmul_high('gtd,de->gte', normed_attn, qkv_weight) + complete_bias))
    query_key_value_rows = query_key_value_rows.reshape(group_size, SLOTS, 3, HEADS, HEAD)
    queries = query_key_value_rows[:, :, 0]
    key_rows = query_key_value_rows[:, :, 1]
    value_rows = query_key_value_rows[:, :, 2]
    scores = low_back(matmul_high('gqhe,gkhe->ghqk', queries, key_rows)) * HEAD ** (-0.5)
    scores = jnp.where(slot_valid[:, None, None, :], scores, MASKED)
    row_max = lax.optimization_barrier(jnp.max(scores, axis=-1, keepdims=True))
    exponent = jnp.exp(scores - row_max)
    probs = exponent / lax.optimization_barrier(jnp.sum(exponent, axis=-1, keepdims=True))
    context = matmul_high('ghqk,gkhe->gqhe', low(probs), value_rows).reshape(group_size, SLOTS, D)
    context = low(low_back(context))
    hidden_activations = value_entries + low_back(matmul_high('gtd,de->gte', context, proj_weight) + proj_bias)
    normed_mlp = low(normalize(hidden_activations) * mlp_gain + mlp_shift)
    preactivation_values = low_back(matmul_high('gtd,df->gtf', normed_mlp, up_weight) + up_bias)
    activation = low(jax.nn.gelu(preactivation_values))
    return row_valid_mask * (hidden_activations + matmul_high('gtf,fd->gtd', activation, down_weight) + down_bias)

def reference(inputs, lengths, cotangent, attn_gain, attn_shift, qkv_weight, qv_bias, proj_weight, proj_bias, mlp_gain, mlp_shift, up_weight, up_bias, down_weight, down_bias):
    params = tuple((member.astype(jnp.float32) for member in (attn_gain, attn_shift, qkv_weight, qv_bias, proj_weight, proj_bias, mlp_gain, mlp_shift, up_weight, up_bias, down_weight, down_bias)))
    blocks = SEQS // SEQ_DEV

    def step(carry, block):
        block_inputs, block_lengths, block_cot = block
        result_rows, pull = jax.vjp(lambda block_rows, weights: forward(block_rows, block_lengths, weights), block_inputs.astype(jnp.float32), params)
        input_grad, weight_grads = pull(block_cot.astype(jnp.float32))
        carry = jax.tree.map(jnp.add, carry, weight_grads)
        return (carry, (result_rows.astype(jnp.bfloat16), input_grad.astype(jnp.bfloat16)))
    start_carry = tuple((jnp.zeros_like(member) for member in params))
    stacked = (inputs.reshape(blocks, SEQ_DEV, SLOTS, D), lengths.reshape(blocks, SEQ_DEV), cotangent.reshape(blocks, SEQ_DEV, SLOTS, D))
    totals, (rows_out, grads_out) = lax.scan(step, start_carry, stacked)
    return (rows_out.reshape(SEQS, SLOTS, D), grads_out.reshape(SEQS, SLOTS, D), totals[0], totals[1], totals[2], totals[3], totals[4], totals[5], totals[6], totals[7], totals[8], totals[9], totals[10], totals[11])
```

```python
import functools
import math

import jax
import jax.numpy as jnp
from jax import lax
from jax.experimental import pallas as pl
from jax.experimental.pallas import tpu as pltpu
from jax.sharding import PartitionSpec as P

HEAD = 64
EPSILON = 1e-06
MASKED = -1e30
TEAM = 8
ZS = 4
F32 = jnp.float32
BF16 = jnp.bfloat16
VMEM_BYTES = 56 * 1024 * 1024


def params():
    return pltpu.CompilerParams(vmem_limit_bytes=VMEM_BYTES)


def cost(flops, nbytes, trans=0):
    return pl.CostEstimate(flops=int(flops), bytes_accessed=int(nbytes), transcendentals=int(trans))


def whole():
    return pl.BlockSpec(memory_space=pltpu.VMEM)


def shape_of(dims, dtype):
    return jax.ShapeDtypeStruct(dims, dtype)


def mm(left, right):
    return lax.dot_general(left, right, (((1,), (0,)), ((), ())), preferred_element_type=F32)


def mm_rt(left, right):
    return lax.dot_general(left, right, (((1,), (1,)), ((), ())), preferred_element_type=F32)


def mm_lt(left, right):
    return lax.dot_general(left, right, (((0,), (0,)), ((), ())), preferred_element_type=F32)


def normalize(rows):
    center = rows - jnp.mean(rows, axis=-1, keepdims=True)
    inverse = lax.rsqrt(jnp.mean(center * center, axis=-1, keepdims=True) + EPSILON)
    return center * inverse, inverse


def norm_back(upstream, unit, inverse, gain):
    scaled = upstream * gain
    return inverse * (
        scaled
        - jnp.mean(scaled, axis=-1, keepdims=True)
        - unit * jnp.mean(scaled * unit, axis=-1, keepdims=True)
    )


def swap(value, mask):
    size = lax.axis_size("fsdp")
    return lax.ppermute(value, "fsdp", [(i, i ^ mask) for i in range(size)])


def shift(value, by):
    return lax.ppermute(value, "seq", [(i, (i + by) % ZS) for i in range(ZS)])


def pick(stack, index, axis=0):
    return lax.dynamic_index_in_dim(stack, index, axis, keepdims=False)


def line_sum(value, z):
    gathered = lax.ppermute(value, "seq", [(0, 1), (3, 2)])
    half = lax.optimization_barrier((value.astype(F32) + gathered.astype(F32)).astype(BF16))
    other = lax.ppermute(half, "seq", [(1, 2), (2, 1)])
    total = lax.optimization_barrier((half.astype(F32) + other.astype(F32)).astype(BF16))
    back = lax.ppermute(total, "seq", [(1, 0), (2, 3)])
    return jnp.where((z == 1) | (z == 2), total, back)


def outer_groups(size):
    outer = size // TEAM
    return [[o * TEAM + t for o in range(outer)] for t in range(TEAM)]


def rows_over_outer(value, size):
    if size == TEAM:
        return value
    return lax.psum_scatter(
        value, "fsdp", scatter_dimension=0, axis_index_groups=outer_groups(size), tiled=True
    )


def gather_over_outer(value, size):
    if size == TEAM:
        return value
    return lax.all_gather(value, "fsdp", axis=0, axis_index_groups=outer_groups(size), tiled=True)


def valid_keys(z, length, slots, local):
    lane = lax.broadcasted_iota(jnp.int32, (1, slots), 1)
    block = jnp.zeros((1, slots), jnp.int32)
    for k in range(1, ZS):
        block = block + (lane >= k * local).astype(jnp.int32)
    slot = (z - block) & (ZS - 1)
    return slot * local + lane - block * local < length


def head_probs(queries, keys, valid):
    scores = mm_rt(queries, keys) * HEAD ** (-0.5)
    scores = jnp.where(valid, scores, MASKED)
    exponent = jnp.exp(scores - jnp.max(scores, axis=-1, keepdims=True))
    return exponent * (1.0 / jnp.sum(exponent, axis=-1, keepdims=True))


def attend_kernel(meta, x0, x1, x2, x3, wq, wk, wv, gain, shift_row, bias, qkv_ref, normed_ref, c0, c1, c2, c3):
    local = x0.shape[1]
    slots = ZS * local
    width = wq.shape[1]
    rows = jnp.concatenate([x[0].astype(F32) for x in (x0, x1, x2, x3)], axis=0)
    unit, _ = normalize(rows)
    normed = (unit * gain[...] + shift_row[...]).astype(BF16)
    normed_ref[0] = normed
    parts = []
    for i, w in enumerate((wq, wk, wv)):
        part = (mm(normed, w[...]) + bias[:, i * width : (i + 1) * width]).astype(BF16)
        qkv_ref[0, :, i * width : (i + 1) * width] = part
        parts.append(part)
    length = meta[pl.program_id(0)]
    z = meta[meta.shape[0] - 1]
    valid = valid_keys(z, length, slots, local)
    first = lax.broadcasted_iota(jnp.int32, (1, 2 * HEAD), 1) < HEAD
    for pair in range(width // (2 * HEAD)):
        lanes = slice(pair * 2 * HEAD, (pair + 1) * 2 * HEAD)
        queries, keys, values = (part[:, lanes] for part in parts)
        outs = []
        for mine in (first, ~first):
            probs = head_probs(jnp.where(mine, queries, jnp.zeros_like(queries)), keys, valid)
            outs.append(mm(probs.astype(BF16), values))
        context = jnp.where(first, outs[0], outs[1]).astype(BF16)
        for k, out in enumerate((c0, c1, c2, c3)):
            out[0, :, lanes] = context[k * local : (k + 1) * local]


def attend(meta, blocks, weights, gain, shift_row, bias):
    count, local, model = blocks[0].shape
    slots, width = ZS * local, model // ZS
    seq_spec = pl.BlockSpec((1, local, model), lambda s, m: (s, 0, 0))
    first = model // width
    weight_specs = [
        pl.BlockSpec((model, width), functools.partial(lambda i, s, m: (0, i), first + i)) for i in range(3)
    ]
    row = pl.BlockSpec((1, model), lambda s, m: (0, 0))
    flops = count * (2 * slots * model * 3 * width + 8 * slots * slots * width)
    return pl.pallas_call(
        attend_kernel,
        name="attend",
        grid_spec=pltpu.PrefetchScalarGridSpec(
            num_scalar_prefetch=1,
            grid=(count,),
            in_specs=[seq_spec] * ZS
            + weight_specs
            + [row, row, pl.BlockSpec((1, 3 * width), lambda s, m: (0, 0))],
            out_specs=[
                pl.BlockSpec((1, slots, 3 * width), lambda s, m: (s, 0, 0)),
                pl.BlockSpec((1, slots, model), lambda s, m: (s, 0, 0)),
            ]
            + [pl.BlockSpec((1, local, width), lambda s, m: (s, 0, 0))] * ZS,
        ),
        out_shape=[
            shape_of((count, slots, 3 * width), BF16),
            shape_of((count, slots, model), BF16),
        ]
        + [shape_of((count, local, width), BF16)] * ZS,
        compiler_params=params(),
        cost_estimate=cost(flops, 2 * count * slots * (2 * model + 4 * width) + 6 * model * width),
    )(meta, *blocks, weights, weights, weights, gain, shift_row, bias)


def attend_back_kernel(meta, x0, x1, x2, x3, d0, d1, d2, d3, qkv_ref, wq, wk, wv, dqkv_ref, p0, p1, p2, p3, sums_ref):
    local = x0.shape[1]
    slots = ZS * local
    width = wq.shape[1]
    model = wq.shape[0]
    upstream = jnp.concatenate([d[0] for d in (d0, d1, d2, d3)], axis=0)
    length = meta[pl.program_id(0)]
    z = meta[meta.shape[0] - 1]
    valid = valid_keys(z, length, slots, local)
    first = lax.broadcasted_iota(jnp.int32, (1, 2 * HEAD), 1) < HEAD
    for pair in range(width // (2 * HEAD)):
        spans = [slice(i * width + pair * 2 * HEAD, i * width + (pair + 1) * 2 * HEAD) for i in range(3)]
        queries, keys, values = (qkv_ref[0, :, span] for span in spans)
        above = upstream[:, spans[0]]
        grads = []
        for mine in (first, ~first):
            probs = head_probs(jnp.where(mine, queries, jnp.zeros_like(queries)), keys, valid)
            probs_grad = mm_rt(jnp.where(mine, above, jnp.zeros_like(above)), values)
            inner = jnp.sum(probs * probs_grad, axis=-1, keepdims=True)
            scores_grad = (probs * (probs_grad - inner) * HEAD ** (-0.5)).astype(BF16)
            grads.append(
                (mm(scores_grad, keys), mm_lt(scores_grad, queries), mm_lt(probs.astype(BF16), above))
            )
        for span, low, high in zip(spans, *grads):
            dqkv_ref[0, :, span] = jnp.where(first, low, high).astype(BF16)
    grad = dqkv_ref[0]
    total = mm_rt(grad[:, :width], wq[...])
    total = total + mm_rt(grad[:, width : 2 * width], wk[...])
    total = total + mm_rt(grad[:, 2 * width :], wv[...])
    for k, out in enumerate((p0, p1, p2, p3)):
        out[0] = total[k * local : (k + 1) * local].astype(BF16)
    rows = jnp.concatenate([x[0].astype(F32) for x in (x0, x1, x2, x3)], axis=0)
    unit, _ = normalize(rows)
    sums_ref[0] = jnp.zeros(sums_ref.shape[1:], F32)
    sums_ref[0, 0:1, :] = jnp.sum(total * unit, axis=0, keepdims=True)
    sums_ref[0, 1:2, :] = jnp.sum(total, axis=0, keepdims=True)
    sums_ref[0, 2:3, : 3 * width] = jnp.sum(grad.astype(F32), axis=0, keepdims=True)


def attend_back(meta, blocks, upstream, qkv, weights):
    count, local, model = blocks[0].shape
    slots, width = ZS * local, model // ZS
    first = model // width
    weight_specs = [
        pl.BlockSpec((model, width), functools.partial(lambda i, s, m: (0, i), first + i)) for i in range(3)
    ]
    wide = pl.BlockSpec((1, local, model), lambda s, m: (s, 0, 0))
    thin = pl.BlockSpec((1, local, width), lambda s, m: (s, 0, 0))
    packed = pl.BlockSpec((1, slots, 3 * width), lambda s, m: (s, 0, 0))
    flops = count * (2 * slots * model * 3 * width + 20 * slots * slots * width)
    return pl.pallas_call(
        attend_back_kernel,
        name="attend_back",
        grid_spec=pltpu.PrefetchScalarGridSpec(
            num_scalar_prefetch=1,
            grid=(count,),
            in_specs=[wide] * ZS + [thin] * ZS + [packed] + weight_specs,
            out_specs=[packed] + [wide] * ZS + [pl.BlockSpec((1, 8, model), lambda s, m: (s, 0, 0))],
        ),
        out_shape=[shape_of((count, slots, 3 * width), BF16)]
        + [shape_of((count, local, model), BF16)] * ZS
        + [shape_of((count, 8, model), F32)],
        compiler_params=params(),
        cost_estimate=cost(flops, 2 * count * slots * (2 * model + 7 * width) + 6 * model * width),
    )(meta, *blocks, *upstream, qkv, weights, weights, weights)


def project_kernel(meta, c0, c1, c2, c3, x, weights, bias, gain, shift_row, hidden_ref, normed_ref):
    width = c0.shape[1]
    model = x.shape[1]
    z = meta[0]
    hidden = x[...].astype(F32) + bias[...]
    for k, part in enumerate((c0, c1, c2, c3)):
        start = pl.multiple_of(((z + k) & (ZS - 1)) * width, width)
        hidden = hidden + mm(part[...], weights[pl.ds(start, width), :])
    hidden_ref[...] = hidden
    unit, _ = normalize(hidden)
    normed_ref[...] = (unit * gain[...] + shift_row[...]).astype(BF16)


def project(z, parts, x, weights, bias, gain, shift_row):
    rows, model = x.shape
    width = parts[0].shape[1]
    whole_block = lambda dims: pl.BlockSpec(dims, lambda i, m: (0,) * len(dims))
    return pl.pallas_call(
        project_kernel,
        name="project",
        grid_spec=pltpu.PrefetchScalarGridSpec(
            num_scalar_prefetch=1,
            grid=(1,),
            in_specs=[whole_block((rows, width))] * ZS
            + [whole_block((rows, model)), whole_block((model, model))]
            + [whole_block((1, model))] * 3,
            out_specs=[whole_block((rows, model))] * 2,
        ),
        out_shape=[shape_of((rows, model), F32), shape_of((rows, model), BF16)],
        compiler_params=params(),
        cost_estimate=cost(2 * rows * model * model, rows * model * 10 + 2 * model * model),
    )(z.reshape(1), *parts, x, weights, bias, gain, shift_row)


def feed_kernel(halves, *refs):
    count = len(halves)
    taken = 0
    pieces = []
    for split in halves:
        if split:
            pieces.append(jnp.concatenate([refs[taken][...], refs[taken + 1][...]], axis=1))
            taken += 2
        else:
            pieces.append(refs[taken][...])
            taken += 1
    above = refs[taken : taken + count]
    up, bias = refs[taken + count], refs[taken + count + 1]
    outs = refs[taken + count + 2 :]
    rows = pieces[0].shape[0]
    normed = jnp.concatenate(pieces, axis=0)
    value = mm(normed, up[...]) + bias[...]
    square = value * value
    root = math.sqrt(2.0 / math.pi)
    bend = jnp.tanh(root * value * (1.0 + 0.044715 * square))
    activation = (0.5 * value * (1.0 + bend)).astype(BF16)
    slope = 0.5 * (1.0 + bend) + 0.5 * value * (1.0 - bend * bend) * root * (1.0 + 3 * 0.044715 * square)
    grad = jnp.concatenate([a[0] for a in above], axis=0) * slope
    grad = grad.astype(BF16)
    back = mm_rt(grad, up[...]).astype(BF16)
    for i in range(count):
        span = slice(i * rows, (i + 1) * rows)
        outs[i][...] = activation[span]
        outs[count + i][...] = grad[span]
        outs[2 * count + i][...] = back[span]


def feed(pieces, above, places, up, bias):
    model, width = up.shape
    rows = above.shape[1]
    step = 80 if rows % 80 == 0 else rows
    halves = tuple(isinstance(piece, tuple) for piece in pieces)
    args, specs = [], []
    for piece in pieces:
        for part in piece if isinstance(piece, tuple) else (piece,):
            args.append(part)
            specs.append(pl.BlockSpec((step, part.shape[1]), lambda i: (i, 0)))
    for place in places:
        args.append(above)
        specs.append(pl.BlockSpec((1, step, width), functools.partial(lambda p, i: (p, i, 0), place)))
    args += [up, bias]
    specs += [pl.BlockSpec((model, width), lambda i: (0, 0)), pl.BlockSpec((1, width), lambda i: (0, 0))]
    count = len(pieces)
    narrow = pl.BlockSpec((step, width), lambda i: (i, 0))
    outs = pl.pallas_call(
        functools.partial(feed_kernel, halves),
        name="feed",
        grid=(rows // step,),
        in_specs=specs,
        out_specs=[narrow] * (2 * count) + [pl.BlockSpec((step, model), lambda i: (i, 0))] * count,
        out_shape=[shape_of((rows, width), BF16)] * (2 * count) + [shape_of((rows, model), BF16)] * count,
        compiler_params=params(),
        cost_estimate=cost(
            count * rows * 4 * model * width,
            count * rows * (4 * model + 8 * width) + 2 * model * width,
            count * rows * width,
        ),
    )(*args)
    return outs[:count], outs[count : 2 * count], outs[2 * count :]


def middle_kernel(meta, g0, g1, gx, gy, gd, hidden, cot, weights, gain, hidden_grad_ref, grad_ref, d0, d1, d2, d3, sums_ref):
    width = d0.shape[1]
    z = meta[0]
    normed_grad = (g0[...].astype(F32) + g1[...].astype(F32)) + (gx[...].astype(F32) + gy[...].astype(F32))
    normed_grad = normed_grad + gd[...].astype(F32)
    unit, inverse = normalize(hidden[...])
    upstream = cot[...].astype(F32)
    hidden_grad = upstream + norm_back(normed_grad, unit, inverse, gain[...])
    hidden_grad_ref[...] = hidden_grad
    grad = hidden_grad.astype(BF16)
    grad_ref[...] = grad
    for k, out in enumerate((d0, d1, d2, d3)):
        start = pl.multiple_of(((z + k) & (ZS - 1)) * width, width)
        out[...] = mm_rt(grad, weights[pl.ds(start, width), :]).astype(BF16)
    sums_ref[0:1, :] = jnp.sum(normed_grad * unit, axis=0, keepdims=True)
    sums_ref[1:2, :] = jnp.sum(normed_grad, axis=0, keepdims=True)
    sums_ref[2:3, :] = jnp.sum(grad.astype(F32), axis=0, keepdims=True)
    sums_ref[3:4, :] = jnp.sum(upstream, axis=0, keepdims=True)


def middle(z, grads, hidden, cot, weights, gain):
    rows, model = hidden.shape
    width = model // ZS
    block = lambda dims: pl.BlockSpec(dims, lambda i, m: (0,) * len(dims))
    return pl.pallas_call(
        middle_kernel,
        name="middle",
        grid_spec=pltpu.PrefetchScalarGridSpec(
            num_scalar_prefetch=1,
            grid=(1,),
            in_specs=[block((rows, model))] * 7 + [block((model, model)), block((1, model))],
            out_specs=[block((rows, model))] * 2 + [block((rows, width))] * ZS + [block((4, model))],
        ),
        out_shape=[shape_of((rows, model), F32), shape_of((rows, model), BF16)]
        + [shape_of((rows, width), BF16)] * ZS
        + [shape_of((4, model), F32)],
        compiler_params=params(),
        cost_estimate=cost(2 * rows * model * model, rows * model * 26 + 2 * model * model),
    )(z.reshape(1), *grads, hidden, cot, weights, gain)


def finish_kernel(x, g0, g1, g2, g3, hidden_grad, gain, out):
    unit, inverse = normalize(x[...].astype(F32))
    upstream = (g0[...].astype(F32) + g1[...].astype(F32)) + (g2[...].astype(F32) + g3[...].astype(F32))
    out[...] = (hidden_grad[...] + norm_back(upstream, unit, inverse, gain[...])).astype(BF16)


def finish(x, grads, hidden_grad, gain):
    rows, model = x.shape
    return pl.pallas_call(
        finish_kernel,
        name="finish",
        in_specs=[whole()] * 7,
        out_specs=whole(),
        out_shape=shape_of((rows, model), BF16),
        compiler_params=params(),
        cost_estimate=cost(20 * rows * model, rows * model * 16),
    )(x, *grads, hidden_grad, gain)


def per_device(
    inputs,
    lengths,
    cotangent,
    attn_gain,
    attn_shift,
    qkv_weight,
    qv_bias,
    proj_weight,
    proj_bias,
    mlp_gain,
    mlp_shift,
    up_weight,
    up_bias,
    down_weight,
    down_bias,
):
    count, local, model = inputs.shape
    size = lax.axis_size("fsdp")
    outer = size // TEAM
    place = lax.axis_index("fsdp")
    z = lax.axis_index("seq").astype(jnp.int32)
    team = place % TEAM
    core = team % 2
    chip = team // 2
    tokens = count * local
    width = model // ZS
    own_rows = qkv_weight.shape[0]
    hidden_units = up_weight.shape[1]
    feed_width = hidden_units // TEAM

    blocks = [inputs] + [shift(inputs, k) for k in range(1, ZS)]

    quarter = pick(qkv_weight.reshape(own_rows, 3, ZS, width), z, 2).reshape(own_rows, 3 * width)
    weights = lax.all_gather(jnp.concatenate([proj_weight, quarter], axis=1), "fsdp", axis=0, tiled=True)
    vectors = (attn_gain, attn_shift, proj_bias, mlp_gain, mlp_shift, down_bias, qv_bias)
    small = lax.all_gather(jnp.concatenate(vectors), "fsdp", axis=0, tiled=False).astype(F32)
    edges = [0]
    for vector in vectors:
        edges.append(edges[-1] + vector.shape[0])
    gain_attn, shift_attn, bias_proj, gain_mlp, shift_mlp, bias_down, bias_qv = (
        small[:, a:b].reshape(1, -1) for a, b in zip(edges[:-1], edges[1:])
    )
    bias_quarter = jnp.concatenate(
        [
            lax.dynamic_slice(bias_qv, (0, z * width), (1, width)),
            jnp.zeros((1, width), F32),
            lax.dynamic_slice(bias_qv, (0, model + z * width), (1, width)),
        ],
        axis=1,
    )
    up_blocks = up_weight.reshape(own_rows, outer, TEAM, feed_width // outer).transpose(2, 0, 1, 3)
    up_blocks = up_blocks.reshape(TEAM, own_rows, feed_width)
    groups = [[o * TEAM + t for t in range(TEAM)] for o in range(outer)]
    up = lax.all_to_all(
        up_blocks, "fsdp", split_axis=0, concat_axis=0, axis_index_groups=groups, tiled=True
    ).reshape(TEAM * own_rows, feed_width)
    up = gather_over_outer(up, size)
    down = gather_over_outer(down_weight, size)
    bias_up = gather_over_outer(up_bias, size).astype(F32).reshape(1, feed_width)

    positions = z * local + jnp.arange(local, dtype=jnp.int32)
    row_valid = (positions[None, :] < lengths[:, None])[:, :, None]
    cot = jnp.where(row_valid, cotangent, jnp.zeros_like(cotangent)).reshape(tokens, model)
    half = model // 2
    cot_x, cot_y = swap(cot, 2), swap(cot, 4)
    cot_d = jnp.concatenate([swap(cot_x[:, :half], 4), swap(cot_y[:, half:], 2)], axis=1)
    cot_even = jnp.concatenate([cot, cot_x, cot_y, cot_d], axis=0)
    cot_all = jnp.concatenate([cot_even, swap(cot_even, 1)], axis=0)
    above = lax.dot_general(
        cot_all, down, (((1,), (1,)), ((), ())), preferred_element_type=F32
    ).reshape(TEAM, tokens, feed_width)

    meta = jnp.concatenate([lengths.astype(jnp.int32), z.reshape(1)])
    qkv, normed_attn, *context = attend(meta, blocks, weights, gain_attn, shift_attn, bias_quarter)
    context = [part.reshape(tokens, width) for part in context]
    context = [context[0]] + [shift(context[k], -k) for k in range(1, ZS)]

    own = inputs.reshape(tokens, model)
    hidden, normed = project(z, context, own, weights, bias_proj, gain_mlp, shift_mlp)

    right_x, right_y = swap(normed, 2), swap(normed, 4)
    core_own = swap(normed, 1)
    diag_a, diag_b = swap(right_x[:, :half], 4), swap(right_y[:, half:], 2)
    core_x, core_y = swap(right_x, 1), swap(right_y, 1)
    core_a, core_b = swap(diag_a, 1), swap(diag_b, 1)
    act0, grad0, back0 = feed([normed, core_own], above, (0, 4), up, bias_up)
    act1, grad1, back1 = feed([right_x, right_y, core_x, core_y], above, (1, 2, 5, 6), up, bias_up)
    act2, grad2, back2 = feed([(diag_a, diag_b), (core_a, core_b)], above, (3, 7), up, bias_up)
    from_core = [swap(b, 1) for b in (back0[1], back1[2], back1[3], back2[1])]

    def joined(first, second):
        return (first.astype(F32) + second.astype(F32)).astype(BF16)

    grad_x = swap(joined(back1[0], from_core[1]), 2)
    grad_y = swap(joined(back1[1], from_core[2]), 4)
    grad_d = swap(joined(back2[0], from_core[3]), 6)
    hidden_grad, attn_grad, *context_grad, mid_sums = middle(
        z, (back0[0], from_core[0], grad_x, grad_y, grad_d), hidden, cot, weights, gain_mlp
    )

    context_grad = [part.reshape(count, local, width) for part in context_grad]
    context_grad = [context_grad[0]] + [shift(context_grad[k], k) for k in range(1, ZS)]
    qkv_grad, *partial, attn_sums = attend_back(meta, blocks, context_grad, qkv, weights)
    partial = [part.reshape(tokens, model) for part in partial]
    partial = [partial[0]] + [shift(partial[k], -k) for k in range(1, ZS)]
    input_grad = finish(own, partial, hidden_grad, gain_attn).reshape(inputs.shape)

    act_even = jnp.concatenate([act0[0], act1[0], act1[1], act2[0]], axis=0)
    act_odd = jnp.concatenate([act0[1], act1[2], act1[3], act2[1]], axis=0)
    out_odd = mm(act_odd, down).astype(BF16)
    out_even = mm(act_even, down)
    out_even = (out_even + swap(out_odd, 1).astype(F32)).astype(BF16).reshape(4, tokens, model)
    moved = swap(out_even[1], 2).astype(F32) + swap(out_even[2], 4).astype(F32) + swap(out_even[3], 6).astype(F32)
    output = hidden + bias_down + out_even[0].astype(F32) + moved
    output = jnp.where(row_valid, output.reshape(inputs.shape), 0.0).astype(BF16)

    act_all = jnp.concatenate([act_even, act_odd], axis=0)
    grad_all = jnp.concatenate(
        [grad0[0], grad1[0], grad1[1], grad2[0], grad0[1], grad1[2], grad1[3], grad2[1]], axis=0
    )
    normed_all = jnp.concatenate(
        [
            normed,
            right_x,
            right_y,
            jnp.concatenate([diag_a, diag_b], axis=1),
            core_own,
            core_x,
            core_y,
            jnp.concatenate([core_a, core_b], axis=1),
        ],
        axis=0,
    )
    down_part = rows_over_outer(mm_lt(act_all, cot_all), size).astype(BF16)
    up_bias_part = rows_over_outer(jnp.sum(grad_all, axis=0, dtype=F32), size)
    up_bias_row = jnp.pad(up_bias_part.reshape(1, -1), ((0, 7), (0, model - up_bias_part.shape[0])))
    down_part = jnp.concatenate([down_part, up_bias_row.astype(BF16)], axis=0)
    down_total = line_sum(down_part, z).astype(F32)
    down_grad = down_total[: down_part.shape[0] - 8]
    up_bias_grad = down_total[down_part.shape[0] - 8, : up_bias_part.shape[0]]

    up_part = rows_over_outer(mm_lt(normed_all, grad_all), size).astype(BF16)
    up_part = up_part.reshape(4, 2, own_rows, feed_width)
    pair = jnp.stack([pick(up_part, core, 1), swap(pick(up_part, 1 - core, 1), 1)], axis=1)
    up_rel = jnp.stack([pick(pair, chip)] + [swap(pick(pair, chip ^ m), 2 * m) for m in (1, 2, 3)])
    up_rel = line_sum(up_rel.reshape(TEAM, own_rows, feed_width), z)
    up_grad = jnp.stack([pick(up_rel, j ^ team) for j in range(TEAM)], axis=1).astype(F32)
    up_grad = up_grad.reshape(own_rows, TEAM, outer, feed_width // outer).transpose(0, 2, 1, 3)
    up_grad = up_grad.reshape(own_rows, hidden_units)

    context_all = jnp.concatenate(context, axis=1)
    proj_part = mm_lt(context_all, attn_grad)
    qkv_grad = qkv_grad.reshape(count * ZS * local, 3 * width)
    qkv_part = mm_lt(normed_attn.reshape(count * ZS * local, model), qkv_grad)
    attn_sums = jnp.sum(attn_sums, axis=0)

    if outer == 1:
        proj_part = proj_part.astype(BF16).reshape(ZS, 2, own_rows, model)
        mid_rows = mid_sums.reshape(4, TEAM, own_rows).transpose(1, 0, 2).reshape(4, 2, 1, 4 * own_rows)
        mid_rows = jnp.pad(mid_rows, ((0, 0), (0, 0), (0, 7), (0, model - 4 * own_rows))).astype(BF16)
        mid_rows = jnp.stack([pick(mid_rows, (z + k) % ZS) for k in range(ZS)])
        proj_part = jnp.concatenate([proj_part, mid_rows], axis=2)
        chip_at = lambda m: ((chip ^ m) - z) % ZS
        qkv_part = qkv_part.astype(BF16).reshape(4, 2, own_rows, 3 * width)
        gains = attn_sums[:2].reshape(2, TEAM, own_rows).transpose(1, 0, 2).reshape(4, 2, 1, 2 * own_rows)
        biases = jnp.concatenate([attn_sums[2, :width], attn_sums[2, 2 * width : 3 * width]])
        biases = jnp.broadcast_to(biases, (4, 2, 1, 2 * width))
        rows = jnp.concatenate([gains, biases], axis=3)
        rows = jnp.pad(rows, ((0, 0), (0, 0), (0, 7), (0, 3 * width - rows.shape[3]))).astype(BF16)
        qkv_part = jnp.concatenate([qkv_part, rows], axis=2)
    else:
        proj_part = proj_part.reshape(ZS, width, model)
        proj_part = jnp.stack([pick(proj_part, (j - z) % ZS) for j in range(ZS)]).reshape(model, model)
        proj_part = rows_over_outer(proj_part, size).astype(BF16).reshape(4, 2, own_rows, model)
        chip_at = lambda m: chip ^ m
        qkv_part = rows_over_outer(qkv_part, size).astype(BF16).reshape(4, 2, own_rows, 3 * width)

    def scattered(part, at):
        keep, give = pick(part, core, 1), pick(part, 1 - core, 1)
        both = joined(keep, swap(give, 1))
        total = pick(both, at(0)).astype(F32)
        for m in (1, 2, 3):
            total = total + swap(pick(both, at(m)), 2 * m).astype(F32)
        return total.astype(BF16)

    proj_total = line_sum(scattered(proj_part, chip_at), z).astype(F32)
    proj_grad = proj_total[:own_rows]
    qkv_mine = lax.optimization_barrier(scattered(qkv_part, lambda m: chip ^ m))
    qkv_parts = jnp.stack([qkv_mine] + [shift(qkv_mine, k) for k in range(1, ZS)])
    ordered = [pick(qkv_parts, (z - j) % ZS).astype(F32) for j in range(ZS)]
    qkv_weight_grad = jnp.stack([part[:own_rows].reshape(own_rows, 3, width) for part in ordered], axis=2)
    qkv_weight_grad = qkv_weight_grad.reshape(own_rows, 3 * model)

    if outer == 1:
        mid = proj_total[own_rows, : 4 * own_rows].reshape(4, own_rows)
        rows = jnp.stack([part[own_rows] for part in ordered])
        gains = rows[:, : 2 * own_rows]
        gains = (gains[0] + gains[1]) + (gains[2] + gains[3])
        attn_gain_grad, attn_shift_grad = gains[:own_rows], gains[own_rows:]
        mine = pick(rows, place % ZS)
        start = 2 * own_rows + (place // ZS) * width
        qv_bias_grad = lax.dynamic_slice(mine, (start,), (width,))
        mlp_gain_grad, mlp_shift_grad, proj_bias_grad, down_bias_grad = mid
    else:
        biases = jnp.zeros((2, ZS, width), F32)
        biases = lax.dynamic_update_slice(
            biases, jnp.stack([attn_sums[2, :width], attn_sums[2, 2 * width : 3 * width]])[:, None], (0, z, 0)
        )
        sums = jnp.concatenate([attn_sums[0], attn_sums[1], mid_sums.reshape(-1)]).reshape(6, size, own_rows)
        sums = jnp.concatenate([sums.transpose(1, 0, 2).reshape(size, -1), biases.reshape(size, -1)], axis=1)
        sums = lax.psum_scatter(sums, "fsdp", scatter_dimension=0, tiled=False)
        sums = lax.psum(sums, "seq")
        vectors = sums[: 6 * own_rows].reshape(6, own_rows)
        attn_gain_grad, attn_shift_grad, mlp_gain_grad, mlp_shift_grad, proj_bias_grad, down_bias_grad = vectors
        qv_bias_grad = sums[6 * own_rows :]

    return (
        output,
        input_grad,
        attn_gain_grad,
        attn_shift_grad,
        qkv_weight_grad,
        qv_bias_grad,
        proj_grad,
        proj_bias_grad,
        mlp_gain_grad,
        mlp_shift_grad,
        up_grad,
        up_bias_grad,
        down_grad,
        down_bias_grad,
    )


def solution(mesh):
    split = P("fsdp")
    tokens = P("fsdp", "seq", None)
    matrix = P("fsdp", None)
    in_specs = (tokens, split, tokens, split, split, matrix, split, matrix) + (split,) * 3 + (matrix, split, matrix, split)
    out_specs = (tokens, tokens, split, split, matrix, split, matrix) + (split,) * 3 + (matrix, split, matrix, split)
    return jax.shard_map(per_device, mesh=mesh, in_specs=in_specs, out_specs=out_specs, check_vma=False)
```

```python
import functools
import math

import jax
import jax.numpy as jnp
from jax import lax
from jax.experimental import pallas as pl
from jax.experimental.pallas import tpu as pltpu
from jax.sharding import PartitionSpec as P

HEAD = 64
EPSILON = 1e-06
MASKED = -1e30
TEAM = 8
ZS = 4
F32 = jnp.float32
BF16 = jnp.bfloat16
VMEM_BYTES = 56 * 1024 * 1024
SCALE = 1024


def params():
    return pltpu.CompilerParams(vmem_limit_bytes=VMEM_BYTES)


def cost(flops, nbytes, trans=0):
    return pl.CostEstimate(flops=int(flops) // SCALE, bytes_accessed=int(nbytes) // SCALE, transcendentals=int(trans) // SCALE)


def shape_of(dims, dtype):
    return jax.ShapeDtypeStruct(dims, dtype)


def mm(left, right):
    return lax.dot_general(left, right, (((1,), (0,)), ((), ())), preferred_element_type=F32)


def mm_rt(left, right):
    return lax.dot_general(left, right, (((1,), (1,)), ((), ())), preferred_element_type=F32)


def mm_lt(left, right):
    return lax.dot_general(left, right, (((0,), (0,)), ((), ())), preferred_element_type=F32)


def normalize(rows):
    center = rows - jnp.mean(rows, axis=-1, keepdims=True)
    inverse = lax.rsqrt(jnp.mean(center * center, axis=-1, keepdims=True) + EPSILON)
    return center * inverse, inverse


def norm_back(upstream, unit, inverse, gain):
    scaled = upstream * gain
    return inverse * (
        scaled
        - jnp.mean(scaled, axis=-1, keepdims=True)
        - unit * jnp.mean(scaled * unit, axis=-1, keepdims=True)
    )


def swap(value, mask):
    size = lax.axis_size("fsdp")
    return lax.ppermute(value, "fsdp", [(i, i ^ mask) for i in range(size)])


def cross(value, mask):
    return lax.ppermute(value, "seq", [(i, i ^ mask) for i in range(ZS)])


def joined(first, second):
    return (first.astype(F32) + second.astype(F32)).astype(BF16)


def after(value, *others):
    return lax.optimization_barrier((value,) + others)[0]


def pick(stack, index, axis=0):
    starts = [jnp.uint32(0)] * stack.ndim
    starts[axis] = index.astype(jnp.uint32)
    sizes = list(stack.shape)
    sizes[axis] = 1
    return lax.dynamic_slice(stack, starts, sizes).reshape(stack.shape[:axis] + stack.shape[axis + 1 :])


def halves(value, z):
    value = value.reshape(2, value.shape[0] // 2, value.shape[1])
    return pick(value, z & 1), pick(value, 1 - (z & 1))


def whole_again(mine, other, z):
    first = (z & 1) == 0
    return jnp.concatenate([jnp.where(first, mine, other), jnp.where(first, other, mine)], axis=0)


def outer_groups(size):
    outer = size // TEAM
    return [[o * TEAM + t for o in range(outer)] for t in range(TEAM)]


def rows_over_outer(value, size):
    if size == TEAM:
        return value
    return lax.psum_scatter(
        value, "fsdp", scatter_dimension=0, axis_index_groups=outer_groups(size), tiled=True
    )


def gather_over_outer(value, size):
    if size == TEAM:
        return value
    return lax.all_gather(value, "fsdp", axis=0, axis_index_groups=outer_groups(size), tiled=True)


def block(*dims):
    return pl.BlockSpec(dims, lambda *i: (0,) * len(dims))


def valid_keys(z, length, slots, local):
    lane = lax.broadcasted_iota(jnp.int32, (1, slots), 1)
    index = jnp.zeros((1, slots), jnp.int32)
    for k in range(1, ZS):
        index = index + (lane >= k * local).astype(jnp.int32)
    return (z ^ index) * local + lane - index * local < length


def head_probs(queries, keys, valid):
    scores = mm_rt(queries, keys) * HEAD ** (-0.5)
    scores = jnp.where(valid, scores, MASKED)
    exponent = jnp.exp(scores - jnp.max(scores, axis=-1, keepdims=True))
    return exponent * (1.0 / jnp.sum(exponent, axis=-1, keepdims=True))


def attend_kernel(base, meta, places, own, two, pair, wq, wk, wv, vecs, bias, *refs):
    qkv_ref, rows_ref, normed_ref, c0, c1, c2, c3 = refs[-7:]
    local = own.shape[1]
    slots = ZS * local
    model = own.shape[2]
    width = wq.shape[2]
    z = meta[meta.shape[0] - 1]
    rows = jnp.concatenate([own[0], pair[0], two[...], pair[1]], axis=0)
    rows_ref[...] = rows
    unit, _ = normalize(rows.astype(F32))
    normed = (unit * vecs[0:1] + vecs[1:2]).astype(BF16)
    normed_ref[0] = normed
    parts = []
    for i, w in enumerate((wq, wk, wv)):
        deep = w.shape[1]
        part = bias[:, i * width : (i + 1) * width]
        for j in range(w.shape[0]):
            part = part + mm(normed[:, j * deep : (j + 1) * deep], w[places[j]])
        part = part.astype(BF16)
        qkv_ref[:, i * width : (i + 1) * width] = part
        parts.append(part)
    valid = valid_keys(z, meta[base], slots, local)
    first = lax.broadcasted_iota(jnp.int32, (1, 2 * HEAD), 1) < HEAD
    for pair_index in range(width // (2 * HEAD)):
        lanes = slice(pair_index * 2 * HEAD, (pair_index + 1) * 2 * HEAD)
        queries, keys, values = (part[:, lanes] for part in parts)
        outs = []
        for mine in (first, ~first):
            probs = head_probs(jnp.where(mine, queries, jnp.zeros_like(queries)), keys, valid)
            outs.append(mm(probs.astype(BF16), values))
        context = jnp.where(first, outs[0], outs[1]).astype(BF16)
        for k, out in enumerate((c0, c1, c2, c3)):
            out[:, lanes] = context[k * local : (k + 1) * local]


def weight_specs(weights, own_rows, width):
    return [
        pl.BlockSpec((weights.shape[0], own_rows, width), functools.partial(lambda i, s, m, p: (0, 0, i), i))
        for i in range(3)
    ]


def attend(base, meta, places, inputs, two, pair, weights, vecs, bias, buffers):
    count, local, model = inputs.shape
    slots, width = ZS * local, model // ZS
    flops = 2 * slots * model * 3 * width + 8 * slots * slots * width
    taken = 2 + 3 + 3 + 2
    return pl.pallas_call(
        functools.partial(attend_kernel, base),
        name="attend",
        grid_spec=pltpu.PrefetchScalarGridSpec(
            num_scalar_prefetch=2,
            grid=(1,),
            in_specs=[
                pl.BlockSpec((1, local, model), lambda s, m, p: (base, 0, 0)),
                block(local, model),
                block(2, local, model),
            ]
            + weight_specs(weights, model // weights.shape[0], width)
            + [block(*vecs.shape), block(1, 3 * width)]
            + [pl.BlockSpec(memory_space=pl.ANY)] * len(buffers),
            out_specs=[block(slots, 3 * width), block(slots, model)]
            + [pl.BlockSpec((1, slots, model), lambda s, m, p: (base, 0, 0))]
            + [pl.BlockSpec((local, width), lambda s, m, p: (base, 0))] * ZS,
        ),
        out_shape=[shape_of((slots, 3 * width), BF16), shape_of((slots, model), BF16)]
        + [shape_of((count, slots, model), BF16)]
        + [shape_of((count * local, width), BF16)] * ZS,
        input_output_aliases={taken + i: 2 + i for i in range(len(buffers))},
        compiler_params=params(),
        cost_estimate=cost(flops, 2 * slots * (3 * model + 4 * width) + 6 * model * width),
    )(meta, places, inputs, two, pair, weights, weights, weights, vecs, bias, *buffers)


def attend_back_kernel(base, meta, places, rows_ref, d0, d1, d2, d3, qkv_ref, wq, wk, wv, *refs):
    dqkv_ref, keep_ref, give_ref, sums_ref = refs[-4:]
    slots, model = rows_ref.shape
    local = slots // ZS
    width = wq.shape[2]
    z = meta[meta.shape[0] - 1]
    upstream = jnp.concatenate([d[...] for d in (d0, d1, d2, d3)], axis=0)
    valid = valid_keys(z, meta[base], slots, local)
    first = lax.broadcasted_iota(jnp.int32, (1, 2 * HEAD), 1) < HEAD
    for pair in range(width // (2 * HEAD)):
        spans = [slice(i * width + pair * 2 * HEAD, i * width + (pair + 1) * 2 * HEAD) for i in range(3)]
        queries, keys, values = (qkv_ref[:, span] for span in spans)
        above = upstream[:, spans[0]]
        grads = []
        for mine in (first, ~first):
            probs = head_probs(jnp.where(mine, queries, jnp.zeros_like(queries)), keys, valid)
            probs_grad = mm_rt(jnp.where(mine, above, jnp.zeros_like(above)), values)
            inner = jnp.sum(probs * probs_grad, axis=-1, keepdims=True)
            scores_grad = (probs * (probs_grad - inner) * HEAD ** (-0.5)).astype(BF16)
            grads.append(
                (mm(scores_grad, keys), mm_lt(scores_grad, queries), mm_lt(probs.astype(BF16), above))
            )
        for span, low, high in zip(spans, *grads):
            dqkv_ref[0, :, span] = jnp.where(first, low, high).astype(BF16)
    grad = dqkv_ref[0]
    columns = []
    for j in range(wq.shape[0]):
        part = mm_rt(grad[:, :width], wq[places[j]])
        part = part + mm_rt(grad[:, width : 2 * width], wk[places[j]])
        columns.append(part + mm_rt(grad[:, 2 * width :], wv[places[j]]))
    total = jnp.concatenate(columns, axis=1)
    for k in range(ZS):
        (keep_ref, give_ref)[k % 2][k // 2] = total[k * local : (k + 1) * local].astype(BF16)
    unit, _ = normalize(rows_ref[...].astype(F32))
    sums_ref[...] = jnp.zeros_like(sums_ref)
    sums_ref[0:1, :] = jnp.sum(total * unit, axis=0, keepdims=True)
    sums_ref[1:2, :] = jnp.sum(total, axis=0, keepdims=True)
    sums_ref[2:3, : 3 * width] = jnp.sum(grad.astype(F32), axis=0, keepdims=True)


def attend_back(base, count, meta, places, rows, upstream, qkv, weights, buffers):
    slots, model = rows.shape
    local, width = slots // ZS, model // ZS
    flops = 2 * slots * model * 3 * width + 20 * slots * slots * width
    taken = 2 + 1 + ZS + 1 + 3
    split = pl.BlockSpec((2, local, model), lambda s, m, p: (0, base, 0))
    return pl.pallas_call(
        functools.partial(attend_back_kernel, base),
        name="attend_back",
        grid_spec=pltpu.PrefetchScalarGridSpec(
            num_scalar_prefetch=2,
            grid=(1,),
            in_specs=[block(slots, model)]
            + [pl.BlockSpec((local, width), lambda s, m, p: (base, 0))] * ZS
            + [block(slots, 3 * width)]
            + weight_specs(weights, model // weights.shape[0], width)
            + [pl.BlockSpec(memory_space=pl.ANY)] * len(buffers),
            out_specs=[pl.BlockSpec((1, slots, 3 * width), lambda s, m, p: (base, 0, 0)), split, split]
            + [block(8, model)],
        ),
        out_shape=[shape_of((count, slots, 3 * width), BF16)]
        + [shape_of((2, count * local, model), BF16)] * 2
        + [shape_of((8, model), F32)],
        input_output_aliases={taken + i: i for i in range(len(buffers))},
        compiler_params=params(),
        cost_estimate=cost(flops, 2 * slots * (2 * model + 7 * width) + 6 * model * width),
    )(meta, places, rows, *upstream, qkv, weights, weights, weights, *buffers)


def project_kernel(meta, places, c0, c1, c2, c3, x, weights, vecs, hidden_ref, normed_ref):
    rows = weights.shape[1]
    z = meta[meta.shape[0] - 1]
    hidden = x[...].astype(F32) + vecs[2:3]
    for k, part in enumerate((c0, c1, c2, c3)):
        for h in range(2):
            hidden = hidden + mm(part[:, h * rows : (h + 1) * rows], weights[places[2 * (z ^ k) + h]])
    hidden_ref[...] = hidden
    unit, _ = normalize(hidden)
    normed_ref[...] = (unit * vecs[3:4] + vecs[4:5]).astype(BF16)


def project(meta, places, parts, x, weights, vecs):
    rows, model = x.shape
    return pl.pallas_call(
        project_kernel,
        name="project",
        grid_spec=pltpu.PrefetchScalarGridSpec(
            num_scalar_prefetch=2,
            grid=(1,),
            in_specs=[block(*part.shape) for part in parts]
            + [block(rows, model), block(*weights.shape), block(*vecs.shape)],
            out_specs=[block(rows, model)] * 2,
        ),
        out_shape=[shape_of((rows, model), F32), shape_of((rows, model), BF16)],
        compiler_params=params(),
        cost_estimate=cost(2 * rows * model * model, rows * model * 10 + 2 * model * model),
    )(meta, places, *parts, x, weights, vecs)


def unpack_kernel(rows, meta, places, small, vecs, bias):
    z = meta[meta.shape[0] - 1]
    count = small.shape[0]
    width = bias.shape[1] // 3
    for j in range(count):
        row = small[places[j]].astype(F32)
        for i in range(6):
            vecs[i : i + 1, j * rows : (j + 1) * rows] = row[0:1, i * rows : (i + 1) * rows]
    bias[...] = jnp.zeros_like(bias)
    per = count // (2 * ZS)
    step = width // per
    for i in range(per):
        for k in range(2):
            row = small[places[k * ZS * per + z * per + i]].astype(F32)
            start = 2 * k * width + i * step
            bias[:, start : start + step] = row[1:2, :step]


def unpack(rows, meta, places, small, width):
    count = small.shape[0]
    return pl.pallas_call(
        functools.partial(unpack_kernel, rows),
        name="unpack",
        grid_spec=pltpu.PrefetchScalarGridSpec(
            num_scalar_prefetch=2,
            grid=(1,),
            in_specs=[block(*small.shape)],
            out_specs=[block(8, count * rows), block(1, 3 * width)],
        ),
        out_shape=[shape_of((8, count * rows), F32), shape_of((1, 3 * width), F32)],
        compiler_params=params(),
        cost_estimate=cost(1, small.size * 4),
    )(meta, places, small)


def feed_kernel(normed, above, up, bias, act_ref, grad_ref, back_ref):
    value = mm(normed[0], up[...]) + bias[...]
    square = value * value
    root = math.sqrt(2.0 / math.pi)
    bend = jnp.tanh(root * value * (1.0 + 0.044715 * square))
    act_ref[0] = (0.5 * value * (1.0 + bend)).astype(BF16)
    slope = 0.5 * (1.0 + bend) + 0.5 * value * (1.0 - bend * bend) * root * (1.0 + 3 * 0.044715 * square)
    grad = (above[0] * slope).astype(BF16)
    grad_ref[0] = grad
    back_ref[0] = mm_rt(grad, up[...]).astype(BF16)


def feed(normed, above, up, bias):
    count, rows, model = normed.shape
    width = up.shape[1]
    wide = pl.BlockSpec((1, rows, model), lambda i: (i, 0, 0))
    thin = pl.BlockSpec((1, rows, width), lambda i: (i, 0, 0))
    return pl.pallas_call(
        feed_kernel,
        name="feed",
        grid=(count,),
        in_specs=[wide, thin, block(model, width), block(1, width)],
        out_specs=[thin, thin, wide],
        out_shape=[shape_of((count, rows, width), BF16)] * 2 + [shape_of((count, rows, model), BF16)],
        compiler_params=params(),
        cost_estimate=cost(
            count * rows * 4 * model * width,
            count * rows * (4 * model + 8 * width) + 2 * model * width,
            count * rows * width,
        ),
    )(normed, above, up, bias)


def feed_grads_kernel(
    act_e, act_o, grad_e, grad_o, normed_e, normed_o, cot_e, cot_o, down, out_e, out_o, down_ref, up_ref, down_sum, up_sum, bias_sum
):
    rows = act_e.shape[1]
    width = down.shape[0]
    act = jnp.concatenate([act_e[0], act_o[0]], axis=0)
    grad = jnp.concatenate([grad_e[0], grad_o[0]], axis=0)
    out = mm(act, down[...]).astype(BF16)
    out_e[0] = out[:rows]
    out_o[0] = out[rows:]

    @pl.when(pl.program_id(0) == 0)
    def _():
        down_sum[...] = jnp.zeros_like(down_sum)
        up_sum[...] = jnp.zeros_like(up_sum)
        bias_sum[...] = jnp.zeros_like(bias_sum)

    down_sum[...] += mm_lt(act, jnp.concatenate([cot_e[0], cot_o[0]], axis=0))
    up_sum[...] += mm_lt(jnp.concatenate([normed_e[0], normed_o[0]], axis=0), grad)
    bias_sum[0:1, :width] += jnp.sum(grad.astype(F32), axis=0, keepdims=True)

    @pl.when(pl.program_id(0) == pl.num_programs(0) - 1)
    def _():
        down_ref[:width] = down_sum[...].astype(BF16)
        down_ref[width:] = bias_sum[...].astype(BF16)
        up_ref[...] = up_sum[...].astype(BF16)


def feed_grads(act, grad, normed, cot, down):
    _, rows, width = act[0].shape
    model = down.shape[1]
    thin = pl.BlockSpec((1, rows, width), lambda i: (i, 0, 0))
    wide = pl.BlockSpec((1, rows, model), lambda i: (i, 0, 0))
    total = 8 * rows
    return pl.pallas_call(
        feed_grads_kernel,
        name="feed_grads",
        grid=(4,),
        in_specs=[thin] * 4 + [wide] * 4 + [block(width, model)],
        out_specs=[wide, wide, block(width + 16, model), block(model, width)],
        scratch_shapes=[
            pltpu.VMEM((width, model), F32),
            pltpu.VMEM((model, width), F32),
            pltpu.VMEM((16, model), F32),
        ],
        out_shape=[
            shape_of((4, rows, model), BF16),
            shape_of((4, rows, model), BF16),
            shape_of((width + 16, model), BF16),
            shape_of((model, width), BF16),
        ],
        compiler_params=params(),
        cost_estimate=cost(6 * total * model * width, 2 * total * (3 * model + 2 * width) + 6 * model * width),
    )(*act, *grad, *normed, *cot, down)


def middle_kernel(meta, places, g0, g1, gx, gy, gd, hidden, cot, weights, vecs, hidden_grad_ref, grad_ref, sums_ref, d0, d1, d2, d3):
    rows = weights.shape[1]
    z = meta[meta.shape[0] - 1]
    normed_grad = (g0[0].astype(F32) + g1[0].astype(F32)) + (gx[...].astype(F32) + gy[...].astype(F32))
    normed_grad = normed_grad + gd[...].astype(F32)
    unit, inverse = normalize(hidden[...])
    upstream = cot[...].astype(F32)
    hidden_grad = upstream + norm_back(normed_grad, unit, inverse, vecs[3:4])
    hidden_grad_ref[...] = hidden_grad
    grad = hidden_grad.astype(BF16)
    grad_ref[...] = grad
    for k, out in enumerate((d0, d1, d2, d3)):
        for h in range(2):
            part = mm_rt(grad, weights[places[2 * (z ^ k) + h]])
            out[:, h * rows : (h + 1) * rows] = part.astype(BF16)
    sums_ref[0:1, :] = jnp.sum(normed_grad * unit, axis=0, keepdims=True)
    sums_ref[1:2, :] = jnp.sum(normed_grad, axis=0, keepdims=True)
    sums_ref[2:3, :] = jnp.sum(grad.astype(F32), axis=0, keepdims=True)
    sums_ref[3:4, :] = jnp.sum(upstream, axis=0, keepdims=True)


def middle(meta, places, stacks, moved, hidden, cot, weights, vecs):
    rows, model = hidden.shape
    width = model // ZS
    return pl.pallas_call(
        middle_kernel,
        name="middle",
        grid_spec=pltpu.PrefetchScalarGridSpec(
            num_scalar_prefetch=2,
            grid=(1,),
            in_specs=[block(1, rows, model)] * 2
            + [block(rows, model)] * 5
            + [block(*weights.shape), block(*vecs.shape)],
            out_specs=[block(rows, model)] * 2 + [block(4, model)] + [block(rows, width)] * ZS,
        ),
        out_shape=[shape_of((rows, model), F32), shape_of((rows, model), BF16), shape_of((4, model), F32)]
        + [shape_of((rows, width), BF16)] * ZS,
        compiler_params=params(),
        cost_estimate=cost(2 * rows * model * model, rows * model * 26 + 2 * model * model),
    )(meta, places, *stacks, *moved, hidden, cot, weights, vecs)


def finish_kernel(x, mine, near, far, hidden_grad, vecs, out):
    unit, inverse = normalize(x[...].astype(F32))
    upstream = mine[0].astype(F32) + near[0].astype(F32) + far[...].astype(F32)
    out[...] = (hidden_grad[...] + norm_back(upstream, unit, inverse, vecs[0:1])).astype(BF16)


def finish(x, mine, near, far, hidden_grad, vecs):
    rows, model = x.shape
    steps = 3 if rows % 48 == 0 else 1
    part = pl.BlockSpec((rows // steps, model), lambda i: (i, 0))
    stack = pl.BlockSpec((1, rows // steps, model), lambda i: (0, i, 0))
    return pl.pallas_call(
        finish_kernel,
        name="finish",
        grid=(steps,),
        in_specs=[part, stack, stack, part, part, block(*vecs.shape)],
        out_specs=part,
        out_shape=shape_of((rows, model), BF16),
        compiler_params=params(),
        cost_estimate=cost(20 * rows * model, rows * model * 12),
    )(x, mine, near, far, hidden_grad, vecs)


def per_device(
    inputs,
    lengths,
    cotangent,
    attn_gain,
    attn_shift,
    qkv_weight,
    qv_bias,
    proj_weight,
    proj_bias,
    mlp_gain,
    mlp_shift,
    up_weight,
    up_bias,
    down_weight,
    down_bias,
):
    count, local, model = inputs.shape
    size = lax.axis_size("fsdp")
    outer = size // TEAM
    place = lax.axis_index("fsdp").astype(jnp.uint32)
    seat = lax.axis_index("seq").astype(jnp.uint32)
    z = seat.astype(jnp.int32)
    team = place & (TEAM - 1)
    core = team & 1
    chip = team >> 1
    tokens = count * local
    width = model // ZS
    own_rows = qkv_weight.shape[0]
    hidden_units = up_weight.shape[1]
    feed_width = hidden_units // TEAM
    meta = jnp.concatenate([lengths.astype(jnp.int32), z.reshape(1)])

    twos = [cross(inputs[s], 2) for s in range(count)]
    pairs = [cross(jnp.stack([inputs[s], twos[s]]), 1) for s in range(count)]

    def over_team(own):
        quad = jnp.stack([own] + [swap(own, 2 * m) for m in (1, 2, 3)])
        return jnp.concatenate([quad, swap(quad, 1)], axis=0)

    columns = [
        lax.dynamic_slice(qkv_weight, (jnp.uint32(0), seat * width + i * model), (own_rows, width)) for i in range(3)
    ]
    vectors = (attn_gain, attn_shift, proj_bias, mlp_gain, mlp_shift, down_bias)
    lanes, spot, packed = 3 * width, 0, []
    for vector in vectors:
        packed.append(jnp.pad(vector, (spot, lanes - spot - vector.shape[0])))
        spot += vector.shape[0]
    row_one = functools.reduce(jnp.add, packed).reshape(1, lanes)
    row_two = jnp.pad(qv_bias, (0, lanes - qv_bias.shape[0])).reshape(1, lanes)
    small_rows = jnp.pad(row_one, ((0, 7), (0, 0))) + jnp.pad(row_two, ((1, 6), (0, 0)))
    piece = jnp.concatenate([jnp.concatenate(columns, axis=1), small_rows], axis=0)
    weights = over_team(after(piece, twos[0]))
    order = jnp.stack([((j ^ team) & 1) * 4 + ((j ^ team) >> 1) for j in range(TEAM)]).astype(jnp.int32)
    if outer == 1:
        proj_own = after(proj_weight, pairs[0], twos[-1])
        proj_quad = jnp.stack([proj_own] + [swap(proj_own, 2 * m) for m in (1, 2, 3)])
        places = order
        vecs, bias_quarter = unpack(own_rows, meta, order, weights[:, own_rows:], width)
    else:
        proj = lax.all_gather(proj_weight, "fsdp", axis=0, tiled=True).reshape(TEAM, model // TEAM, model)
        places = jnp.arange(TEAM, dtype=jnp.int32)
        proj_quad = proj
        weights = gather_over_outer(jnp.stack([pick(weights, order[j]) for j in range(TEAM)]), size)
        vecs = weights[:, own_rows, : 6 * own_rows].reshape(size, 6, own_rows).transpose(1, 0, 2)
        vecs = vecs.reshape(6, model).astype(F32)
        bias_qv = weights[:, own_rows + 1, : qv_bias.shape[0]].reshape(1, 2 * model).astype(F32)
        bias_quarter = jnp.concatenate(
            [
                lax.dynamic_slice(bias_qv, (jnp.uint32(0), seat * width), (1, width)),
                jnp.zeros((1, width), F32),
                lax.dynamic_slice(bias_qv, (jnp.uint32(0), model + seat * width), (1, width)),
            ],
            axis=1,
        )
        weights = weights[:, :own_rows].reshape(TEAM, model // TEAM, 3 * width)

    up_blocks = up_weight.reshape(own_rows, outer, TEAM, feed_width // outer).transpose(2, 0, 1, 3)
    up_blocks = up_blocks.reshape(TEAM, own_rows, feed_width)
    groups = [[o * TEAM + t for t in range(TEAM)] for o in range(outer)]
    up = lax.all_to_all(
        up_blocks, "fsdp", split_axis=0, concat_axis=0, axis_index_groups=groups, tiled=True
    ).reshape(TEAM * own_rows, feed_width)
    up = gather_over_outer(up, size)
    down = gather_over_outer(down_weight, size)
    bias_up = gather_over_outer(up_bias, size).astype(F32).reshape(1, feed_width)

    half = model // 2

    def over_chips(own):
        by_x, by_y = swap(own, 2), swap(own, 4)
        diagonal = jnp.concatenate([swap(by_x[:, :half], 4), swap(by_y[:, half:], 2)], axis=1)
        return jnp.stack([own, by_x, by_y, diagonal])

    positions = z * local + jnp.arange(local, dtype=jnp.int32)
    row_valid = (positions[None, :] < lengths[:, None])[:, :, None]
    cot = jnp.where(row_valid, cotangent, jnp.zeros_like(cotangent)).reshape(tokens, model)
    cot = after(cot, pairs[0])
    cot_x, cot_y = swap(cot, 2), swap(cot, 4)

    def down_back(stack):
        out = lax.dot_general(stack, down, (((2,), (1,)), ((), ())), preferred_element_type=F32)
        return out


    def attention(s, pair, buffers):
        kept, seen, *buffers = attend(s, meta, places, inputs, twos[s], pair, weights, vecs, bias_quarter, buffers)
        qkv.append(kept)
        rows.append(seen)
        return buffers

    qkv, rows = [], []
    buffers = attention(0, pairs[0], ())
    cot_x, cot_y = after(cot_x, qkv[0]), after(cot_y, qkv[0])
    for s in range(1, count - 1):
        buffers = attention(s, after(pairs[s], cot_x, cot_y, up), buffers)
    cot_d = jnp.concatenate([swap(cot_x[:, :half], 4), swap(cot_y[:, half:], 2)], axis=1)
    cot_even = jnp.stack([cot, cot_x, cot_y, after(cot_d, qkv[-1])])
    proj_quad = after(proj_quad, qkv[-1])
    buffers = attention(count - 1, after(pairs[-1], cot_even, proj_quad), buffers)
    cot_odd = swap(cot_even, 1)
    if outer == 1:
        proj = jnp.concatenate([proj_quad, swap(proj_quad, 1)], axis=0)
    normed_attn, *context = buffers
    context = [context[0]] + [cross(context[k], k) for k in range(1, ZS)]
    above_even = down_back(after(cot_even, qkv[-1]))
    above_odd = down_back(after(cot_odd, qkv[-1]))
    own = inputs.reshape(tokens, model)
    context[0] = after(context[0], above_even)
    hidden, normed = project(meta, places, context, own, proj, vecs)

    normed_even = over_chips(normed)
    normed_odd = swap(normed_even, 1)
    act_even, grad_even, back_even = feed(normed_even, above_even, up, bias_up)
    act_odd, grad_odd, back_odd = feed(normed_odd, above_odd, up, bias_up)
    back_core = swap(back_odd, 1)
    sums = [joined(back_even[m], back_core[m]) for m in (1, 2, 3)]
    moved = [swap(part, 2 * m) for m, part in zip((1, 2, 3), sums)]
    act_even = after(act_even, *sums)
    out_even, out_odd, down_part, up_part = feed_grads(
        (act_even, act_odd), (grad_even, grad_odd), (normed_even, normed_odd), (cot_even, cot_odd), down
    )
    if outer > 1:
        bias_part = rows_over_outer(down_part[feed_width, :feed_width].astype(F32), size)
        bias_part = jnp.pad(bias_part.reshape(1, -1), ((0, 15), (0, model - bias_part.shape[0])))
        down_part = rows_over_outer(down_part[:feed_width], size)
        down_part = jnp.concatenate([down_part, bias_part.astype(BF16)], axis=0)
    down_rows = down_weight.shape[0]
    down_keep, down_give = halves(down_part, seat)
    top = down_give.shape[0] // 16 * 8
    down_near = jnp.concatenate([cross(down_give[:top], 1), cross(down_give[top:], 1)], axis=0)
    down_half = joined(down_keep, down_near)
    up_part = rows_over_outer(up_part, size).reshape(4, 2, own_rows, feed_width)
    hidden_grad, attn_grad, mid_sums, *context_grad = middle(
        meta, places, (back_even, back_core), moved, after(hidden, out_even, down_half), cot, proj, vecs
    )

    def over_core(part, *others):
        keep, give = pick(part, core, 1), pick(part, 1 - core, 1)
        return joined(after(keep, *others), swap(give, 1))

    def over_team_chips(both, at, *others):
        total = after(pick(both, at(0)), *others).astype(F32)
        for m in (1, 2, 3):
            total = total + swap(pick(both, at(m)), 2 * m).astype(F32)
        return total.astype(BF16)

    proj_part = mm_lt(jnp.concatenate(context, axis=1), attn_grad)
    if outer == 1:
        proj_part = proj_part.astype(BF16).reshape(ZS, 2, own_rows, model)
        mid_rows = mid_sums.reshape(4, TEAM, own_rows).transpose(1, 0, 2).reshape(4, 2, 1, 4 * own_rows)
        mid_rows = jnp.pad(mid_rows, ((0, 0), (0, 0), (0, 7), (0, model - 4 * own_rows))).astype(BF16)
        mid_rows = jnp.stack([pick(mid_rows, seat ^ k) for k in range(ZS)])
        proj_part = jnp.concatenate([proj_part, mid_rows], axis=2)
        chip_at = lambda m: chip ^ m ^ seat
    else:
        proj_part = proj_part.reshape(ZS, width, model)
        proj_part = jnp.stack([pick(proj_part, seat ^ j) for j in range(ZS)]).reshape(model, model)
        proj_part = rows_over_outer(proj_part, size).astype(BF16).reshape(4, 2, own_rows, model)
        chip_at = lambda m: chip ^ m

    context_grad = [context_grad[0]] + [cross(context_grad[k], k) for k in range(1, ZS)]
    up_core = swap(after(pick(up_part, 1 - core, 1), *context_grad), 1)
    out_core = swap(after(out_odd, *context_grad), 1)
    down_other = cross(after(down_half, *context_grad), 2)
    pair = jnp.stack([after(pick(up_part, core, 1), *context_grad), up_core], axis=1)
    up_own = pick(pair, chip)
    up_moved = [swap(pick(pair, chip ^ m), 2 * m) for m in (1, 2, 3)]

    def backward(s, buffers, *others):
        kept = after(qkv[s], *others)
        *buffers, sums = attend_back(s, count, meta, places, rows[s], context_grad, kept, weights, buffers)
        return buffers, sums

    buffers, attn_sums = backward(0, (), down_half, pair, proj_part)
    up_rel = jnp.stack([after(up_own, *buffers)] + up_moved).reshape(TEAM * own_rows, feed_width)
    up_rows = up_rel.shape[0]
    proj_both = over_core(proj_part, *buffers)
    out_sums = [joined(after(out_even[m], *buffers), out_core[m]) for m in (1, 2, 3)]
    out_moved = [swap(part, 2 * m) for m, part in zip((1, 2, 3), out_sums)]
    waits = (up_rel, proj_both, *out_sums)
    for s in range(1, count - 1):
        buffers, sums = backward(s, buffers, *waits)
        attn_sums, waits = attn_sums + sums, ()
    proj_mine = over_team_chips(proj_both, chip_at, *buffers)
    rest = jnp.concatenate([up_rel, proj_mine.reshape(-1, feed_width)], axis=0)
    rest_keep, rest_give = halves(rest, seat)
    down_total = lax.optimization_barrier(joined(after(down_half, *buffers), down_other))
    buffers, sums = backward(count - 1, buffers, rest_give, down_total, out_moved[0])
    attn_sums = attn_sums + sums
    qkv_grad, mine, give = buffers
    near = cross(give, 1)
    rest_near = cross(rest_give, 1)
    down_back_half = cross(down_total, 1)

    qkv_part = mm_lt(normed_attn.reshape(-1, model), qkv_grad.reshape(-1, 3 * width)).astype(BF16)

    if outer == 1:
        qkv_part = qkv_part.reshape(4, 2, own_rows, 3 * width)
        gains = attn_sums[:2].reshape(2, TEAM, own_rows).transpose(1, 0, 2).reshape(4, 2, 1, 2 * own_rows)
        biases = jnp.concatenate([attn_sums[2, :width], attn_sums[2, 2 * width : 3 * width]])
        biases = jnp.broadcast_to(biases, (4, 2, 1, 2 * width))
        packed = jnp.concatenate([gains, biases], axis=3)
        packed = jnp.pad(packed, ((0, 0), (0, 0), (0, 7), (0, 3 * width - packed.shape[3]))).astype(BF16)
        qkv_part = jnp.concatenate([qkv_part, packed], axis=2)
    else:
        qkv_part = rows_over_outer(qkv_part, size).reshape(4, 2, own_rows, 3 * width)

    qkv_both = over_core(qkv_part)
    far = cross(joined(after(mine[1], qkv_part), near[1]), 2)
    rest_half = joined(after(rest_keep, qkv_part), rest_near)
    rest_other = cross(rest_half, 2)
    qkv_mine = lax.optimization_barrier(over_team_chips(qkv_both, lambda m: chip ^ m))
    down_sum = whole_again(down_total, down_back_half, seat)
    rest_total = lax.optimization_barrier(joined(after(rest_half, qkv_mine), rest_other))
    rest_sum = whole_again(rest_total, cross(rest_total, 1), seat)

    output = hidden + vecs[5:6] + out_even[0].astype(F32) + out_core[0].astype(F32)
    for part in out_moved:
        output = output + part.astype(F32)
    output = jnp.where(row_valid, output.reshape(inputs.shape), 0.0).astype(BF16)

    input_grad = finish(own, mine, near, far, after(hidden_grad, qkv_mine, output), vecs).reshape(inputs.shape)

    down_sum = down_sum.astype(F32)
    down_grad = down_sum[:down_rows]
    up_bias_grad = down_sum[down_rows, : up_bias.shape[0]]
    up_rel = rest_sum[:up_rows].reshape(TEAM, own_rows, feed_width)
    proj_total = rest_sum[up_rows:].reshape(-1, model).astype(F32)
    up_grad = jnp.stack([pick(up_rel, j ^ team) for j in range(TEAM)], axis=1).astype(F32)
    up_grad = up_grad.reshape(own_rows, TEAM, outer, feed_width // outer).transpose(0, 2, 1, 3)
    up_grad = up_grad.reshape(own_rows, hidden_units)
    proj_grad = proj_total[:own_rows]
    qkv_two = cross(after(qkv_mine, near), 2)
    qkv_near = cross(jnp.stack([qkv_mine, qkv_two]), 1)
    qkv_parts = jnp.stack([qkv_mine, qkv_near[0], qkv_two, qkv_near[1]])
    ordered = [pick(qkv_parts, seat ^ j).astype(F32) for j in range(ZS)]
    qkv_weight_grad = jnp.concatenate(
        [part[:own_rows, i * width : (i + 1) * width] for i in range(3) for part in ordered], axis=1
    )

    if outer == 1:
        mid = proj_total[own_rows, : 4 * own_rows].reshape(4, own_rows)
        packed = jnp.stack([part[own_rows] for part in ordered])
        gains = packed[:, : 2 * own_rows]
        gains = (gains[0] + gains[1]) + (gains[2] + gains[3])
        attn_gain_grad, attn_shift_grad = gains[:own_rows], gains[own_rows:]
        mine = pick(packed, place & (ZS - 1))
        start = 2 * own_rows + (place >> 2) * width
        qv_bias_grad = lax.dynamic_slice(mine, (start,), (width,))
        mlp_gain_grad, mlp_shift_grad, proj_bias_grad, down_bias_grad = mid
    else:
        biases = jnp.zeros((2, ZS, width), F32)
        biases = lax.dynamic_update_slice(
            biases, jnp.stack([attn_sums[2, :width], attn_sums[2, 2 * width : 3 * width]])[:, None], (0, z, 0)
        )
        packed = jnp.concatenate([attn_sums[0], attn_sums[1], mid_sums.reshape(-1)]).reshape(6, size, own_rows)
        packed = jnp.concatenate([packed.transpose(1, 0, 2).reshape(size, -1), biases.reshape(size, -1)], axis=1)
        packed = lax.psum_scatter(packed, "fsdp", scatter_dimension=0, tiled=False)
        packed = lax.psum(packed, "seq")
        vectors = packed[: 6 * own_rows].reshape(6, own_rows)
        attn_gain_grad, attn_shift_grad, mlp_gain_grad, mlp_shift_grad, proj_bias_grad, down_bias_grad = vectors
        qv_bias_grad = packed[6 * own_rows :]

    return (
        output,
        input_grad,
        attn_gain_grad,
        attn_shift_grad,
        qkv_weight_grad,
        qv_bias_grad,
        proj_grad,
        proj_bias_grad,
        mlp_gain_grad,
        mlp_shift_grad,
        up_grad,
        up_bias_grad,
        down_grad,
        down_bias_grad,
    )


def solution(mesh):
    split = P("fsdp")
    tokens = P("fsdp", "seq", None)
    matrix = P("fsdp", None)
    in_specs = (tokens, split, tokens, split, split, matrix, split, matrix) + (split,) * 3 + (matrix, split, matrix, split)
    out_specs = (tokens, tokens, split, split, matrix, split, matrix) + (split,) * 3 + (matrix, split, matrix, split)
    return jax.shard_map(per_device, mesh=mesh, in_specs=in_specs, out_specs=out_specs, check_vma=False)
```

```python
import functools
import math

import jax
import jax.numpy as jnp
from jax import lax
from jax.experimental import pallas as pl
from jax.experimental.pallas import tpu as pltpu
from jax.sharding import PartitionSpec as P

HEAD = 64
EPSILON = 1e-06
MASKED = -1e30
TEAM = 8
ZS = 4
F32 = jnp.float32
BF16 = jnp.bfloat16
VMEM_BYTES = 56 * 1024 * 1024
SCALE = 1024


def params():
    return pltpu.CompilerParams(vmem_limit_bytes=VMEM_BYTES)


def cost(flops, nbytes, trans=0):
    return pl.CostEstimate(flops=int(flops) // SCALE, bytes_accessed=int(nbytes) // SCALE, transcendentals=int(trans) // SCALE)


def shape_of(dims, dtype):
    return jax.ShapeDtypeStruct(dims, dtype)


def mm(left, right):
    return lax.dot_general(left, right, (((1,), (0,)), ((), ())), preferred_element_type=F32)


def mm_rt(left, right):
    return lax.dot_general(left, right, (((1,), (1,)), ((), ())), preferred_element_type=F32)


def mm_lt(left, right):
    return lax.dot_general(left, right, (((0,), (0,)), ((), ())), preferred_element_type=F32)


def normalize(rows):
    center = rows - jnp.mean(rows, axis=-1, keepdims=True)
    inverse = lax.rsqrt(jnp.mean(center * center, axis=-1, keepdims=True) + EPSILON)
    return center * inverse, inverse


def norm_back(upstream, unit, inverse, gain):
    scaled = upstream * gain
    return inverse * (
        scaled
        - jnp.mean(scaled, axis=-1, keepdims=True)
        - unit * jnp.mean(scaled * unit, axis=-1, keepdims=True)
    )


def swap(value, mask):
    size = lax.axis_size("fsdp")
    return lax.ppermute(value, "fsdp", [(i, i ^ mask) for i in range(size)])


def cross(value, mask):
    return lax.ppermute(value, "seq", [(i, i ^ mask) for i in range(ZS)])


def joined(first, second):
    return (first.astype(F32) + second.astype(F32)).astype(BF16)


def after(value, *others):
    return lax.optimization_barrier((value,) + others)[0]


def pick(stack, index, axis=0):
    starts = [jnp.uint32(0)] * stack.ndim
    starts[axis] = index.astype(jnp.uint32)
    sizes = list(stack.shape)
    sizes[axis] = 1
    return lax.dynamic_slice(stack, starts, sizes).reshape(stack.shape[:axis] + stack.shape[axis + 1 :])


def outer_groups(size):
    outer = size // TEAM
    return [[o * TEAM + t for o in range(outer)] for t in range(TEAM)]


def rows_over_outer(value, size):
    if size == TEAM:
        return value
    return lax.psum_scatter(
        value, "fsdp", scatter_dimension=0, axis_index_groups=outer_groups(size), tiled=True
    )


def gather_over_outer(value, size):
    if size == TEAM:
        return value
    return lax.all_gather(value, "fsdp", axis=0, axis_index_groups=outer_groups(size), tiled=True)


def block(*dims):
    return pl.BlockSpec(dims, lambda *i: (0,) * len(dims))


def chosen(values, index):
    out = values[-1]
    for i in range(len(values) - 1):
        out = jnp.where(index == i, values[i], out)
    return out


def head_probs(queries, keys, valid):
    scores = mm_rt(queries, keys) * HEAD ** (-0.5)
    scores = jnp.where(valid, scores, MASKED)
    exponent = jnp.exp(scores - jnp.max(scores, axis=-1, keepdims=True))
    return exponent * (1.0 / jnp.sum(exponent, axis=-1, keepdims=True))


def attend_kernel(meta, rows_ref, wq, wk, wv, vecs, bias, qkv_ref, normed_ref, c0, c1, c2, c3):
    local = rows_ref.shape[2]
    slots = ZS * local
    model = rows_ref.shape[3]
    width = wq.shape[2]
    length = meta[pl.program_id(0)]
    z = meta[meta.shape[0] - 1]
    unit, _ = normalize(rows_ref[:, 0].reshape(slots, model).astype(F32))
    normed = (unit * vecs[0:1] + vecs[1:2]).astype(BF16)
    normed_ref[0] = normed
    parts = []
    for i, w in enumerate((wq, wk, wv)):
        part = (mm(normed, w[...].reshape(model, width)) + bias[:, i * width : (i + 1) * width]).astype(BF16)
        qkv_ref[0, :, i * width : (i + 1) * width] = part
        parts.append(part)
    valid = lax.broadcasted_iota(jnp.int32, (1, slots), 1) < length
    first = lax.broadcasted_iota(jnp.int32, (1, 2 * HEAD), 1) < HEAD
    for pair in range(width // (2 * HEAD)):
        lanes = slice(pair * 2 * HEAD, (pair + 1) * 2 * HEAD)
        queries, keys, values = (part[:, lanes] for part in parts)
        outs = []
        for mine in (first, ~first):
            probs = head_probs(jnp.where(mine, queries, jnp.zeros_like(queries)), keys, valid)
            outs.append(mm(probs.astype(BF16), values))
        context = jnp.where(first, outs[0], outs[1])
        pieces = [context[k * local : (k + 1) * local] for k in range(ZS)]
        for k, out in enumerate((c0, c1, c2, c3)):
            out[:, lanes] = chosen(pieces, z ^ k).astype(BF16)


def weight_specs(weights, own_rows, width):
    return [
        pl.BlockSpec((weights.shape[0], own_rows, width), functools.partial(lambda i, s, m: (0, 0, i), i))
        for i in range(3)
    ]


def attend(meta, rows, weights, vecs, bias):
    _, count, local, model = rows.shape
    slots, width = ZS * local, model // ZS
    flops = count * (2 * slots * model * 3 * width + 8 * slots * slots * width)
    per_sequence = lambda *dims: pl.BlockSpec((1,) + dims, lambda s, m: (s, 0, 0))
    return pl.pallas_call(
        attend_kernel,
        name="attend",
        grid_spec=pltpu.PrefetchScalarGridSpec(
            num_scalar_prefetch=1,
            grid=(count,),
            in_specs=[pl.BlockSpec((ZS, 1, local, model), lambda s, m: (0, s, 0, 0))]
            + weight_specs(weights, model // weights.shape[0], width)
            + [block(*vecs.shape), block(1, 3 * width)],
            out_specs=[per_sequence(slots, 3 * width), per_sequence(slots, model)]
            + [pl.BlockSpec((local, width), lambda s, m: (s, 0))] * ZS,
        ),
        out_shape=[shape_of((count, slots, 3 * width), BF16), shape_of((count, slots, model), BF16)]
        + [shape_of((count * local, width), BF16)] * ZS,
        compiler_params=params(),
        cost_estimate=cost(flops, 2 * count * slots * (2 * model + 4 * width) + 6 * model * width),
    )(meta, rows, weights, weights, weights, vecs, bias)


def attend_back_kernel(meta, rows_ref, d0, d1, d2, d3, qkv_ref, wq, wk, wv, *refs):
    dqkv_ref, keep_ref, give_ref, sums_ref = refs
    local = rows_ref.shape[2]
    slots = ZS * local
    model = rows_ref.shape[3]
    width = wq.shape[2]
    length = meta[pl.program_id(0)]
    z = meta[meta.shape[0] - 1]
    given = [d[...] for d in (d0, d1, d2, d3)]
    upstream = jnp.concatenate([chosen(given, z ^ k) for k in range(ZS)], axis=0)
    valid = lax.broadcasted_iota(jnp.int32, (1, slots), 1) < length
    first = lax.broadcasted_iota(jnp.int32, (1, 2 * HEAD), 1) < HEAD
    for pair in range(width // (2 * HEAD)):
        spans = [slice(i * width + pair * 2 * HEAD, i * width + (pair + 1) * 2 * HEAD) for i in range(3)]
        queries, keys, values = (qkv_ref[0, :, span] for span in spans)
        above = upstream[:, spans[0]]
        grads = []
        for mine in (first, ~first):
            probs = head_probs(jnp.where(mine, queries, jnp.zeros_like(queries)), keys, valid)
            probs_grad = mm_rt(jnp.where(mine, above, jnp.zeros_like(above)), values)
            inner = jnp.sum(probs * probs_grad, axis=-1, keepdims=True)
            scores_grad = (probs * (probs_grad - inner) * HEAD ** (-0.5)).astype(BF16)
            grads.append(
                (mm(scores_grad, keys), mm_lt(scores_grad, queries), mm_lt(probs.astype(BF16), above))
            )
        for span, low, high in zip(spans, *grads):
            dqkv_ref[0, :, span] = jnp.where(first, low, high).astype(BF16)
    grad = dqkv_ref[0]
    total = mm_rt(grad[:, :width], wq[...].reshape(model, width))
    total = total + mm_rt(grad[:, width : 2 * width], wk[...].reshape(model, width))
    total = total + mm_rt(grad[:, 2 * width :], wv[...].reshape(model, width))
    pieces = [total[k * local : (k + 1) * local] for k in range(ZS)]
    for k in range(ZS):
        (keep_ref, give_ref)[k % 2][k // 2] = chosen(pieces, z ^ k).astype(BF16)
    unit, _ = normalize(rows_ref[:, 0].reshape(slots, model).astype(F32))

    @pl.when(pl.program_id(0) == 0)
    def _():
        sums_ref[...] = jnp.zeros_like(sums_ref)

    sums_ref[0:1, :] += jnp.sum(total * unit, axis=0, keepdims=True)
    sums_ref[1:2, :] += jnp.sum(total, axis=0, keepdims=True)
    sums_ref[2:3, : 3 * width] += jnp.sum(grad.astype(F32), axis=0, keepdims=True)


def attend_back(meta, rows, upstream, qkv, weights):
    _, count, local, model = rows.shape
    slots, width = ZS * local, model // ZS
    packed = pl.BlockSpec((1, slots, 3 * width), lambda s, m: (s, 0, 0))
    split = pl.BlockSpec((2, local, model), lambda s, m: (0, s, 0))
    flops = count * (2 * slots * model * 3 * width + 20 * slots * slots * width)
    return pl.pallas_call(
        attend_back_kernel,
        name="attend_back",
        grid_spec=pltpu.PrefetchScalarGridSpec(
            num_scalar_prefetch=1,
            grid=(count,),
            in_specs=[pl.BlockSpec((ZS, 1, local, model), lambda s, m: (0, s, 0, 0))]
            + [pl.BlockSpec((local, width), lambda s, m: (s, 0))] * ZS
            + [packed]
            + weight_specs(weights, model // weights.shape[0], width),
            out_specs=[packed, split, split, block(8, model)],
        ),
        out_shape=[shape_of((count, slots, 3 * width), BF16)]
        + [shape_of((2, count * local, model), BF16)] * 2
        + [shape_of((8, model), F32)],
        compiler_params=params(),
        cost_estimate=cost(flops, 2 * count * slots * (2 * model + 7 * width) + 6 * model * width),
    )(meta, rows, *upstream, qkv, weights, weights, weights)


def project_kernel(meta, c0, c1, c2, c3, x, weights, vecs, hidden_ref, normed_ref):
    width = c0.shape[1]
    z = meta[meta.shape[0] - 1]
    hidden = x[...].astype(F32) + vecs[2:3]
    for k, part in enumerate((c0, c1, c2, c3)):
        start = pl.multiple_of((z ^ k) * width, width)
        hidden = hidden + mm(part[...], weights[pl.ds(start, width), :])
    hidden_ref[...] = hidden
    unit, _ = normalize(hidden)
    normed_ref[...] = (unit * vecs[3:4] + vecs[4:5]).astype(BF16)


def project(meta, parts, x, weights, vecs):
    rows, model = x.shape
    return pl.pallas_call(
        project_kernel,
        name="project",
        grid_spec=pltpu.PrefetchScalarGridSpec(
            num_scalar_prefetch=1,
            grid=(1,),
            in_specs=[block(*part.shape) for part in parts]
            + [block(rows, model), block(model, model), block(*vecs.shape)],
            out_specs=[block(rows, model)] * 2,
        ),
        out_shape=[shape_of((rows, model), F32), shape_of((rows, model), BF16)],
        compiler_params=params(),
        cost_estimate=cost(2 * rows * model * model, rows * model * 10 + 2 * model * model),
    )(meta, *parts, x, weights, vecs)


def feed_kernel(normed, above, up, bias, act_ref, grad_ref, back_ref):
    value = mm(normed[0], up[...]) + bias[...]
    square = value * value
    root = math.sqrt(2.0 / math.pi)
    bend = jnp.tanh(root * value * (1.0 + 0.044715 * square))
    act_ref[0] = (0.5 * value * (1.0 + bend)).astype(BF16)
    slope = 0.5 * (1.0 + bend) + 0.5 * value * (1.0 - bend * bend) * root * (1.0 + 3 * 0.044715 * square)
    grad = (above[0] * slope).astype(BF16)
    grad_ref[0] = grad
    back_ref[0] = mm_rt(grad, up[...]).astype(BF16)


def feed(normed, above, up, bias):
    count, rows, model = normed.shape
    width = up.shape[1]
    wide = pl.BlockSpec((1, rows, model), lambda i: (i, 0, 0))
    thin = pl.BlockSpec((1, rows, width), lambda i: (i, 0, 0))
    return pl.pallas_call(
        feed_kernel,
        name="feed",
        grid=(count,),
        in_specs=[wide, thin, block(model, width), block(1, width)],
        out_specs=[thin, thin, wide],
        out_shape=[shape_of((count, rows, width), BF16)] * 2 + [shape_of((count, rows, model), BF16)],
        compiler_params=params(),
        cost_estimate=cost(
            count * rows * 4 * model * width,
            count * rows * (4 * model + 8 * width) + 2 * model * width,
            count * rows * width,
        ),
    )(normed, above, up, bias)


def feed_grads_kernel(
    act_e, act_o, grad_e, grad_o, normed_e, normed_o, cot_e, cot_o, down, out_e, out_o, down_ref, up_ref, down_sum, up_sum, bias_sum
):
    rows = act_e.shape[1]
    width = down.shape[0]
    act = jnp.concatenate([act_e[0], act_o[0]], axis=0)
    grad = jnp.concatenate([grad_e[0], grad_o[0]], axis=0)
    out = mm(act, down[...]).astype(BF16)
    out_e[0] = out[:rows]
    out_o[0] = out[rows:]

    @pl.when(pl.program_id(0) == 0)
    def _():
        down_sum[...] = jnp.zeros_like(down_sum)
        up_sum[...] = jnp.zeros_like(up_sum)
        bias_sum[...] = jnp.zeros_like(bias_sum)

    down_sum[...] += mm_lt(act, jnp.concatenate([cot_e[0], cot_o[0]], axis=0))
    up_sum[...] += mm_lt(jnp.concatenate([normed_e[0], normed_o[0]], axis=0), grad)
    bias_sum[0:1, :width] += jnp.sum(grad.astype(F32), axis=0, keepdims=True)

    @pl.when(pl.program_id(0) == pl.num_programs(0) - 1)
    def _():
        down_ref[:width] = down_sum[...].astype(BF16)
        down_ref[width:] = bias_sum[...].astype(BF16)
        up_ref[...] = up_sum[...].astype(BF16)


def feed_grads(act, grad, normed, cot, down):
    _, rows, width = act[0].shape
    model = down.shape[1]
    thin = pl.BlockSpec((1, rows, width), lambda i: (i, 0, 0))
    wide = pl.BlockSpec((1, rows, model), lambda i: (i, 0, 0))
    total = 8 * rows
    return pl.pallas_call(
        feed_grads_kernel,
        name="feed_grads",
        grid=(4,),
        in_specs=[thin] * 4 + [wide] * 4 + [block(width, model)],
        out_specs=[wide, wide, block(width + 16, model), block(model, width)],
        scratch_shapes=[
            pltpu.VMEM((width, model), F32),
            pltpu.VMEM((model, width), F32),
            pltpu.VMEM((16, model), F32),
        ],
        out_shape=[
            shape_of((4, rows, model), BF16),
            shape_of((4, rows, model), BF16),
            shape_of((width + 16, model), BF16),
            shape_of((model, width), BF16),
        ],
        compiler_params=params(),
        cost_estimate=cost(6 * total * model * width, 2 * total * (3 * model + 2 * width) + 6 * model * width),
    )(*act, *grad, *normed, *cot, down)


def middle_kernel(meta, g0, g1, gx, gy, gd, hidden, cot, weights, vecs, hidden_grad_ref, grad_ref, sums_ref, d0, d1, d2, d3):
    width = d0.shape[1]
    z = meta[meta.shape[0] - 1]
    normed_grad = (g0[0].astype(F32) + g1[0].astype(F32)) + (gx[...].astype(F32) + gy[...].astype(F32))
    normed_grad = normed_grad + gd[...].astype(F32)
    unit, inverse = normalize(hidden[...])
    upstream = cot[...].astype(F32)
    hidden_grad = upstream + norm_back(normed_grad, unit, inverse, vecs[3:4])
    hidden_grad_ref[...] = hidden_grad
    grad = hidden_grad.astype(BF16)
    grad_ref[...] = grad
    for k, out in enumerate((d0, d1, d2, d3)):
        start = pl.multiple_of((z ^ k) * width, width)
        out[...] = mm_rt(grad, weights[pl.ds(start, width), :]).astype(BF16)
    sums_ref[0:1, :] = jnp.sum(normed_grad * unit, axis=0, keepdims=True)
    sums_ref[1:2, :] = jnp.sum(normed_grad, axis=0, keepdims=True)
    sums_ref[2:3, :] = jnp.sum(grad.astype(F32), axis=0, keepdims=True)
    sums_ref[3:4, :] = jnp.sum(upstream, axis=0, keepdims=True)


def middle(meta, stacks, moved, hidden, cot, weights, vecs):
    rows, model = hidden.shape
    width = model // ZS
    return pl.pallas_call(
        middle_kernel,
        name="middle",
        grid_spec=pltpu.PrefetchScalarGridSpec(
            num_scalar_prefetch=1,
            grid=(1,),
            in_specs=[block(1, rows, model)] * 2
            + [block(rows, model)] * 5
            + [block(model, model), block(*vecs.shape)],
            out_specs=[block(rows, model)] * 2 + [block(4, model)] + [block(rows, width)] * ZS,
        ),
        out_shape=[shape_of((rows, model), F32), shape_of((rows, model), BF16), shape_of((4, model), F32)]
        + [shape_of((rows, width), BF16)] * ZS,
        compiler_params=params(),
        cost_estimate=cost(2 * rows * model * model, rows * model * 26 + 2 * model * model),
    )(meta, *stacks, *moved, hidden, cot, weights, vecs)


def finish_kernel(x, mine, near, far, hidden_grad, vecs, out):
    unit, inverse = normalize(x[...].astype(F32))
    upstream = mine[0].astype(F32) + near[...].astype(F32) + far[...].astype(F32)
    out[...] = (hidden_grad[...] + norm_back(upstream, unit, inverse, vecs[0:1])).astype(BF16)


def finish(x, mine, near, far, hidden_grad, vecs):
    rows, model = x.shape
    steps = 3 if rows % 48 == 0 else 1
    part = pl.BlockSpec((rows // steps, model), lambda i: (i, 0))
    stack = pl.BlockSpec((1, rows // steps, model), lambda i: (0, i, 0))
    return pl.pallas_call(
        finish_kernel,
        name="finish",
        grid=(steps,),
        in_specs=[part, stack, part, part, part, block(*vecs.shape)],
        out_specs=part,
        out_shape=shape_of((rows, model), BF16),
        compiler_params=params(),
        cost_estimate=cost(20 * rows * model, rows * model * 12),
    )(x, mine, near, far, hidden_grad, vecs)


def per_device(
    inputs,
    lengths,
    cotangent,
    attn_gain,
    attn_shift,
    qkv_weight,
    qv_bias,
    proj_weight,
    proj_bias,
    mlp_gain,
    mlp_shift,
    up_weight,
    up_bias,
    down_weight,
    down_bias,
):
    count, local, model = inputs.shape
    size = lax.axis_size("fsdp")
    outer = size // TEAM
    place = lax.axis_index("fsdp").astype(jnp.uint32)
    seat = lax.axis_index("seq").astype(jnp.uint32)
    z = seat.astype(jnp.int32)
    team = place & (TEAM - 1)
    core = team & 1
    chip = team >> 1
    tokens = count * local
    width = model // ZS
    own_rows = qkv_weight.shape[0]
    hidden_units = up_weight.shape[1]
    feed_width = hidden_units // TEAM
    meta = jnp.concatenate([lengths.astype(jnp.int32), z.reshape(1)])

    rows = lax.all_gather(inputs, "seq", axis=0, tiled=False)

    def over_team(own):
        quad = jnp.stack([own] + [swap(own, 2 * m) for m in (1, 2, 3)])
        return jnp.concatenate([quad, swap(quad, 1)], axis=0)

    columns = [
        lax.dynamic_slice(qkv_weight, (jnp.uint32(0), seat * width + i * model), (own_rows, width)) for i in range(3)
    ]
    vectors = (attn_gain, attn_shift, proj_bias, mlp_gain, mlp_shift, down_bias)
    lanes, spot, packed = 3 * width, 0, []
    for vector in vectors:
        packed.append(jnp.pad(vector, (spot, lanes - spot - vector.shape[0])))
        spot += vector.shape[0]
    row_one = functools.reduce(jnp.add, packed).reshape(1, lanes)
    row_two = jnp.pad(qv_bias, (0, lanes - qv_bias.shape[0])).reshape(1, lanes)
    small_rows = jnp.pad(row_one, ((0, 7), (0, 0))) + jnp.pad(row_two, ((1, 6), (0, 0)))
    piece = jnp.concatenate([jnp.concatenate(columns, axis=1), small_rows], axis=0)
    pieces = over_team(piece)
    weights = jnp.stack([pick(pieces, ((j ^ team) & 1) * 4 + ((j ^ team) >> 1)) for j in range(TEAM)])
    weights = gather_over_outer(weights, size)
    vecs = weights[:, own_rows, : 6 * own_rows].reshape(size, 6, own_rows).transpose(1, 0, 2)
    vecs = vecs.reshape(6, model).astype(F32)
    bias_qv = weights[:, own_rows + 1, : qv_bias.shape[0]].reshape(1, 2 * model).astype(F32)
    bias_quarter = jnp.concatenate(
        [
            lax.dynamic_slice(bias_qv, (jnp.uint32(0), seat * width), (1, width)),
            jnp.zeros((1, width), F32),
            lax.dynamic_slice(bias_qv, (jnp.uint32(0), model + seat * width), (1, width)),
        ],
        axis=1,
    )
    proj = lax.all_gather(proj_weight, "fsdp", axis=0, tiled=True)

    up_blocks = up_weight.reshape(own_rows, outer, TEAM, feed_width // outer).transpose(2, 0, 1, 3)
    up_blocks = up_blocks.reshape(TEAM, own_rows, feed_width)
    groups = [[o * TEAM + t for t in range(TEAM)] for o in range(outer)]
    up = lax.all_to_all(
        up_blocks, "fsdp", split_axis=0, concat_axis=0, axis_index_groups=groups, tiled=True
    ).reshape(TEAM * own_rows, feed_width)
    up = gather_over_outer(up, size)
    down = gather_over_outer(down_weight, size)
    bias_up = gather_over_outer(up_bias, size).astype(F32).reshape(1, feed_width)

    half = model // 2

    def over_chips(own):
        by_x, by_y = swap(own, 2), swap(own, 4)
        diagonal = jnp.concatenate([swap(by_x[:, :half], 4), swap(by_y[:, half:], 2)], axis=1)
        return jnp.stack([own, by_x, by_y, diagonal])

    positions = z * local + jnp.arange(local, dtype=jnp.int32)
    row_valid = (positions[None, :] < lengths[:, None])[:, :, None]
    cot = jnp.where(row_valid, cotangent, jnp.zeros_like(cotangent)).reshape(tokens, model)
    cot_even = over_chips(cot)
    cot_odd = swap(cot_even, 1)

    def down_back(stack):
        out = lax.dot_general(stack, down, (((2,), (1,)), ((), ())), preferred_element_type=F32)
        return out

    above_even, above_odd = down_back(cot_even), down_back(cot_odd)

    qkv, normed_attn, *context = attend(meta, after(rows, above_even, above_odd, up), weights, vecs, bias_quarter)
    context = [context[0]] + [cross(context[k], k) for k in range(1, ZS)]
    own = inputs.reshape(tokens, model)
    hidden, normed = project(meta, context, own, proj, vecs)

    normed_even = over_chips(normed)
    normed_odd = swap(normed_even, 1)
    act_even, grad_even, back_even = feed(normed_even, above_even, up, bias_up)
    act_odd, grad_odd, back_odd = feed(normed_odd, above_odd, up, bias_up)
    back_core = swap(back_odd, 1)
    sums = [joined(back_even[m], back_core[m]) for m in (1, 2, 3)]
    moved = [swap(part, 2 * m) for m, part in zip((1, 2, 3), sums)]
    act_even = after(act_even, *sums)
    out_even, out_odd, down_part, up_part = feed_grads(
        (act_even, act_odd), (grad_even, grad_odd), (normed_even, normed_odd), (cot_even, cot_odd), down
    )
    if outer > 1:
        bias_part = rows_over_outer(down_part[feed_width, :feed_width].astype(F32), size)
        bias_part = jnp.pad(bias_part.reshape(1, -1), ((0, 15), (0, model - bias_part.shape[0])))
        down_part = rows_over_outer(down_part[:feed_width], size)
        down_part = jnp.concatenate([down_part, bias_part.astype(BF16)], axis=0)
    down_rows = down_weight.shape[0]
    up_part = rows_over_outer(up_part, size)
    down_total = lax.psum(down_part, "seq")
    side = seat & 1
    half_width = feed_width // 2
    up_keep, up_give = (
        lax.dynamic_slice(up_part, (jnp.uint32(0), part * half_width), (up_part.shape[0], half_width))
        for part in (side, 1 - side)
    )

    hidden_grad, attn_grad, mid_sums, *context_grad = middle(
        meta, (back_even, back_core), moved, after(hidden, out_even), cot, proj, vecs
    )

    def over_core(part, *others):
        keep, give = pick(part, core, 1), pick(part, 1 - core, 1)
        return joined(after(keep, *others), swap(give, 1))

    def over_team_chips(both, at, *others):
        total = after(pick(both, at(0)), *others).astype(F32)
        for m in (1, 2, 3):
            total = total + swap(pick(both, at(m)), 2 * m).astype(F32)
        return total.astype(BF16)

    proj_part = mm_lt(jnp.concatenate(context, axis=1), attn_grad)
    if outer == 1:
        proj_part = proj_part.astype(BF16).reshape(ZS, 2, own_rows, model)
        mid_rows = mid_sums.reshape(4, TEAM, own_rows).transpose(1, 0, 2).reshape(4, 2, 1, 4 * own_rows)
        mid_rows = jnp.pad(mid_rows, ((0, 0), (0, 0), (0, 7), (0, model - 4 * own_rows))).astype(BF16)
        mid_rows = jnp.stack([pick(mid_rows, seat ^ k) for k in range(ZS)])
        proj_part = jnp.concatenate([proj_part, mid_rows], axis=2)
        chip_at = lambda m: chip ^ m ^ seat
    else:
        proj_part = proj_part.reshape(ZS, width, model)
        proj_part = jnp.stack([pick(proj_part, seat ^ j) for j in range(ZS)]).reshape(model, model)
        proj_part = rows_over_outer(proj_part, size).astype(BF16).reshape(4, 2, own_rows, model)
        chip_at = lambda m: chip ^ m

    context_grad = [context_grad[0]] + [cross(context_grad[k], k) for k in range(1, ZS)]
    up_half = joined(after(up_keep, *context_grad), cross(up_give, 1))
    up_across = cross(up_half, 2)
    qkv_grad, mine, give, attn_sums = attend_back(meta, rows, context_grad, after(qkv, up_half), weights)

    qkv_part = mm_lt(normed_attn.reshape(-1, model), qkv_grad.reshape(-1, 3 * width)).astype(BF16)

    if outer == 1:
        qkv_part = qkv_part.reshape(4, 2, own_rows, 3 * width)
        gains = attn_sums[:2].reshape(2, TEAM, own_rows).transpose(1, 0, 2).reshape(4, 2, 1, 2 * own_rows)
        biases = jnp.concatenate([attn_sums[2, :width], attn_sums[2, 2 * width : 3 * width]])
        biases = jnp.broadcast_to(biases, (4, 2, 1, 2 * width))
        packed = jnp.concatenate([gains, biases], axis=3)
        packed = jnp.pad(packed, ((0, 0), (0, 0), (0, 7), (0, 3 * width - packed.shape[3]))).astype(BF16)
        qkv_part = jnp.concatenate([qkv_part, packed], axis=2)
    else:
        qkv_part = rows_over_outer(qkv_part, size).reshape(4, 2, own_rows, 3 * width)

    near = [cross(give[k], 1) for k in range(2)]
    qkv_both = over_core(qkv_part)
    proj_both = over_core(proj_part, qkv_both)
    middle_sum = joined(after(mine[1], proj_both), near[1])
    far = cross(middle_sum, 2)
    up_sum = lax.optimization_barrier(joined(after(up_half, middle_sum), up_across))
    up_sum = up_sum.reshape(4, 2, own_rows, half_width)
    qkv_mine = lax.optimization_barrier(over_team_chips(qkv_both, lambda m: chip ^ m, up_sum))
    pair = jnp.stack([after(pick(up_sum, core, 1), qkv_mine), swap(pick(up_sum, 1 - core, 1), 1)], axis=1)
    proj_mine = over_team_chips(proj_both, chip_at, pair)
    lanes = qkv_mine.shape[1]
    packed = jnp.concatenate([qkv_mine, proj_mine], axis=1)
    packed_two = cross(packed, 2)
    up_rel = [after(pick(pair, chip), packed)] + [swap(pick(pair, chip ^ m), 2 * m) for m in (1, 2, 3)]
    up_rel = lax.optimization_barrier(jnp.stack(up_rel).reshape(TEAM, own_rows, half_width))
    up_other = cross(up_rel, 1)
    out_core = swap(after(out_odd, give), 1)
    out_sums = [joined(after(out_even[m], up_rel), out_core[m]) for m in (1, 2, 3)]
    out_moved = [swap(part, 2 * m) for m, part in zip((1, 2, 3), out_sums)]
    down_grad = after(down_total, qkv_both)[:down_rows].astype(F32)
    input_grad = finish(own, mine, near[0], far, after(hidden_grad, *out_sums), vecs)
    qkv_two = after(packed_two, input_grad)[:, :lanes]
    proj_two = lax.optimization_barrier(joined(proj_mine, packed_two[:, lanes:]))
    packed_one = cross(jnp.concatenate([qkv_mine, qkv_two, proj_two], axis=1), 1)
    qkv_near = [packed_one[:, :lanes], packed_one[:, lanes : 2 * lanes]]
    proj_total = joined(proj_two, packed_one[:, 2 * lanes :]).astype(F32)
    input_grad = input_grad.reshape(inputs.shape)

    output = after(hidden, qkv_two) + vecs[5:6] + out_even[0].astype(F32) + out_core[0].astype(F32)
    for part in out_moved:
        output = output + part.astype(F32)
    output = jnp.where(row_valid, output.reshape(inputs.shape), 0.0).astype(BF16)

    up_bias_grad = down_total[down_rows, : up_bias.shape[0]].astype(F32)
    up_first = jnp.where(side == 0, up_rel, up_other)
    up_second = jnp.where(side == 0, up_other, up_rel)
    up_rel = jnp.concatenate([up_first, up_second], axis=2)
    up_grad = jnp.stack([pick(up_rel, j ^ team) for j in range(TEAM)], axis=1).astype(F32)
    up_grad = up_grad.reshape(own_rows, TEAM, outer, feed_width // outer).transpose(0, 2, 1, 3)
    up_grad = up_grad.reshape(own_rows, hidden_units)
    proj_grad = proj_total[:own_rows]
    qkv_parts = jnp.stack([qkv_mine, qkv_near[0], qkv_two, qkv_near[1]])
    ordered = [pick(qkv_parts, seat ^ j).astype(F32) for j in range(ZS)]
    qkv_weight_grad = jnp.concatenate(
        [part[:own_rows, i * width : (i + 1) * width] for i in range(3) for part in ordered], axis=1
    )

    if outer == 1:
        mid = proj_total[own_rows, : 4 * own_rows].reshape(4, own_rows)
        packed = jnp.stack([part[own_rows] for part in ordered])
        gains = packed[:, : 2 * own_rows]
        gains = (gains[0] + gains[1]) + (gains[2] + gains[3])
        attn_gain_grad, attn_shift_grad = gains[:own_rows], gains[own_rows:]
        mine = pick(packed, place & (ZS - 1))
        start = 2 * own_rows + (place >> 2) * width
        qv_bias_grad = lax.dynamic_slice(mine, (start,), (width,))
        mlp_gain_grad, mlp_shift_grad, proj_bias_grad, down_bias_grad = mid
    else:
        biases = jnp.zeros((2, ZS, width), F32)
        biases = lax.dynamic_update_slice(
            biases, jnp.stack([attn_sums[2, :width], attn_sums[2, 2 * width : 3 * width]])[:, None], (0, z, 0)
        )
        packed = jnp.concatenate([attn_sums[0], attn_sums[1], mid_sums.reshape(-1)]).reshape(6, size, own_rows)
        packed = jnp.concatenate([packed.transpose(1, 0, 2).reshape(size, -1), biases.reshape(size, -1)], axis=1)
        packed = lax.psum_scatter(packed, "fsdp", scatter_dimension=0, tiled=False)
        packed = lax.psum(packed, "seq")
        vectors = packed[: 6 * own_rows].reshape(6, own_rows)
        attn_gain_grad, attn_shift_grad, mlp_gain_grad, mlp_shift_grad, proj_bias_grad, down_bias_grad = vectors
        qv_bias_grad = packed[6 * own_rows :]

    return (
        output,
        input_grad,
        attn_gain_grad,
        attn_shift_grad,
        qkv_weight_grad,
        qv_bias_grad,
        proj_grad,
        proj_bias_grad,
        mlp_gain_grad,
        mlp_shift_grad,
        up_grad,
        up_bias_grad,
        down_grad,
        down_bias_grad,
    )


def solution(mesh):
    split = P("fsdp")
    tokens = P("fsdp", "seq", None)
    matrix = P("fsdp", None)
    in_specs = (tokens, split, tokens, split, split, matrix, split, matrix) + (split,) * 3 + (matrix, split, matrix, split)
    out_specs = (tokens, tokens, split, split, matrix, split, matrix) + (split,) * 3 + (matrix, split, matrix, split)
    return jax.shard_map(per_device, mesh=mesh, in_specs=in_specs, out_specs=out_specs, check_vma=False)
```

```python
import functools
import math

import jax
import jax.numpy as jnp
from jax import lax
from jax.experimental import pallas as pl
from jax.experimental.pallas import tpu as pltpu
from jax.sharding import PartitionSpec as P

HEAD = 64
EPSILON = 1e-06
MASKED = -1e30
TEAM = 8
ZS = 4
F32 = jnp.float32
BF16 = jnp.bfloat16
VMEM_BYTES = 56 * 1024 * 1024
SCALE = 1024


def params():
    return pltpu.CompilerParams(vmem_limit_bytes=VMEM_BYTES)


def cost(flops, nbytes, trans=0):
    return pl.CostEstimate(flops=int(flops) // SCALE, bytes_accessed=int(nbytes) // SCALE, transcendentals=int(trans) // SCALE)


def shape_of(dims, dtype):
    return jax.ShapeDtypeStruct(dims, dtype)


def mm(left, right):
    return lax.dot_general(left, right, (((1,), (0,)), ((), ())), preferred_element_type=F32)


def mm_rt(left, right):
    return lax.dot_general(left, right, (((1,), (1,)), ((), ())), preferred_element_type=F32)


def mm_lt(left, right):
    return lax.dot_general(left, right, (((0,), (0,)), ((), ())), preferred_element_type=F32)


def normalize(rows):
    center = rows - jnp.mean(rows, axis=-1, keepdims=True)
    inverse = lax.rsqrt(jnp.mean(center * center, axis=-1, keepdims=True) + EPSILON)
    return center * inverse, inverse


def norm_back(upstream, unit, inverse, gain):
    scaled = upstream * gain
    return inverse * (
        scaled
        - jnp.mean(scaled, axis=-1, keepdims=True)
        - unit * jnp.mean(scaled * unit, axis=-1, keepdims=True)
    )


def swap(value, mask):
    size = lax.axis_size("fsdp")
    return lax.ppermute(value, "fsdp", [(i, i ^ mask) for i in range(size)])


def cross(value, mask):
    return lax.ppermute(value, "seq", [(i, i ^ mask) for i in range(ZS)])


def joined(first, second):
    return (first.astype(F32) + second.astype(F32)).astype(BF16)


def after(value, *others):
    return lax.optimization_barrier((value,) + others)[0]


def pick(stack, index, axis=0):
    starts = [jnp.uint32(0)] * stack.ndim
    starts[axis] = index.astype(jnp.uint32)
    sizes = list(stack.shape)
    sizes[axis] = 1
    return lax.dynamic_slice(stack, starts, sizes).reshape(stack.shape[:axis] + stack.shape[axis + 1 :])


def outer_groups(size):
    outer = size // TEAM
    return [[o * TEAM + t for o in range(outer)] for t in range(TEAM)]


def rows_over_outer(value, size):
    if size == TEAM:
        return value
    return lax.psum_scatter(
        value, "fsdp", scatter_dimension=0, axis_index_groups=outer_groups(size), tiled=True
    )


def gather_over_outer(value, size):
    if size == TEAM:
        return value
    return lax.all_gather(value, "fsdp", axis=0, axis_index_groups=outer_groups(size), tiled=True)


def block(*dims):
    return pl.BlockSpec(dims, lambda *i: (0,) * len(dims))


def chosen(values, index):
    out = values[-1]
    for i in range(len(values) - 1):
        out = jnp.where(index == i, values[i], out)
    return out


def head_probs(queries, keys, valid):
    scores = mm_rt(keys, queries) * HEAD ** (-0.5)
    scores = jnp.where(valid, scores, MASKED)
    exponent = jnp.exp(scores - jnp.max(scores, axis=0, keepdims=True))
    return exponent * (1.0 / jnp.sum(exponent, axis=0, keepdims=True))


def both_heads(low, high):
    return jnp.concatenate([low[:HEAD], high[HEAD:]], axis=0).T


def attend_kernel(meta, rows_ref, wq, wk, wv, vecs, bias, qkv_ref, normed_ref, c0, c1, c2, c3):
    local = rows_ref.shape[2]
    slots = ZS * local
    model = rows_ref.shape[3]
    width = wq.shape[2]
    length = meta[pl.program_id(0)]
    z = meta[meta.shape[0] - 1]
    unit, _ = normalize(rows_ref[:, 0].reshape(slots, model).astype(F32))
    normed = (unit * vecs[0:1] + vecs[1:2]).astype(BF16)
    normed_ref[0] = normed
    parts = []
    for i, w in enumerate((wq, wk, wv)):
        part = (mm(normed, w[...].reshape(model, width)) + bias[:, i * width : (i + 1) * width]).astype(BF16)
        qkv_ref[0, :, i * width : (i + 1) * width] = part
        parts.append(part)
    valid = lax.broadcasted_iota(jnp.int32, (slots, slots), 0) < length
    first = lax.broadcasted_iota(jnp.int32, (1, 2 * HEAD), 1) < HEAD
    for pair in range(width // (2 * HEAD)):
        lanes = slice(pair * 2 * HEAD, (pair + 1) * 2 * HEAD)
        queries, keys, values = (part[:, lanes] for part in parts)
        outs = []
        for mine in (first, ~first):
            probs = head_probs(queries, jnp.where(mine, keys, jnp.zeros_like(keys)), valid)
            outs.append(mm_lt(values, probs.astype(BF16)))
        context = both_heads(*outs)
        pieces = [context[k * local : (k + 1) * local] for k in range(ZS)]
        for k, out in enumerate((c0, c1, c2, c3)):
            out[:, lanes] = chosen(pieces, z ^ k).astype(BF16)


def weight_specs(weights, own_rows, width):
    return [
        pl.BlockSpec((weights.shape[0], own_rows, width), functools.partial(lambda i, s, m: (0, 0, i), i))
        for i in range(3)
    ]


def attend(meta, rows, weights, vecs, bias):
    _, count, local, model = rows.shape
    slots, width = ZS * local, model // ZS
    flops = count * (2 * slots * model * 3 * width + 8 * slots * slots * width)
    per_sequence = lambda *dims: pl.BlockSpec((1,) + dims, lambda s, m: (s, 0, 0))
    return pl.pallas_call(
        attend_kernel,
        name="attend",
        grid_spec=pltpu.PrefetchScalarGridSpec(
            num_scalar_prefetch=1,
            grid=(count,),
            in_specs=[pl.BlockSpec((ZS, 1, local, model), lambda s, m: (0, s, 0, 0))]
            + weight_specs(weights, model // weights.shape[0], width)
            + [block(*vecs.shape), block(1, 3 * width)],
            out_specs=[per_sequence(slots, 3 * width), per_sequence(slots, model)]
            + [pl.BlockSpec((local, width), lambda s, m: (s, 0))] * ZS,
        ),
        out_shape=[shape_of((count, slots, 3 * width), BF16), shape_of((count, slots, model), BF16)]
        + [shape_of((count * local, width), BF16)] * ZS,
        compiler_params=params(),
        cost_estimate=cost(flops, 2 * count * slots * (2 * model + 4 * width) + 6 * model * width),
    )(meta, rows, weights, weights, weights, vecs, bias)


def attend_back_kernel(meta, rows_ref, d0, d1, d2, d3, qkv_ref, wq, wk, wv, *refs):
    dqkv_ref, keep_ref, give_ref, sums_ref = refs
    local = rows_ref.shape[2]
    slots = ZS * local
    model = rows_ref.shape[3]
    width = wq.shape[2]
    length = meta[pl.program_id(0)]
    z = meta[meta.shape[0] - 1]
    given = [d[...] for d in (d0, d1, d2, d3)]
    upstream = jnp.concatenate([chosen(given, z ^ k) for k in range(ZS)], axis=0)
    valid = lax.broadcasted_iota(jnp.int32, (slots, slots), 0) < length
    first = lax.broadcasted_iota(jnp.int32, (1, 2 * HEAD), 1) < HEAD
    for pair in range(width // (2 * HEAD)):
        spans = [slice(i * width + pair * 2 * HEAD, i * width + (pair + 1) * 2 * HEAD) for i in range(3)]
        queries, keys, values = (qkv_ref[0, :, span] for span in spans)
        above = upstream[:, spans[0]]
        grads = []
        for mine in (first, ~first):
            probs = head_probs(queries, jnp.where(mine, keys, jnp.zeros_like(keys)), valid)
            probs_grad = mm_rt(jnp.where(mine, values, jnp.zeros_like(values)), above)
            inner = jnp.sum(probs * probs_grad, axis=0, keepdims=True)
            scores_grad = (probs * (probs_grad - inner) * HEAD ** (-0.5)).astype(BF16)
            grads.append(
                (mm_lt(keys, scores_grad), mm(scores_grad, queries), mm(probs.astype(BF16), above))
            )
        dqkv_ref[0, :, spans[0]] = both_heads(grads[0][0], grads[1][0]).astype(BF16)
        for span, low, high in zip(spans[1:], grads[0][1:], grads[1][1:]):
            dqkv_ref[0, :, span] = jnp.where(first, low, high).astype(BF16)
    grad = dqkv_ref[0]
    total = mm_rt(grad[:, :width], wq[...].reshape(model, width))
    total = total + mm_rt(grad[:, width : 2 * width], wk[...].reshape(model, width))
    total = total + mm_rt(grad[:, 2 * width :], wv[...].reshape(model, width))
    pieces = [total[k * local : (k + 1) * local] for k in range(ZS)]
    for k in range(ZS):
        (keep_ref, give_ref)[k % 2][k // 2] = chosen(pieces, z ^ k).astype(BF16)
    unit, _ = normalize(rows_ref[:, 0].reshape(slots, model).astype(F32))

    @pl.when(pl.program_id(0) == 0)
    def _():
        sums_ref[...] = jnp.zeros_like(sums_ref)

    sums_ref[0:1, :] += jnp.sum(total * unit, axis=0, keepdims=True)
    sums_ref[1:2, :] += jnp.sum(total, axis=0, keepdims=True)
    sums_ref[2:3, : 3 * width] += jnp.sum(grad.astype(F32), axis=0, keepdims=True)


def attend_back(meta, rows, upstream, qkv, weights):
    _, count, local, model = rows.shape
    slots, width = ZS * local, model // ZS
    packed = pl.BlockSpec((1, slots, 3 * width), lambda s, m: (s, 0, 0))
    split = pl.BlockSpec((2, local, model), lambda s, m: (0, s, 0))
    flops = count * (2 * slots * model * 3 * width + 20 * slots * slots * width)
    return pl.pallas_call(
        attend_back_kernel,
        name="attend_back",
        grid_spec=pltpu.PrefetchScalarGridSpec(
            num_scalar_prefetch=1,
            grid=(count,),
            in_specs=[pl.BlockSpec((ZS, 1, local, model), lambda s, m: (0, s, 0, 0))]
            + [pl.BlockSpec((local, width), lambda s, m: (s, 0))] * ZS
            + [packed]
            + weight_specs(weights, model // weights.shape[0], width),
            out_specs=[packed, split, split, block(8, model)],
        ),
        out_shape=[shape_of((count, slots, 3 * width), BF16)]
        + [shape_of((2, count * local, model), BF16)] * 2
        + [shape_of((8, model), F32)],
        compiler_params=params(),
        cost_estimate=cost(flops, 2 * count * slots * (2 * model + 7 * width) + 6 * model * width),
    )(meta, rows, *upstream, qkv, weights, weights, weights)


def project_kernel(meta, c0, c1, c2, c3, x, weights, vecs, hidden_ref, normed_ref):
    width = c0.shape[1]
    z = meta[meta.shape[0] - 1]
    hidden = x[...].astype(F32) + vecs[2:3]
    for k, part in enumerate((c0, c1, c2, c3)):
        start = pl.multiple_of((z ^ k) * width, width)
        hidden = hidden + mm(part[...], weights[pl.ds(start, width), :])
    hidden_ref[...] = hidden
    unit, _ = normalize(hidden)
    normed_ref[...] = (unit * vecs[3:4] + vecs[4:5]).astype(BF16)


def project(meta, parts, x, weights, vecs):
    rows, model = x.shape
    return pl.pallas_call(
        project_kernel,
        name="project",
        grid_spec=pltpu.PrefetchScalarGridSpec(
            num_scalar_prefetch=1,
            grid=(1,),
            in_specs=[block(*part.shape) for part in parts]
            + [block(rows, model), block(model, model), block(*vecs.shape)],
            out_specs=[block(rows, model)] * 2,
        ),
        out_shape=[shape_of((rows, model), F32), shape_of((rows, model), BF16)],
        compiler_params=params(),
        cost_estimate=cost(2 * rows * model * model, rows * model * 10 + 2 * model * model),
    )(meta, *parts, x, weights, vecs)


def feed_kernel(normed, above, up, bias, act_ref, grad_ref, back_ref):
    count, rows, model = normed.shape
    width = up.shape[1]
    value = mm(normed[...].reshape(count * rows, model), up[...]) + bias[...]
    square = value * value
    root = math.sqrt(2.0 / math.pi)
    bend = jnp.tanh(root * value * (1.0 + 0.044715 * square))
    half = 0.5 * (1.0 + bend)
    act_ref[...] = (value * half).astype(BF16).reshape(count, rows, width)
    slope = half + 0.5 * value * (1.0 - bend * bend) * (root + 3 * 0.044715 * root * square)
    grad = (above[...].reshape(count * rows, width) * slope).astype(BF16)
    grad_ref[...] = grad.reshape(count, rows, width)
    back_ref[...] = mm_rt(grad, up[...]).astype(BF16).reshape(count, rows, model)


def feed(normed, above, up, bias):
    count, rows, model = normed.shape
    width = up.shape[1]
    wide = pl.BlockSpec((2, rows, model), lambda i: (i, 0, 0))
    thin = pl.BlockSpec((2, rows, width), lambda i: (i, 0, 0))
    return pl.pallas_call(
        feed_kernel,
        name="feed",
        grid=(count // 2,),
        in_specs=[wide, thin, block(model, width), block(1, width)],
        out_specs=[thin, thin, wide],
        out_shape=[shape_of((count, rows, width), BF16)] * 2 + [shape_of((count, rows, model), BF16)],
        compiler_params=params(),
        cost_estimate=cost(
            count * rows * 4 * model * width,
            count * rows * (4 * model + 8 * width) + 2 * model * width,
            count * rows * width,
        ),
    )(normed, above, up, bias)


def feed_grads_kernel(
    act_e, act_o, grad_e, grad_o, normed_e, normed_o, cot_e, cot_o, down, out_e, out_o, down_ref, up_ref, down_sum, up_sum, bias_sum
):
    rows = act_e.shape[1]
    width = down.shape[0]
    act = jnp.concatenate([act_e[0], act_o[0]], axis=0)
    grad = jnp.concatenate([grad_e[0], grad_o[0]], axis=0)
    out = mm(act, down[...]).astype(BF16)
    out_e[0] = out[:rows]
    out_o[0] = out[rows:]

    @pl.when(pl.program_id(0) == 0)
    def _():
        down_sum[...] = jnp.zeros_like(down_sum)
        up_sum[...] = jnp.zeros_like(up_sum)
        bias_sum[...] = jnp.zeros_like(bias_sum)

    down_sum[...] += mm_lt(act, jnp.concatenate([cot_e[0], cot_o[0]], axis=0))
    up_sum[...] += mm_lt(jnp.concatenate([normed_e[0], normed_o[0]], axis=0), grad)
    bias_sum[0:1, :width] += jnp.sum(grad.astype(F32), axis=0, keepdims=True)

    @pl.when(pl.program_id(0) == pl.num_programs(0) - 1)
    def _():
        down_ref[:width] = down_sum[...].astype(BF16)
        down_ref[width:] = bias_sum[...].astype(BF16)
        up_ref[...] = up_sum[...].astype(BF16)


def feed_grads(act, grad, normed, cot, down):
    _, rows, width = act[0].shape
    model = down.shape[1]
    thin = pl.BlockSpec((1, rows, width), lambda i: (i, 0, 0))
    wide = pl.BlockSpec((1, rows, model), lambda i: (i, 0, 0))
    total = 8 * rows
    return pl.pallas_call(
        feed_grads_kernel,
        name="feed_grads",
        grid=(4,),
        in_specs=[thin] * 4 + [wide] * 4 + [block(width, model)],
        out_specs=[wide, wide, block(width + 16, model), block(model, width)],
        scratch_shapes=[
            pltpu.VMEM((width, model), F32),
            pltpu.VMEM((model, width), F32),
            pltpu.VMEM((16, model), F32),
        ],
        out_shape=[
            shape_of((4, rows, model), BF16),
            shape_of((4, rows, model), BF16),
            shape_of((width + 16, model), BF16),
            shape_of((model, width), BF16),
        ],
        compiler_params=params(),
        cost_estimate=cost(6 * total * model * width, 2 * total * (3 * model + 2 * width) + 6 * model * width),
    )(*act, *grad, *normed, *cot, down)


def middle_kernel(meta, g0, g1, gx, gy, gd, hidden, cot, weights, vecs, hidden_grad_ref, grad_ref, sums_ref, d0, d1, d2, d3):
    width = d0.shape[1]
    z = meta[meta.shape[0] - 1]
    normed_grad = (g0[0].astype(F32) + g1[0].astype(F32)) + (gx[...].astype(F32) + gy[...].astype(F32))
    normed_grad = normed_grad + gd[...].astype(F32)
    unit, inverse = normalize(hidden[...])
    upstream = cot[...].astype(F32)
    hidden_grad = upstream + norm_back(normed_grad, unit, inverse, vecs[3:4])
    hidden_grad_ref[...] = hidden_grad
    grad = hidden_grad.astype(BF16)
    grad_ref[...] = grad
    for k, out in enumerate((d0, d1, d2, d3)):
        start = pl.multiple_of((z ^ k) * width, width)
        out[...] = mm_rt(grad, weights[pl.ds(start, width), :]).astype(BF16)
    sums_ref[0:1, :] = jnp.sum(normed_grad * unit, axis=0, keepdims=True)
    sums_ref[1:2, :] = jnp.sum(normed_grad, axis=0, keepdims=True)
    sums_ref[2:3, :] = jnp.sum(grad.astype(F32), axis=0, keepdims=True)
    sums_ref[3:4, :] = jnp.sum(upstream, axis=0, keepdims=True)


def middle(meta, stacks, moved, hidden, cot, weights, vecs):
    rows, model = hidden.shape
    width = model // ZS
    return pl.pallas_call(
        middle_kernel,
        name="middle",
        grid_spec=pltpu.PrefetchScalarGridSpec(
            num_scalar_prefetch=1,
            grid=(1,),
            in_specs=[block(1, rows, model)] * 2
            + [block(rows, model)] * 5
            + [block(model, model), block(*vecs.shape)],
            out_specs=[block(rows, model)] * 2 + [block(4, model)] + [block(rows, width)] * ZS,
        ),
        out_shape=[shape_of((rows, model), F32), shape_of((rows, model), BF16), shape_of((4, model), F32)]
        + [shape_of((rows, width), BF16)] * ZS,
        compiler_params=params(),
        cost_estimate=cost(2 * rows * model * model, rows * model * 26 + 2 * model * model),
    )(meta, *stacks, *moved, hidden, cot, weights, vecs)


def finish_kernel(x, mine, near, far, hidden_grad, vecs, out):
    unit, inverse = normalize(x[...].astype(F32))
    upstream = mine[0].astype(F32) + near[...].astype(F32) + far[...].astype(F32)
    out[...] = (hidden_grad[...] + norm_back(upstream, unit, inverse, vecs[0:1])).astype(BF16)


def finish(x, mine, near, far, hidden_grad, vecs):
    rows, model = x.shape
    steps = 3 if rows % 48 == 0 else 1
    part = pl.BlockSpec((rows // steps, model), lambda i: (i, 0))
    stack = pl.BlockSpec((1, rows // steps, model), lambda i: (0, i, 0))
    return pl.pallas_call(
        finish_kernel,
        name="finish",
        grid=(steps,),
        in_specs=[part, stack, part, part, part, block(*vecs.shape)],
        out_specs=part,
        out_shape=shape_of((rows, model), BF16),
        compiler_params=params(),
        cost_estimate=cost(20 * rows * model, rows * model * 12),
    )(x, mine, near, far, hidden_grad, vecs)


def per_device(
    inputs,
    lengths,
    cotangent,
    attn_gain,
    attn_shift,
    qkv_weight,
    qv_bias,
    proj_weight,
    proj_bias,
    mlp_gain,
    mlp_shift,
    up_weight,
    up_bias,
    down_weight,
    down_bias,
):
    count, local, model = inputs.shape
    size = lax.axis_size("fsdp")
    outer = size // TEAM
    place = lax.axis_index("fsdp").astype(jnp.uint32)
    seat = lax.axis_index("seq").astype(jnp.uint32)
    z = seat.astype(jnp.int32)
    team = place & (TEAM - 1)
    core = team & 1
    chip = team >> 1
    tokens = count * local
    width = model // ZS
    own_rows = qkv_weight.shape[0]
    hidden_units = up_weight.shape[1]
    feed_width = hidden_units // TEAM
    meta = jnp.concatenate([lengths.astype(jnp.int32), z.reshape(1)])

    rows = lax.all_gather(inputs, "seq", axis=0, tiled=False)

    def over_team(own):
        quad = jnp.stack([own] + [swap(own, 2 * m) for m in (1, 2, 3)])
        return jnp.concatenate([quad, swap(quad, 1)], axis=0)

    columns = [
        lax.dynamic_slice(qkv_weight, (jnp.uint32(0), seat * width + i * model), (own_rows, width)) for i in range(3)
    ]
    vectors = (attn_gain, attn_shift, proj_bias, mlp_gain, mlp_shift, down_bias)
    lanes, spot, packed = 3 * width, 0, []
    for vector in vectors:
        packed.append(jnp.pad(vector, (spot, lanes - spot - vector.shape[0])))
        spot += vector.shape[0]
    row_one = functools.reduce(jnp.add, packed).reshape(1, lanes)
    row_two = jnp.pad(qv_bias, (0, lanes - qv_bias.shape[0])).reshape(1, lanes)
    small_rows = jnp.pad(row_one, ((0, 7), (0, 0))) + jnp.pad(row_two, ((1, 6), (0, 0)))
    piece = jnp.concatenate([jnp.concatenate(columns, axis=1), small_rows], axis=0)
    pieces = over_team(piece)
    weights = jnp.stack([pick(pieces, ((j ^ team) & 1) * 4 + ((j ^ team) >> 1)) for j in range(TEAM)])
    weights = gather_over_outer(weights, size)
    vecs = weights[:, own_rows, : 6 * own_rows].reshape(size, 6, own_rows).transpose(1, 0, 2)
    vecs = vecs.reshape(6, model).astype(F32)
    bias_qv = weights[:, own_rows + 1, : qv_bias.shape[0]].reshape(1, 2 * model).astype(F32)
    bias_quarter = jnp.concatenate(
        [
            lax.dynamic_slice(bias_qv, (jnp.uint32(0), seat * width), (1, width)),
            jnp.zeros((1, width), F32),
            lax.dynamic_slice(bias_qv, (jnp.uint32(0), model + seat * width), (1, width)),
        ],
        axis=1,
    )
    proj = lax.all_gather(proj_weight, "fsdp", axis=0, tiled=True)

    up_blocks = up_weight.reshape(own_rows, outer, TEAM, feed_width // outer).transpose(2, 0, 1, 3)
    up_blocks = up_blocks.reshape(TEAM, own_rows, feed_width)
    groups = [[o * TEAM + t for t in range(TEAM)] for o in range(outer)]
    up = lax.all_to_all(
        up_blocks, "fsdp", split_axis=0, concat_axis=0, axis_index_groups=groups, tiled=True
    ).reshape(TEAM * own_rows, feed_width)
    up = gather_over_outer(up, size)
    down = gather_over_outer(down_weight, size)
    bias_up = gather_over_outer(up_bias, size).astype(F32).reshape(1, feed_width)

    half = model // 2

    def over_chips(own):
        by_x, by_y = swap(own, 2), swap(own, 4)
        diagonal = jnp.concatenate([swap(by_x[:, :half], 4), swap(by_y[:, half:], 2)], axis=1)
        return jnp.stack([own, by_x, by_y, diagonal])

    positions = z * local + jnp.arange(local, dtype=jnp.int32)
    row_valid = (positions[None, :] < lengths[:, None])[:, :, None]
    cot = jnp.where(row_valid, cotangent, jnp.zeros_like(cotangent)).reshape(tokens, model)
    cot_even = over_chips(cot)
    cot_odd = swap(cot_even, 1)

    def down_back(stack):
        out = lax.dot_general(stack, down, (((2,), (1,)), ((), ())), preferred_element_type=F32)
        return out

    above_even, above_odd = down_back(cot_even), down_back(cot_odd)

    qkv, normed_attn, *context = attend(meta, after(rows, above_even, above_odd, up), weights, vecs, bias_quarter)
    context = [context[0]] + [cross(context[k], k) for k in range(1, ZS)]
    own = inputs.reshape(tokens, model)
    hidden, normed = project(meta, context, own, proj, vecs)

    normed_even = over_chips(normed)
    normed_odd = swap(normed_even, 1)
    act_even, grad_even, back_even = feed(normed_even, above_even, up, bias_up)
    act_odd, grad_odd, back_odd = feed(normed_odd, above_odd, up, bias_up)
    back_core = swap(back_odd, 1)
    sums = [joined(back_even[m], back_core[m]) for m in (1, 2, 3)]
    moved = [swap(part, 2 * m) for m, part in zip((1, 2, 3), sums)]
    act_even = after(act_even, *sums)
    out_even, out_odd, down_part, up_part = feed_grads(
        (act_even, act_odd), (grad_even, grad_odd), (normed_even, normed_odd), (cot_even, cot_odd), down
    )
    if outer > 1:
        bias_part = rows_over_outer(down_part[feed_width, :feed_width].astype(F32), size)
        bias_part = jnp.pad(bias_part.reshape(1, -1), ((0, 15), (0, model - bias_part.shape[0])))
        down_part = rows_over_outer(down_part[:feed_width], size)
        down_part = jnp.concatenate([down_part, bias_part.astype(BF16)], axis=0)
    down_rows = down_weight.shape[0]
    up_part = rows_over_outer(up_part, size)
    down_total = lax.psum(down_part, "seq")
    side = seat & 1
    half_width = feed_width // 2
    up_keep, up_give = (
        lax.dynamic_slice(up_part, (jnp.uint32(0), part * half_width), (up_part.shape[0], half_width))
        for part in (side, 1 - side)
    )

    hidden_grad, attn_grad, mid_sums, *context_grad = middle(
        meta, (back_even, back_core), moved, after(hidden, out_even), cot, proj, vecs
    )

    def over_core(part, *others):
        keep, give = pick(part, core, 1), pick(part, 1 - core, 1)
        return joined(after(keep, *others), swap(give, 1))

    def over_team_chips(both, at, *others):
        total = after(pick(both, at(0)), *others).astype(F32)
        for m in (1, 2, 3):
            total = total + swap(pick(both, at(m)), 2 * m).astype(F32)
        return total.astype(BF16)

    proj_part = mm_lt(jnp.concatenate(context, axis=1), attn_grad)
    if outer == 1:
        proj_part = proj_part.astype(BF16).reshape(ZS, 2, own_rows, model)
        mid_rows = mid_sums.reshape(4, TEAM, own_rows).transpose(1, 0, 2).reshape(4, 2, 1, 4 * own_rows)
        mid_rows = jnp.pad(mid_rows, ((0, 0), (0, 0), (0, 7), (0, model - 4 * own_rows))).astype(BF16)
        mid_rows = jnp.stack([pick(mid_rows, seat ^ k) for k in range(ZS)])
        proj_part = jnp.concatenate([proj_part, mid_rows], axis=2)
        chip_at = lambda m: chip ^ m ^ seat
    else:
        proj_part = proj_part.reshape(ZS, width, model)
        proj_part = jnp.stack([pick(proj_part, seat ^ j) for j in range(ZS)]).reshape(model, model)
        proj_part = rows_over_outer(proj_part, size).astype(BF16).reshape(4, 2, own_rows, model)
        chip_at = lambda m: chip ^ m

    context_grad = [context_grad[0]] + [cross(context_grad[k], k) for k in range(1, ZS)]
    up_half = joined(after(up_keep, *context_grad), cross(up_give, 1))
    up_across = cross(up_half, 2)
    qkv_grad, mine, give, attn_sums = attend_back(meta, rows, context_grad, after(qkv, up_half), weights)

    qkv_part = mm_lt(normed_attn.reshape(-1, model), qkv_grad.reshape(-1, 3 * width)).astype(BF16)

    if outer == 1:
        qkv_part = qkv_part.reshape(4, 2, own_rows, 3 * width)
        gains = attn_sums[:2].reshape(2, TEAM, own_rows).transpose(1, 0, 2).reshape(4, 2, 1, 2 * own_rows)
        biases = jnp.concatenate([attn_sums[2, :width], attn_sums[2, 2 * width : 3 * width]])
        biases = jnp.broadcast_to(biases, (4, 2, 1, 2 * width))
        packed = jnp.concatenate([gains, biases], axis=3)
        packed = jnp.pad(packed, ((0, 0), (0, 0), (0, 7), (0, 3 * width - packed.shape[3]))).astype(BF16)
        qkv_part = jnp.concatenate([qkv_part, packed], axis=2)
    else:
        qkv_part = rows_over_outer(qkv_part, size).reshape(4, 2, own_rows, 3 * width)

    near = [cross(give[k], 1) for k in range(2)]
    qkv_both = over_core(qkv_part)
    proj_both = over_core(proj_part, qkv_both)
    middle_sum = joined(after(mine[1], proj_both), near[1])
    far = cross(middle_sum, 2)
    up_sum = lax.optimization_barrier(joined(after(up_half, middle_sum), up_across))
    up_sum = up_sum.reshape(4, 2, own_rows, half_width)
    pair = jnp.stack([pick(up_sum, core, 1), swap(pick(up_sum, 1 - core, 1), 1)], axis=1)
    up_moved = [swap(pick(pair, chip ^ m), 2 * m) for m in (1, 2, 3)]
    out_core = swap(after(out_odd, give), 1)
    out_sums = [joined(after(out_even[m], up_sum), out_core[m]) for m in (1, 2, 3)]
    out_moved = [swap(part, 2 * m) for m, part in zip((1, 2, 3), out_sums)]
    down_grad = after(down_total, qkv_both)[:down_rows].astype(F32)
    input_grad = finish(own, mine, near[0], far, after(hidden_grad, pair, down_grad, *out_sums), vecs)
    qkv_mine = lax.optimization_barrier(over_team_chips(qkv_both, lambda m: chip ^ m, up_sum))
    proj_mine = over_team_chips(proj_both, chip_at, up_sum)
    lanes = qkv_mine.shape[1]
    packed = jnp.concatenate([after(qkv_mine, far), proj_mine], axis=1)
    packed_two = cross(packed, 2)
    up_rel = jnp.stack([after(pick(pair, chip), packed)] + up_moved)
    up_rel = lax.optimization_barrier(up_rel.reshape(TEAM, own_rows, half_width))
    up_other = cross(up_rel, 1)
    packed_two = after(packed_two, up_rel)
    qkv_two = packed_two[:, :lanes]
    proj_two = lax.optimization_barrier(joined(proj_mine, packed_two[:, lanes:]))
    packed_one = cross(jnp.concatenate([qkv_mine, qkv_two, proj_two], axis=1), 1)
    qkv_near = [packed_one[:, :lanes], packed_one[:, lanes : 2 * lanes]]
    proj_total = joined(proj_two, packed_one[:, 2 * lanes :]).astype(F32)
    input_grad = input_grad.reshape(inputs.shape)

    output = after(hidden, qkv_two) + vecs[5:6] + out_even[0].astype(F32) + out_core[0].astype(F32)
    for part in out_moved:
        output = output + part.astype(F32)
    output = jnp.where(row_valid, output.reshape(inputs.shape), 0.0).astype(BF16)

    up_bias_grad = down_total[down_rows, : up_bias.shape[0]].astype(F32)
    up_first = jnp.where(side == 0, up_rel, up_other)
    up_second = jnp.where(side == 0, up_other, up_rel)
    up_rel = jnp.concatenate([up_first, up_second], axis=2)
    up_grad = jnp.stack([pick(up_rel, j ^ team) for j in range(TEAM)], axis=1).astype(F32)
    up_grad = up_grad.reshape(own_rows, TEAM, outer, feed_width // outer).transpose(0, 2, 1, 3)
    up_grad = up_grad.reshape(own_rows, hidden_units)
    proj_grad = proj_total[:own_rows]
    qkv_parts = jnp.stack([qkv_mine, qkv_near[0], qkv_two, qkv_near[1]])
    ordered = [pick(qkv_parts, seat ^ j).astype(F32) for j in range(ZS)]
    qkv_weight_grad = jnp.concatenate(
        [part[:own_rows, i * width : (i + 1) * width] for i in range(3) for part in ordered], axis=1
    )

    if outer == 1:
        mid = proj_total[own_rows, : 4 * own_rows].reshape(4, own_rows)
        packed = jnp.stack([part[own_rows] for part in ordered])
        gains = packed[:, : 2 * own_rows]
        gains = (gains[0] + gains[1]) + (gains[2] + gains[3])
        attn_gain_grad, attn_shift_grad = gains[:own_rows], gains[own_rows:]
        mine = pick(packed, place & (ZS - 1))
        start = 2 * own_rows + (place >> 2) * width
        qv_bias_grad = lax.dynamic_slice(mine, (start,), (width,))
        mlp_gain_grad, mlp_shift_grad, proj_bias_grad, down_bias_grad = mid
    else:
        biases = jnp.zeros((2, ZS, width), F32)
        biases = lax.dynamic_update_slice(
            biases, jnp.stack([attn_sums[2, :width], attn_sums[2, 2 * width : 3 * width]])[:, None], (0, z, 0)
        )
        packed = jnp.concatenate([attn_sums[0], attn_sums[1], mid_sums.reshape(-1)]).reshape(6, size, own_rows)
        packed = jnp.concatenate([packed.transpose(1, 0, 2).reshape(size, -1), biases.reshape(size, -1)], axis=1)
        packed = lax.psum_scatter(packed, "fsdp", scatter_dimension=0, tiled=False)
        packed = lax.psum(packed, "seq")
        vectors = packed[: 6 * own_rows].reshape(6, own_rows)
        attn_gain_grad, attn_shift_grad, mlp_gain_grad, mlp_shift_grad, proj_bias_grad, down_bias_grad = vectors
        qv_bias_grad = packed[6 * own_rows :]

    return (
        output,
        input_grad,
        attn_gain_grad,
        attn_shift_grad,
        qkv_weight_grad,
        qv_bias_grad,
        proj_grad,
        proj_bias_grad,
        mlp_gain_grad,
        mlp_shift_grad,
        up_grad,
        up_bias_grad,
        down_grad,
        down_bias_grad,
    )


def solution(mesh):
    split = P("fsdp")
    tokens = P("fsdp", "seq", None)
    matrix = P("fsdp", None)
    in_specs = (tokens, split, tokens, split, split, matrix, split, matrix) + (split,) * 3 + (matrix, split, matrix, split)
    out_specs = (tokens, tokens, split, split, matrix, split, matrix) + (split,) * 3 + (matrix, split, matrix, split)
    return jax.shard_map(per_device, mesh=mesh, in_specs=in_specs, out_specs=out_specs, check_vma=False)
```

```python
import functools
import math

import jax
import jax.numpy as jnp
from jax import lax
from jax.experimental import pallas as pl
from jax.experimental.pallas import tpu as pltpu
from jax.sharding import PartitionSpec as P

HEAD = 64
EPSILON = 1e-06
MASKED = -1e30
TEAM = 8
ZS = 4
F32 = jnp.float32
BF16 = jnp.bfloat16
VMEM_BYTES = 56 * 1024 * 1024
SCALE = 1024


def params():
    return pltpu.CompilerParams(vmem_limit_bytes=VMEM_BYTES)


def cost(flops, nbytes, trans=0):
    return pl.CostEstimate(flops=int(flops) // SCALE, bytes_accessed=int(nbytes) // SCALE, transcendentals=int(trans) // SCALE)


def shape_of(dims, dtype):
    return jax.ShapeDtypeStruct(dims, dtype)


def mm(left, right):
    return lax.dot_general(left, right, (((1,), (0,)), ((), ())), preferred_element_type=F32)


def mm_rt(left, right):
    return lax.dot_general(left, right, (((1,), (1,)), ((), ())), preferred_element_type=F32)


def mm_lt(left, right):
    return lax.dot_general(left, right, (((0,), (0,)), ((), ())), preferred_element_type=F32)


def normalize(rows):
    center = rows - jnp.mean(rows, axis=-1, keepdims=True)
    inverse = lax.rsqrt(jnp.mean(center * center, axis=-1, keepdims=True) + EPSILON)
    return center * inverse, inverse


def norm_back(upstream, unit, inverse, gain):
    scaled = upstream * gain
    return inverse * (
        scaled
        - jnp.mean(scaled, axis=-1, keepdims=True)
        - unit * jnp.mean(scaled * unit, axis=-1, keepdims=True)
    )


def swap(value, mask):
    size = lax.axis_size("fsdp")
    return lax.ppermute(value, "fsdp", [(i, i ^ mask) for i in range(size)])


def cross(value, mask):
    return lax.ppermute(value, "seq", [(i, i ^ mask) for i in range(ZS)])


def joined(first, second):
    return (first.astype(F32) + second.astype(F32)).astype(BF16)


def after(value, *others):
    return lax.optimization_barrier((value,) + others)[0]


def pick(stack, index, axis=0):
    starts = [jnp.uint32(0)] * stack.ndim
    starts[axis] = index.astype(jnp.uint32)
    sizes = list(stack.shape)
    sizes[axis] = 1
    return lax.dynamic_slice(stack, starts, sizes).reshape(stack.shape[:axis] + stack.shape[axis + 1 :])


def outer_groups(size):
    outer = size // TEAM
    return [[o * TEAM + t for o in range(outer)] for t in range(TEAM)]


def rows_over_outer(value, size):
    if size == TEAM:
        return value
    return lax.psum_scatter(
        value, "fsdp", scatter_dimension=0, axis_index_groups=outer_groups(size), tiled=True
    )


def gather_over_outer(value, size):
    if size == TEAM:
        return value
    return lax.all_gather(value, "fsdp", axis=0, axis_index_groups=outer_groups(size), tiled=True)


def block(*dims):
    return pl.BlockSpec(dims, lambda *i: (0,) * len(dims))


def chosen(values, index):
    out = values[-1]
    for i in range(len(values) - 1):
        out = jnp.where(index == i, values[i], out)
    return out


def head_probs(queries, keys, valid):
    scores = mm_rt(keys, queries) * HEAD ** (-0.5)
    scores = jnp.where(valid, scores, MASKED)
    exponent = jnp.exp(scores - jnp.max(scores, axis=0, keepdims=True))
    return exponent * (1.0 / jnp.sum(exponent, axis=0, keepdims=True))


def both_heads(low, high):
    return jnp.concatenate([low[:HEAD], high[HEAD:]], axis=0).T


def attend_kernel(meta, rows_ref, wq, wk, wv, vecs, bias, qkv_ref, normed_ref, c0, c1, c2, c3):
    local = rows_ref.shape[2]
    slots = ZS * local
    model = rows_ref.shape[3]
    width = wq.shape[2]
    length = meta[pl.program_id(0)]
    z = meta[meta.shape[0] - 1]
    unit, _ = normalize(rows_ref[:, 0].reshape(slots, model).astype(F32))
    normed = (unit * vecs[0:1] + vecs[1:2]).astype(BF16)
    normed_ref[0] = normed
    parts = []
    for i, w in enumerate((wq, wk, wv)):
        part = (mm(normed, w[...].reshape(model, width)) + bias[:, i * width : (i + 1) * width]).astype(BF16)
        qkv_ref[0, :, i * width : (i + 1) * width] = part
        parts.append(part)
    valid = lax.broadcasted_iota(jnp.int32, (slots, slots), 0) < length
    first = lax.broadcasted_iota(jnp.int32, (1, 2 * HEAD), 1) < HEAD
    for pair in range(width // (2 * HEAD)):
        lanes = slice(pair * 2 * HEAD, (pair + 1) * 2 * HEAD)
        queries, keys, values = (part[:, lanes] for part in parts)
        outs = []
        for mine in (first, ~first):
            probs = head_probs(queries, jnp.where(mine, keys, jnp.zeros_like(keys)), valid)
            outs.append(mm_lt(values, probs.astype(BF16)))
        context = both_heads(*outs)
        pieces = [context[k * local : (k + 1) * local] for k in range(ZS)]
        for k, out in enumerate((c0, c1, c2, c3)):
            out[:, lanes] = chosen(pieces, z ^ k).astype(BF16)


def weight_specs(weights, own_rows, width):
    return [
        pl.BlockSpec((weights.shape[0], own_rows, width), functools.partial(lambda i, s, m: (0, 0, i), i))
        for i in range(3)
    ]


def attend(meta, rows, weights, vecs, bias):
    _, count, local, model = rows.shape
    slots, width = ZS * local, model // ZS
    flops = count * (2 * slots * model * 3 * width + 8 * slots * slots * width)
    per_sequence = lambda *dims: pl.BlockSpec((1,) + dims, lambda s, m: (s, 0, 0))
    return pl.pallas_call(
        attend_kernel,
        name="attend",
        grid_spec=pltpu.PrefetchScalarGridSpec(
            num_scalar_prefetch=1,
            grid=(count,),
            in_specs=[pl.BlockSpec((ZS, 1, local, model), lambda s, m: (0, s, 0, 0))]
            + weight_specs(weights, model // weights.shape[0], width)
            + [block(*vecs.shape), block(1, 3 * width)],
            out_specs=[per_sequence(slots, 3 * width), per_sequence(slots, model)]
            + [pl.BlockSpec((local, width), lambda s, m: (s, 0))] * ZS,
        ),
        out_shape=[shape_of((count, slots, 3 * width), BF16), shape_of((count, slots, model), BF16)]
        + [shape_of((count * local, width), BF16)] * ZS,
        compiler_params=params(),
        cost_estimate=cost(flops, 2 * count * slots * (2 * model + 4 * width) + 6 * model * width),
    )(meta, rows, weights, weights, weights, vecs, bias)


def attend_back_kernel(meta, rows_ref, d0, d1, d2, d3, qkv_ref, wq, wk, wv, *refs):
    dqkv_ref, sums_ref, *outs = refs
    local = rows_ref.shape[2]
    slots = ZS * local
    model = rows_ref.shape[3]
    width = wq.shape[2]
    length = meta[pl.program_id(0)]
    z = meta[meta.shape[0] - 1]
    given = [d[...] for d in (d0, d1, d2, d3)]
    upstream = jnp.concatenate([chosen(given, z ^ k) for k in range(ZS)], axis=0)
    valid = lax.broadcasted_iota(jnp.int32, (slots, slots), 0) < length
    first = lax.broadcasted_iota(jnp.int32, (1, 2 * HEAD), 1) < HEAD
    for pair in range(width // (2 * HEAD)):
        spans = [slice(i * width + pair * 2 * HEAD, i * width + (pair + 1) * 2 * HEAD) for i in range(3)]
        queries, keys, values = (qkv_ref[0, :, span] for span in spans)
        above = upstream[:, spans[0]]
        grads = []
        for mine in (first, ~first):
            probs = head_probs(queries, jnp.where(mine, keys, jnp.zeros_like(keys)), valid)
            probs_grad = mm_rt(jnp.where(mine, values, jnp.zeros_like(values)), above)
            inner = jnp.sum(probs * probs_grad, axis=0, keepdims=True)
            scores_grad = (probs * (probs_grad - inner) * HEAD ** (-0.5)).astype(BF16)
            grads.append(
                (mm_lt(keys, scores_grad), mm(scores_grad, queries), mm(probs.astype(BF16), above))
            )
        dqkv_ref[0, :, spans[0]] = both_heads(grads[0][0], grads[1][0]).astype(BF16)
        for span, low, high in zip(spans[1:], grads[0][1:], grads[1][1:]):
            dqkv_ref[0, :, span] = jnp.where(first, low, high).astype(BF16)
    grad = dqkv_ref[0]
    total = mm_rt(grad[:, :width], wq[...].reshape(model, width))
    total = total + mm_rt(grad[:, width : 2 * width], wk[...].reshape(model, width))
    total = total + mm_rt(grad[:, 2 * width :], wv[...].reshape(model, width))
    pieces = [total[k * local : (k + 1) * local] for k in range(ZS)]
    for k in range(ZS):
        outs[k][...] = chosen(pieces, z ^ k).astype(BF16)
    unit, _ = normalize(rows_ref[:, 0].reshape(slots, model).astype(F32))

    @pl.when(pl.program_id(0) == 0)
    def _():
        sums_ref[...] = jnp.zeros_like(sums_ref)

    sums_ref[0:1, :] += jnp.sum(total * unit, axis=0, keepdims=True)
    sums_ref[1:2, :] += jnp.sum(total, axis=0, keepdims=True)
    sums_ref[2:3, : 3 * width] += jnp.sum(grad.astype(F32), axis=0, keepdims=True)


def attend_back(meta, rows, upstream, qkv, weights):
    _, count, local, model = rows.shape
    slots, width = ZS * local, model // ZS
    packed = pl.BlockSpec((1, slots, 3 * width), lambda s, m: (s, 0, 0))
    split = pl.BlockSpec((local, model), lambda s, m: (s, 0))
    flops = count * (2 * slots * model * 3 * width + 20 * slots * slots * width)
    return pl.pallas_call(
        attend_back_kernel,
        name="attend_back",
        grid_spec=pltpu.PrefetchScalarGridSpec(
            num_scalar_prefetch=1,
            grid=(count,),
            in_specs=[pl.BlockSpec((ZS, 1, local, model), lambda s, m: (0, s, 0, 0))]
            + [pl.BlockSpec((local, width), lambda s, m: (s, 0))] * ZS
            + [packed]
            + weight_specs(weights, model // weights.shape[0], width),
            out_specs=[packed, block(8, model)] + [split] * ZS,
        ),
        out_shape=[shape_of((count, slots, 3 * width), BF16)]
        + [shape_of((8, model), F32)]
        + [shape_of((count * local, model), BF16)] * ZS,
        compiler_params=params(),
        cost_estimate=cost(flops, 2 * count * slots * (2 * model + 7 * width) + 6 * model * width),
    )(meta, rows, *upstream, qkv, weights, weights, weights)


def project_kernel(meta, c0, c1, c2, c3, x, weights, vecs, hidden_ref, normed_ref):
    width = c0.shape[1]
    z = meta[meta.shape[0] - 1]
    hidden = x[...].astype(F32) + vecs[2:3]
    for k, part in enumerate((c0, c1, c2, c3)):
        start = pl.multiple_of((z ^ k) * width, width)
        hidden = hidden + mm(part[...], weights[pl.ds(start, width), :])
    hidden_ref[...] = hidden
    unit, _ = normalize(hidden)
    normed_ref[...] = (unit * vecs[3:4] + vecs[4:5]).astype(BF16)


def project(meta, parts, x, weights, vecs):
    rows, model = x.shape
    return pl.pallas_call(
        project_kernel,
        name="project",
        grid_spec=pltpu.PrefetchScalarGridSpec(
            num_scalar_prefetch=1,
            grid=(1,),
            in_specs=[block(*part.shape) for part in parts]
            + [block(rows, model), block(model, model), block(*vecs.shape)],
            out_specs=[block(rows, model)] * 2,
        ),
        out_shape=[shape_of((rows, model), F32), shape_of((rows, model), BF16)],
        compiler_params=params(),
        cost_estimate=cost(2 * rows * model * model, rows * model * 10 + 2 * model * model),
    )(meta, *parts, x, weights, vecs)


def feed_kernel(normed, above, up, bias, act_ref, grad_ref, back_ref):
    count, rows, model = normed.shape
    width = up.shape[1]
    value = mm(normed[...].reshape(count * rows, model), up[...]) + bias[...]
    square = value * value
    root = math.sqrt(2.0 / math.pi)
    bend = jnp.tanh(root * value * (1.0 + 0.044715 * square))
    half = 0.5 * (1.0 + bend)
    act_ref[...] = (value * half).astype(BF16).reshape(count, rows, width)
    slope = half + 0.5 * value * (1.0 - bend * bend) * (root + 3 * 0.044715 * root * square)
    grad = (above[...].reshape(count * rows, width) * slope).astype(BF16)
    grad_ref[...] = grad.reshape(count, rows, width)
    back_ref[...] = mm_rt(grad, up[...]).astype(BF16).reshape(count, rows, model)


def feed(normed, above, up, bias):
    count, rows, model = normed.shape
    width = up.shape[1]
    wide = pl.BlockSpec((2, rows, model), lambda i: (i, 0, 0))
    thin = pl.BlockSpec((2, rows, width), lambda i: (i, 0, 0))
    return pl.pallas_call(
        feed_kernel,
        name="feed",
        grid=(count // 2,),
        in_specs=[wide, thin, block(model, width), block(1, width)],
        out_specs=[thin, thin, wide],
        out_shape=[shape_of((count, rows, width), BF16)] * 2 + [shape_of((count, rows, model), BF16)],
        compiler_params=params(),
        cost_estimate=cost(
            count * rows * 4 * model * width,
            count * rows * (4 * model + 8 * width) + 2 * model * width,
            count * rows * width,
        ),
    )(normed, above, up, bias)


def both(even, odd):
    return jnp.concatenate([even[0], odd[0]], axis=0)


def down_grad_kernel(act_e, act_o, grad_e, grad_o, cot_e, cot_o, down_ref, down_sum, bias_sum):
    width = act_e.shape[2]

    @pl.when(pl.program_id(0) == 0)
    def _():
        down_sum[...] = jnp.zeros_like(down_sum)
        bias_sum[...] = jnp.zeros_like(bias_sum)

    down_sum[...] += mm_lt(both(act_e, act_o), both(cot_e, cot_o))
    bias_sum[0:1, :width] += jnp.sum(both(grad_e, grad_o).astype(F32), axis=0, keepdims=True)

    @pl.when(pl.program_id(0) == pl.num_programs(0) - 1)
    def _():
        down_ref[:width] = down_sum[...].astype(BF16)
        down_ref[width:] = bias_sum[...].astype(BF16)


def down_gradient(act, grad, cot):
    _, rows, width = act[0].shape
    model = cot[0].shape[2]
    thin = pl.BlockSpec((1, rows, width), lambda i: (i, 0, 0))
    wide = pl.BlockSpec((1, rows, model), lambda i: (i, 0, 0))
    return pl.pallas_call(
        down_grad_kernel,
        name="down_gradient",
        grid=(4,),
        in_specs=[thin] * 4 + [wide] * 2,
        out_specs=block(width + 16, model),
        scratch_shapes=[pltpu.VMEM((width, model), F32), pltpu.VMEM((16, model), F32)],
        out_shape=shape_of((width + 16, model), BF16),
        compiler_params=params(),
        cost_estimate=cost(16 * rows * model * width, 16 * rows * (model + 2 * width)),
    )(*act, *grad, *cot)


def feed_grads_kernel(act_e, act_o, grad_e, grad_o, normed_e, normed_o, down, out_e, out_o, up_ref, up_sum):
    rows = act_e.shape[1]
    out = mm(both(act_e, act_o), down[...]).astype(BF16)
    out_e[0] = out[:rows]
    out_o[0] = out[rows:]

    @pl.when(pl.program_id(0) == 0)
    def _():
        up_sum[...] = jnp.zeros_like(up_sum)

    up_sum[...] += mm_lt(both(normed_e, normed_o), both(grad_e, grad_o))

    @pl.when(pl.program_id(0) == pl.num_programs(0) - 1)
    def _():
        up_ref[...] = up_sum[...].astype(BF16)


def feed_grads(act, grad, normed, down):
    _, rows, width = act[0].shape
    model = down.shape[1]
    thin = pl.BlockSpec((1, rows, width), lambda i: (i, 0, 0))
    wide = pl.BlockSpec((1, rows, model), lambda i: (i, 0, 0))
    return pl.pallas_call(
        feed_grads_kernel,
        name="feed_grads",
        grid=(4,),
        in_specs=[thin] * 4 + [wide] * 2 + [block(width, model)],
        out_specs=[wide, wide, block(model, width)],
        scratch_shapes=[pltpu.VMEM((model, width), F32)],
        out_shape=[shape_of((4, rows, model), BF16)] * 2 + [shape_of((model, width), BF16)],
        compiler_params=params(),
        cost_estimate=cost(32 * rows * model * width, 16 * rows * (2 * model + 2 * width)),
    )(*act, *grad, *normed, down)


def middle_kernel(meta, g0, g1, gx, gy, gd, hidden, cot, weights, vecs, hidden_grad_ref, grad_ref, sums_ref, d0, d1, d2, d3):
    width = d0.shape[1]
    z = meta[meta.shape[0] - 1]
    normed_grad = (g0[0].astype(F32) + g1[0].astype(F32)) + (gx[...].astype(F32) + gy[...].astype(F32))
    normed_grad = normed_grad + gd[...].astype(F32)
    unit, inverse = normalize(hidden[...])
    upstream = cot[...].astype(F32)
    hidden_grad = upstream + norm_back(normed_grad, unit, inverse, vecs[3:4])
    hidden_grad_ref[...] = hidden_grad
    grad = hidden_grad.astype(BF16)
    grad_ref[...] = grad
    for k, out in enumerate((d0, d1, d2, d3)):
        start = pl.multiple_of((z ^ k) * width, width)
        out[...] = mm_rt(grad, weights[pl.ds(start, width), :]).astype(BF16)
    sums_ref[0:1, :] = jnp.sum(normed_grad * unit, axis=0, keepdims=True)
    sums_ref[1:2, :] = jnp.sum(normed_grad, axis=0, keepdims=True)
    sums_ref[2:3, :] = jnp.sum(grad.astype(F32), axis=0, keepdims=True)
    sums_ref[3:4, :] = jnp.sum(upstream, axis=0, keepdims=True)


def middle(meta, stacks, moved, hidden, cot, weights, vecs):
    rows, model = hidden.shape
    width = model // ZS
    return pl.pallas_call(
        middle_kernel,
        name="middle",
        grid_spec=pltpu.PrefetchScalarGridSpec(
            num_scalar_prefetch=1,
            grid=(1,),
            in_specs=[block(1, rows, model)] * 2
            + [block(rows, model)] * 5
            + [block(model, model), block(*vecs.shape)],
            out_specs=[block(rows, model)] * 2 + [block(4, model)] + [block(rows, width)] * ZS,
        ),
        out_shape=[shape_of((rows, model), F32), shape_of((rows, model), BF16), shape_of((4, model), F32)]
        + [shape_of((rows, width), BF16)] * ZS,
        compiler_params=params(),
        cost_estimate=cost(2 * rows * model * model, rows * model * 26 + 2 * model * model),
    )(meta, *stacks, *moved, hidden, cot, weights, vecs)


def finish_kernel(x, mine, near, far, hidden_grad, vecs, out):
    unit, inverse = normalize(x[...].astype(F32))
    upstream = mine[...].astype(F32) + near[...].astype(F32) + far[...].astype(F32)
    out[...] = (hidden_grad[...] + norm_back(upstream, unit, inverse, vecs[0:1])).astype(BF16)


def finish(x, mine, near, far, hidden_grad, vecs):
    rows, model = x.shape
    steps = 3 if rows % 48 == 0 else 1
    part = pl.BlockSpec((rows // steps, model), lambda i: (i, 0))
    return pl.pallas_call(
        finish_kernel,
        name="finish",
        grid=(steps,),
        in_specs=[part] * 5 + [block(*vecs.shape)],
        out_specs=part,
        out_shape=shape_of((rows, model), BF16),
        compiler_params=params(),
        cost_estimate=cost(20 * rows * model, rows * model * 12),
    )(x, mine, near, far, hidden_grad, vecs)


def per_device(
    inputs,
    lengths,
    cotangent,
    attn_gain,
    attn_shift,
    qkv_weight,
    qv_bias,
    proj_weight,
    proj_bias,
    mlp_gain,
    mlp_shift,
    up_weight,
    up_bias,
    down_weight,
    down_bias,
):
    count, local, model = inputs.shape
    size = lax.axis_size("fsdp")
    outer = size // TEAM
    place = lax.axis_index("fsdp").astype(jnp.uint32)
    seat = lax.axis_index("seq").astype(jnp.uint32)
    z = seat.astype(jnp.int32)
    team = place & (TEAM - 1)
    core = team & 1
    chip = team >> 1
    tokens = count * local
    width = model // ZS
    own_rows = qkv_weight.shape[0]
    hidden_units = up_weight.shape[1]
    feed_width = hidden_units // TEAM
    meta = jnp.concatenate([lengths.astype(jnp.int32), z.reshape(1)])

    rows = lax.all_gather(inputs, "seq", axis=0, tiled=False)

    def over_team(own):
        quad = jnp.stack([own] + [swap(own, 2 * m) for m in (1, 2, 3)])
        return jnp.concatenate([quad, swap(quad, 1)], axis=0)

    columns = [
        lax.dynamic_slice(qkv_weight, (jnp.uint32(0), seat * width + i * model), (own_rows, width)) for i in range(3)
    ]
    vectors = (attn_gain, attn_shift, proj_bias, mlp_gain, mlp_shift, down_bias)
    lanes, spot, packed = 3 * width, 0, []
    for vector in vectors:
        packed.append(jnp.pad(vector, (spot, lanes - spot - vector.shape[0])))
        spot += vector.shape[0]
    row_one = functools.reduce(jnp.add, packed).reshape(1, lanes)
    row_two = jnp.pad(qv_bias, (0, lanes - qv_bias.shape[0])).reshape(1, lanes)
    small_rows = jnp.pad(row_one, ((0, 7), (0, 0))) + jnp.pad(row_two, ((1, 6), (0, 0)))
    piece = jnp.concatenate([jnp.concatenate(columns, axis=1), small_rows], axis=0)
    pieces = over_team(piece)
    weights = jnp.stack([pick(pieces, ((j ^ team) & 1) * 4 + ((j ^ team) >> 1)) for j in range(TEAM)])
    weights = gather_over_outer(weights, size)
    vecs = weights[:, own_rows, : 6 * own_rows].reshape(size, 6, own_rows).transpose(1, 0, 2)
    vecs = vecs.reshape(6, model).astype(F32)
    bias_qv = weights[:, own_rows + 1, : qv_bias.shape[0]].reshape(1, 2 * model).astype(F32)
    bias_quarter = jnp.concatenate(
        [
            lax.dynamic_slice(bias_qv, (jnp.uint32(0), seat * width), (1, width)),
            jnp.zeros((1, width), F32),
            lax.dynamic_slice(bias_qv, (jnp.uint32(0), model + seat * width), (1, width)),
        ],
        axis=1,
    )
    proj = lax.all_gather(proj_weight, "fsdp", axis=0, tiled=True)

    up_blocks = up_weight.reshape(own_rows, outer, TEAM, feed_width // outer).transpose(2, 0, 1, 3)
    up_blocks = up_blocks.reshape(TEAM, own_rows, feed_width)
    groups = [[o * TEAM + t for t in range(TEAM)] for o in range(outer)]
    up = lax.all_to_all(
        up_blocks, "fsdp", split_axis=0, concat_axis=0, axis_index_groups=groups, tiled=True
    ).reshape(TEAM * own_rows, feed_width)
    up = gather_over_outer(up, size)
    down = gather_over_outer(down_weight, size)
    bias_up = gather_over_outer(up_bias, size).astype(F32).reshape(1, feed_width)

    half = model // 2

    def over_chips(own):
        by_x, by_y = swap(own, 2), swap(own, 4)
        diagonal = jnp.concatenate([swap(by_x[:, :half], 4), swap(by_y[:, half:], 2)], axis=1)
        return jnp.stack([own, by_x, by_y, diagonal])

    positions = z * local + jnp.arange(local, dtype=jnp.int32)
    row_valid = (positions[None, :] < lengths[:, None])[:, :, None]
    cot = jnp.where(row_valid, cotangent, jnp.zeros_like(cotangent)).reshape(tokens, model)
    cot_even = over_chips(cot)
    cot_odd = swap(cot_even, 1)

    def down_back(stack):
        out = lax.dot_general(stack, down, (((2,), (1,)), ((), ())), preferred_element_type=F32)
        return out


    qkv, normed_attn, *context = attend(meta, after(rows, cot_odd, up), weights, vecs, bias_quarter)
    context = [context[0]] + [cross(context[k], k) for k in range(1, ZS)]
    above_even, above_odd = (down_back(after(part, qkv)) for part in (cot_even, cot_odd))
    own = inputs.reshape(tokens, model)
    context[0] = after(context[0], above_even, above_odd)
    hidden, normed = project(meta, context, own, proj, vecs)

    normed_even = over_chips(normed)
    normed_odd = swap(normed_even, 1)
    act_even, grad_even, back_even = feed(normed_even, above_even, up, bias_up)
    act_odd, grad_odd, back_odd = feed(normed_odd, above_odd, up, bias_up)
    back_core = swap(back_odd, 1)
    sums = [joined(back_even[m], back_core[m]) for m in (1, 2, 3)]
    moved = [swap(part, 2 * m) for m, part in zip((1, 2, 3), sums)]
    act_even = after(act_even, *sums)
    down_part = down_gradient((act_even, act_odd), (grad_even, grad_odd), (cot_even, cot_odd))
    out_even, out_odd, up_part = feed_grads(
        (act_even, after(act_odd, down_part)), (grad_even, grad_odd), (normed_even, normed_odd), down
    )
    if outer > 1:
        bias_part = rows_over_outer(down_part[feed_width, :feed_width].astype(F32), size)
        bias_part = jnp.pad(bias_part.reshape(1, -1), ((0, 15), (0, model - bias_part.shape[0])))
        down_part = rows_over_outer(down_part[:feed_width], size)
        down_part = jnp.concatenate([down_part, bias_part.astype(BF16)], axis=0)
    down_rows = down_weight.shape[0]
    up_part = rows_over_outer(up_part, size)
    down_total = lax.psum(down_part, "seq")
    side = seat & 1
    half_width = feed_width // 2
    up_keep, up_give = (
        lax.dynamic_slice(up_part, (jnp.uint32(0), part * half_width), (up_part.shape[0], half_width))
        for part in (side, 1 - side)
    )

    hidden_grad, attn_grad, mid_sums, *context_grad = middle(
        meta, (back_even, back_core), moved, after(hidden, out_even), cot, proj, vecs
    )

    def over_core(part, *others):
        keep, give = pick(part, core, 1), pick(part, 1 - core, 1)
        return joined(after(keep, *others), swap(give, 1))

    def over_team_chips(both, at, *others):
        total = after(pick(both, at(0)), *others).astype(F32)
        for m in (1, 2, 3):
            total = total + swap(pick(both, at(m)), 2 * m).astype(F32)
        return total.astype(BF16)

    proj_part = mm_lt(jnp.concatenate(context, axis=1), attn_grad)
    if outer == 1:
        proj_part = proj_part.astype(BF16).reshape(ZS, 2, own_rows, model)
        mid_rows = mid_sums.reshape(4, TEAM, own_rows).transpose(1, 0, 2).reshape(4, 2, 1, 4 * own_rows)
        mid_rows = jnp.pad(mid_rows, ((0, 0), (0, 0), (0, 7), (0, model - 4 * own_rows))).astype(BF16)
        mid_rows = jnp.stack([pick(mid_rows, seat ^ k) for k in range(ZS)])
        proj_part = jnp.concatenate([proj_part, mid_rows], axis=2)
        chip_at = lambda m: chip ^ m ^ seat
    else:
        proj_part = proj_part.reshape(ZS, width, model)
        proj_part = jnp.stack([pick(proj_part, seat ^ j) for j in range(ZS)]).reshape(model, model)
        proj_part = rows_over_outer(proj_part, size).astype(BF16).reshape(4, 2, own_rows, model)
        chip_at = lambda m: chip ^ m

    context_grad = [context_grad[0]] + [cross(context_grad[k], k) for k in range(1, ZS)]
    up_half = joined(after(up_keep, *context_grad), cross(up_give, 1))
    up_across = cross(up_half, 2)
    qkv_grad, attn_sums, *parts = attend_back(meta, rows, context_grad, after(qkv, up_half), weights)

    qkv_part = mm_lt(normed_attn.reshape(-1, model), qkv_grad.reshape(-1, 3 * width)).astype(BF16)

    if outer == 1:
        qkv_part = qkv_part.reshape(4, 2, own_rows, 3 * width)
        gains = attn_sums[:2].reshape(2, TEAM, own_rows).transpose(1, 0, 2).reshape(4, 2, 1, 2 * own_rows)
        biases = jnp.concatenate([attn_sums[2, :width], attn_sums[2, 2 * width : 3 * width]])
        biases = jnp.broadcast_to(biases, (4, 2, 1, 2 * width))
        packed = jnp.concatenate([gains, biases], axis=3)
        packed = jnp.pad(packed, ((0, 0), (0, 0), (0, 7), (0, 3 * width - packed.shape[3]))).astype(BF16)
        qkv_part = jnp.concatenate([qkv_part, packed], axis=2)
    else:
        qkv_part = rows_over_outer(qkv_part, size).reshape(4, 2, own_rows, 3 * width)

    near = [cross(parts[k], 1) for k in (1, 3)]
    qkv_both = over_core(qkv_part)
    down_grad = down_total[:down_rows].astype(F32)
    proj_both = over_core(proj_part, qkv_both, down_grad)
    middle_sum = joined(after(parts[2], proj_both), near[1])
    far = cross(middle_sum, 2)
    up_sum = lax.optimization_barrier(joined(after(up_half, middle_sum), up_across))
    up_sum = up_sum.reshape(4, 2, own_rows, half_width)
    pair = jnp.stack([pick(up_sum, core, 1), swap(pick(up_sum, 1 - core, 1), 1)], axis=1)
    up_moved = [swap(pick(pair, chip ^ m), 2 * m) for m in (1, 2, 3)]
    out_core = swap(after(out_odd, qkv_grad), 1)
    out_sums = [joined(after(out_even[m], up_sum), out_core[m]) for m in (1, 2, 3)]
    out_moved = [swap(part, 2 * m) for m, part in zip((1, 2, 3), out_sums)]
    input_grad = finish(own, parts[0], near[0], far, after(hidden_grad, pair, down_grad, *out_sums), vecs)
    qkv_mine = lax.optimization_barrier(over_team_chips(qkv_both, lambda m: chip ^ m, up_sum))
    proj_mine = over_team_chips(proj_both, chip_at, up_sum)
    lanes = qkv_mine.shape[1]
    packed = jnp.concatenate([after(qkv_mine, far), proj_mine], axis=1)
    packed_two = cross(packed, 2)
    up_rel = jnp.stack([after(pick(pair, chip), packed)] + up_moved)
    up_rel = lax.optimization_barrier(up_rel.reshape(TEAM, own_rows, half_width))
    up_other = cross(up_rel, 1)
    packed_two = after(packed_two, up_rel)
    qkv_two = packed_two[:, :lanes]
    proj_two = lax.optimization_barrier(joined(proj_mine, packed_two[:, lanes:]))
    packed_one = cross(jnp.concatenate([qkv_mine, qkv_two, proj_two], axis=1), 1)
    qkv_near = [packed_one[:, :lanes], packed_one[:, lanes : 2 * lanes]]
    proj_total = joined(proj_two, packed_one[:, 2 * lanes :]).astype(F32)
    input_grad = input_grad.reshape(inputs.shape)

    output = after(hidden, qkv_two) + vecs[5:6] + out_even[0].astype(F32) + out_core[0].astype(F32)
    for part in out_moved:
        output = output + part.astype(F32)
    output = jnp.where(row_valid, output.reshape(inputs.shape), 0.0).astype(BF16)

    up_bias_grad = down_total[down_rows, : up_bias.shape[0]].astype(F32)
    up_first = jnp.where(side == 0, up_rel, up_other)
    up_second = jnp.where(side == 0, up_other, up_rel)
    up_rel = jnp.concatenate([up_first, up_second], axis=2)
    up_grad = jnp.stack([pick(up_rel, j ^ team) for j in range(TEAM)], axis=1).astype(F32)
    up_grad = up_grad.reshape(own_rows, TEAM, outer, feed_width // outer).transpose(0, 2, 1, 3)
    up_grad = up_grad.reshape(own_rows, hidden_units)
    proj_grad = proj_total[:own_rows]
    qkv_parts = jnp.stack([qkv_mine, qkv_near[0], qkv_two, qkv_near[1]])
    ordered = [pick(qkv_parts, seat ^ j).astype(F32) for j in range(ZS)]
    qkv_weight_grad = jnp.concatenate(
        [part[:own_rows, i * width : (i + 1) * width] for i in range(3) for part in ordered], axis=1
    )

    if outer == 1:
        mid = proj_total[own_rows, : 4 * own_rows].reshape(4, own_rows)
        packed = jnp.stack([part[own_rows] for part in ordered])
        gains = packed[:, : 2 * own_rows]
        gains = (gains[0] + gains[1]) + (gains[2] + gains[3])
        attn_gain_grad, attn_shift_grad = gains[:own_rows], gains[own_rows:]
        mine = pick(packed, place & (ZS - 1))
        start = 2 * own_rows + (place >> 2) * width
        qv_bias_grad = lax.dynamic_slice(mine, (start,), (width,))
        mlp_gain_grad, mlp_shift_grad, proj_bias_grad, down_bias_grad = mid
    else:
        biases = jnp.zeros((2, ZS, width), F32)
        biases = lax.dynamic_update_slice(
            biases, jnp.stack([attn_sums[2, :width], attn_sums[2, 2 * width : 3 * width]])[:, None], (0, z, 0)
        )
        packed = jnp.concatenate([attn_sums[0], attn_sums[1], mid_sums.reshape(-1)]).reshape(6, size, own_rows)
        packed = jnp.concatenate([packed.transpose(1, 0, 2).reshape(size, -1), biases.reshape(size, -1)], axis=1)
        packed = lax.psum_scatter(packed, "fsdp", scatter_dimension=0, tiled=False)
        packed = lax.psum(packed, "seq")
        vectors = packed[: 6 * own_rows].reshape(6, own_rows)
        attn_gain_grad, attn_shift_grad, mlp_gain_grad, mlp_shift_grad, proj_bias_grad, down_bias_grad = vectors
        qv_bias_grad = packed[6 * own_rows :]

    return (
        output,
        input_grad,
        attn_gain_grad,
        attn_shift_grad,
        qkv_weight_grad,
        qv_bias_grad,
        proj_grad,
        proj_bias_grad,
        mlp_gain_grad,
        mlp_shift_grad,
        up_grad,
        up_bias_grad,
        down_grad,
        down_bias_grad,
    )


def solution(mesh):
    split = P("fsdp")
    tokens = P("fsdp", "seq", None)
    matrix = P("fsdp", None)
    in_specs = (tokens, split, tokens, split, split, matrix, split, matrix) + (split,) * 3 + (matrix, split, matrix, split)
    out_specs = (tokens, tokens, split, split, matrix, split, matrix) + (split,) * 3 + (matrix, split, matrix, split)
    return jax.shard_map(per_device, mesh=mesh, in_specs=in_specs, out_specs=out_specs, check_vma=False)
```

```python
import functools
import math

import jax
import jax.numpy as jnp
from jax import lax
from jax.experimental import pallas as pl
from jax.experimental.pallas import tpu as pltpu
from jax.sharding import PartitionSpec as P

HEAD = 64
EPSILON = 1e-06
MASKED = -1e30
TEAM = 8
ZS = 4
F32 = jnp.float32
BF16 = jnp.bfloat16
VMEM_BYTES = 56 * 1024 * 1024
SCALE = 1024


def params():
    return pltpu.CompilerParams(vmem_limit_bytes=VMEM_BYTES)


def cost(flops, nbytes, trans=0):
    return pl.CostEstimate(flops=int(flops) // SCALE, bytes_accessed=int(nbytes) // SCALE, transcendentals=int(trans) // SCALE)


def shape_of(dims, dtype):
    return jax.ShapeDtypeStruct(dims, dtype)


def mm(left, right):
    return lax.dot_general(left, right, (((1,), (0,)), ((), ())), preferred_element_type=F32)


def mm_rt(left, right):
    return lax.dot_general(left, right, (((1,), (1,)), ((), ())), preferred_element_type=F32)


def mm_lt(left, right):
    return lax.dot_general(left, right, (((0,), (0,)), ((), ())), preferred_element_type=F32)


def normalize(rows):
    center = rows - jnp.mean(rows, axis=-1, keepdims=True)
    inverse = lax.rsqrt(jnp.mean(center * center, axis=-1, keepdims=True) + EPSILON)
    return center * inverse, inverse


def norm_back(upstream, unit, inverse, gain):
    scaled = upstream * gain
    return inverse * (
        scaled
        - jnp.mean(scaled, axis=-1, keepdims=True)
        - unit * jnp.mean(scaled * unit, axis=-1, keepdims=True)
    )


def swap(value, mask):
    size = lax.axis_size("fsdp")
    return lax.ppermute(value, "fsdp", [(i, i ^ mask) for i in range(size)])


def cross(value, mask):
    return lax.ppermute(value, "seq", [(i, i ^ mask) for i in range(ZS)])


def joined(first, second):
    return (first.astype(F32) + second.astype(F32)).astype(BF16)


def after(value, *others):
    return lax.optimization_barrier((value,) + others)[0]


def pick(stack, index, axis=0):
    starts = [jnp.uint32(0)] * stack.ndim
    starts[axis] = index.astype(jnp.uint32)
    sizes = list(stack.shape)
    sizes[axis] = 1
    return lax.dynamic_slice(stack, starts, sizes).reshape(stack.shape[:axis] + stack.shape[axis + 1 :])


def outer_groups(size):
    outer = size // TEAM
    return [[o * TEAM + t for o in range(outer)] for t in range(TEAM)]


def rows_over_outer(value, size):
    if size == TEAM:
        return value
    return lax.psum_scatter(
        value, "fsdp", scatter_dimension=0, axis_index_groups=outer_groups(size), tiled=True
    )


def gather_over_outer(value, size):
    if size == TEAM:
        return value
    return lax.all_gather(value, "fsdp", axis=0, axis_index_groups=outer_groups(size), tiled=True)


def block(*dims):
    return pl.BlockSpec(dims, lambda *i: (0,) * len(dims))


def chosen(values, index):
    out = values[-1]
    for i in range(len(values) - 1):
        out = jnp.where(index == i, values[i], out)
    return out


def head_probs(queries, keys, valid):
    scores = mm_rt(keys, queries) * HEAD ** (-0.5)
    scores = jnp.where(valid, scores, MASKED)
    exponent = jnp.exp(scores - jnp.max(scores, axis=0, keepdims=True))
    return exponent * (1.0 / jnp.sum(exponent, axis=0, keepdims=True))


def both_heads(low, high):
    return jnp.concatenate([low[:HEAD], high[HEAD:]], axis=0).T


def attend_kernel(meta, rows_ref, wq, wk, wv, vecs, bias, qkv_ref, normed_ref, c0, c1, c2, c3):
    local = rows_ref.shape[2]
    slots = ZS * local
    model = rows_ref.shape[3]
    width = wq.shape[2]
    length = meta[pl.program_id(0)]
    z = meta[meta.shape[0] - 1]
    unit, _ = normalize(rows_ref[:, 0].reshape(slots, model).astype(F32))
    normed = (unit * vecs[0:1] + vecs[1:2]).astype(BF16)
    normed_ref[0] = normed
    parts = []
    for i, w in enumerate((wq, wk, wv)):
        part = (mm(normed, w[...].reshape(model, width)) + bias[:, i * width : (i + 1) * width]).astype(BF16)
        qkv_ref[0, :, i * width : (i + 1) * width] = part
        parts.append(part)
    valid = lax.broadcasted_iota(jnp.int32, (slots, slots), 0) < length
    first = lax.broadcasted_iota(jnp.int32, (1, 2 * HEAD), 1) < HEAD
    for pair in range(width // (2 * HEAD)):
        lanes = slice(pair * 2 * HEAD, (pair + 1) * 2 * HEAD)
        queries, keys, values = (part[:, lanes] for part in parts)
        outs = []
        for mine in (first, ~first):
            probs = head_probs(queries, jnp.where(mine, keys, jnp.zeros_like(keys)), valid)
            outs.append(mm_lt(values, probs.astype(BF16)))
        context = both_heads(*outs)
        pieces = [context[k * local : (k + 1) * local] for k in range(ZS)]
        for k, out in enumerate((c0, c1, c2, c3)):
            out[:, lanes] = chosen(pieces, z ^ k).astype(BF16)


def weight_specs(weights, own_rows, width):
    return [
        pl.BlockSpec((weights.shape[0], own_rows, width), functools.partial(lambda i, s, m: (0, 0, i), i))
        for i in range(3)
    ]


def attend(meta, rows, weights, vecs, bias):
    _, count, local, model = rows.shape
    slots, width = ZS * local, model // ZS
    flops = count * (2 * slots * model * 3 * width + 8 * slots * slots * width)
    per_sequence = lambda *dims: pl.BlockSpec((1,) + dims, lambda s, m: (s, 0, 0))
    return pl.pallas_call(
        attend_kernel,
        name="attend",
        grid_spec=pltpu.PrefetchScalarGridSpec(
            num_scalar_prefetch=1,
            grid=(count,),
            in_specs=[pl.BlockSpec((ZS, 1, local, model), lambda s, m: (0, s, 0, 0))]
            + weight_specs(weights, model // weights.shape[0], width)
            + [block(*vecs.shape), block(1, 3 * width)],
            out_specs=[per_sequence(slots, 3 * width), per_sequence(slots, model)]
            + [pl.BlockSpec((local, width), lambda s, m: (s, 0))] * ZS,
        ),
        out_shape=[shape_of((count, slots, 3 * width), BF16), shape_of((count, slots, model), BF16)]
        + [shape_of((count * local, width), BF16)] * ZS,
        compiler_params=params(),
        cost_estimate=cost(flops, 2 * count * slots * (2 * model + 4 * width) + 6 * model * width),
    )(meta, rows, weights, weights, weights, vecs, bias)


def attend_back_kernel(meta, rows_ref, d0, d1, d2, d3, qkv_ref, wq, wk, wv, *refs):
    dqkv_ref, sums_ref, *outs = refs
    local = rows_ref.shape[2]
    slots = ZS * local
    model = rows_ref.shape[3]
    width = wq.shape[2]
    length = meta[pl.program_id(0)]
    z = meta[meta.shape[0] - 1]
    given = [d[...] for d in (d0, d1, d2, d3)]
    upstream = jnp.concatenate([chosen(given, z ^ k) for k in range(ZS)], axis=0)
    valid = lax.broadcasted_iota(jnp.int32, (slots, slots), 0) < length
    first = lax.broadcasted_iota(jnp.int32, (1, 2 * HEAD), 1) < HEAD
    for pair in range(width // (2 * HEAD)):
        spans = [slice(i * width + pair * 2 * HEAD, i * width + (pair + 1) * 2 * HEAD) for i in range(3)]
        queries, keys, values = (qkv_ref[0, :, span] for span in spans)
        above = upstream[:, spans[0]]
        grads = []
        for mine in (first, ~first):
            probs = head_probs(queries, jnp.where(mine, keys, jnp.zeros_like(keys)), valid)
            probs_grad = mm_rt(jnp.where(mine, values, jnp.zeros_like(values)), above)
            inner = jnp.sum(probs * probs_grad, axis=0, keepdims=True)
            scores_grad = (probs * (probs_grad - inner) * HEAD ** (-0.5)).astype(BF16)
            grads.append(
                (mm_lt(keys, scores_grad), mm(scores_grad, queries), mm(probs.astype(BF16), above))
            )
        dqkv_ref[0, :, spans[0]] = both_heads(grads[0][0], grads[1][0]).astype(BF16)
        for span, low, high in zip(spans[1:], grads[0][1:], grads[1][1:]):
            dqkv_ref[0, :, span] = jnp.where(first, low, high).astype(BF16)
    grad = dqkv_ref[0]
    total = mm_rt(grad[:, :width], wq[...].reshape(model, width))
    total = total + mm_rt(grad[:, width : 2 * width], wk[...].reshape(model, width))
    total = total + mm_rt(grad[:, 2 * width :], wv[...].reshape(model, width))
    pieces = [total[k * local : (k + 1) * local] for k in range(ZS)]
    for k in range(ZS):
        outs[k][...] = chosen(pieces, z ^ k).astype(BF16)
    unit, _ = normalize(rows_ref[:, 0].reshape(slots, model).astype(F32))

    @pl.when(pl.program_id(0) == 0)
    def _():
        sums_ref[...] = jnp.zeros_like(sums_ref)

    sums_ref[0:1, :] += jnp.sum(total * unit, axis=0, keepdims=True)
    sums_ref[1:2, :] += jnp.sum(total, axis=0, keepdims=True)
    sums_ref[2:3, : 3 * width] += jnp.sum(grad.astype(F32), axis=0, keepdims=True)


def attend_back(meta, rows, upstream, qkv, weights):
    _, count, local, model = rows.shape
    slots, width = ZS * local, model // ZS
    packed = pl.BlockSpec((1, slots, 3 * width), lambda s, m: (s, 0, 0))
    split = pl.BlockSpec((local, model), lambda s, m: (s, 0))
    flops = count * (2 * slots * model * 3 * width + 20 * slots * slots * width)
    return pl.pallas_call(
        attend_back_kernel,
        name="attend_back",
        grid_spec=pltpu.PrefetchScalarGridSpec(
            num_scalar_prefetch=1,
            grid=(count,),
            in_specs=[pl.BlockSpec((ZS, 1, local, model), lambda s, m: (0, s, 0, 0))]
            + [pl.BlockSpec((local, width), lambda s, m: (s, 0))] * ZS
            + [packed]
            + weight_specs(weights, model // weights.shape[0], width),
            out_specs=[packed, block(8, model)] + [split] * ZS,
        ),
        out_shape=[shape_of((count, slots, 3 * width), BF16)]
        + [shape_of((8, model), F32)]
        + [shape_of((count * local, model), BF16)] * ZS,
        compiler_params=params(),
        cost_estimate=cost(flops, 2 * count * slots * (2 * model + 7 * width) + 6 * model * width),
    )(meta, rows, *upstream, qkv, weights, weights, weights)


def project_kernel(meta, c0, c1, c2, c3, x, weights, vecs, hidden_ref, normed_ref):
    width = c0.shape[1]
    z = meta[meta.shape[0] - 1]
    hidden = x[...].astype(F32) + vecs[2:3]
    for k, part in enumerate((c0, c1, c2, c3)):
        start = pl.multiple_of((z ^ k) * width, width)
        hidden = hidden + mm(part[...], weights[pl.ds(start, width), :])
    hidden_ref[...] = hidden
    unit, _ = normalize(hidden)
    normed_ref[...] = (unit * vecs[3:4] + vecs[4:5]).astype(BF16)


def project(meta, parts, x, weights, vecs):
    rows, model = x.shape
    return pl.pallas_call(
        project_kernel,
        name="project",
        grid_spec=pltpu.PrefetchScalarGridSpec(
            num_scalar_prefetch=1,
            grid=(1,),
            in_specs=[block(*part.shape) for part in parts]
            + [block(rows, model), block(model, model), block(*vecs.shape)],
            out_specs=[block(rows, model)] * 2,
        ),
        out_shape=[shape_of((rows, model), F32), shape_of((rows, model), BF16)],
        compiler_params=params(),
        cost_estimate=cost(2 * rows * model * model, rows * model * 10 + 2 * model * model),
    )(meta, *parts, x, weights, vecs)


def feed_kernel(normed, above, up, bias, act_ref, grad_ref, back_ref):
    count, rows, model = normed.shape
    width = up.shape[1]
    value = mm(normed[...].reshape(count * rows, model), up[...]) + bias[...]
    square = value * value
    root = math.sqrt(2.0 / math.pi)
    bend = jnp.tanh(root * value * (1.0 + 0.044715 * square))
    half = 0.5 * (1.0 + bend)
    act_ref[...] = (value * half).astype(BF16).reshape(count, rows, width)
    slope = half + 0.5 * value * (1.0 - bend * bend) * (root + 3 * 0.044715 * root * square)
    grad = (above[...].reshape(count * rows, width) * slope).astype(BF16)
    grad_ref[...] = grad.reshape(count, rows, width)
    back_ref[...] = mm_rt(grad, up[...]).astype(BF16).reshape(count, rows, model)


def feed(normed, above, up, bias):
    count, rows, model = normed.shape
    width = up.shape[1]
    wide = pl.BlockSpec((2, rows, model), lambda i: (i, 0, 0))
    thin = pl.BlockSpec((2, rows, width), lambda i: (i, 0, 0))
    return pl.pallas_call(
        feed_kernel,
        name="feed",
        grid=(count // 2,),
        in_specs=[wide, thin, block(model, width), block(1, width)],
        out_specs=[thin, thin, wide],
        out_shape=[shape_of((count, rows, width), BF16)] * 2 + [shape_of((count, rows, model), BF16)],
        compiler_params=params(),
        cost_estimate=cost(
            count * rows * 4 * model * width,
            count * rows * (4 * model + 8 * width) + 2 * model * width,
            count * rows * width,
        ),
    )(normed, above, up, bias)


def both(even, odd):
    return jnp.concatenate([even[0], odd[0]], axis=0)


def down_grad_kernel(act_e, act_o, grad_e, grad_o, cot_e, cot_o, down_ref, down_sum, bias_sum):
    width = act_e.shape[2]

    @pl.when(pl.program_id(0) == 0)
    def _():
        down_sum[...] = jnp.zeros_like(down_sum)
        bias_sum[...] = jnp.zeros_like(bias_sum)

    down_sum[...] += mm_lt(both(act_e, act_o), both(cot_e, cot_o))
    bias_sum[0:1, :width] += jnp.sum(both(grad_e, grad_o).astype(F32), axis=0, keepdims=True)

    @pl.when(pl.program_id(0) == pl.num_programs(0) - 1)
    def _():
        down_ref[:width] = down_sum[...].astype(BF16)
        down_ref[width:] = bias_sum[...].astype(BF16)


def down_gradient(act, grad, cot):
    _, rows, width = act[0].shape
    model = cot[0].shape[2]
    thin = pl.BlockSpec((1, rows, width), lambda i: (i, 0, 0))
    wide = pl.BlockSpec((1, rows, model), lambda i: (i, 0, 0))
    return pl.pallas_call(
        down_grad_kernel,
        name="down_gradient",
        grid=(4,),
        in_specs=[thin] * 4 + [wide] * 2,
        out_specs=block(width + 16, model),
        scratch_shapes=[pltpu.VMEM((width, model), F32), pltpu.VMEM((16, model), F32)],
        out_shape=shape_of((width + 16, model), BF16),
        compiler_params=params(),
        cost_estimate=cost(16 * rows * model * width, 16 * rows * (model + 2 * width)),
    )(*act, *grad, *cot)


def feed_grads_kernel(act_e, act_o, grad_e, grad_o, normed_e, normed_o, down, out_e, out_o, up_ref, up_sum):
    rows = act_e.shape[1]
    out = mm(both(act_e, act_o), down[...]).astype(BF16)
    out_e[0] = out[:rows]
    out_o[0] = out[rows:]

    @pl.when(pl.program_id(0) == 0)
    def _():
        up_sum[...] = jnp.zeros_like(up_sum)

    up_sum[...] += mm_lt(both(normed_e, normed_o), both(grad_e, grad_o))

    @pl.when(pl.program_id(0) == pl.num_programs(0) - 1)
    def _():
        up_ref[...] = up_sum[...].astype(BF16)


def feed_grads(act, grad, normed, down):
    _, rows, width = act[0].shape
    model = down.shape[1]
    thin = pl.BlockSpec((1, rows, width), lambda i: (i, 0, 0))
    wide = pl.BlockSpec((1, rows, model), lambda i: (i, 0, 0))
    return pl.pallas_call(
        feed_grads_kernel,
        name="feed_grads",
        grid=(4,),
        in_specs=[thin] * 4 + [wide] * 2 + [block(width, model)],
        out_specs=[wide, wide, block(model, width)],
        scratch_shapes=[pltpu.VMEM((model, width), F32)],
        out_shape=[shape_of((4, rows, model), BF16)] * 2 + [shape_of((model, width), BF16)],
        compiler_params=params(),
        cost_estimate=cost(32 * rows * model * width, 16 * rows * (2 * model + 2 * width)),
    )(*act, *grad, *normed, down)


def middle_kernel(meta, g0, g1, gx, gy, gd, hidden, cot, weights, vecs, hidden_grad_ref, grad_ref, sums_ref, d0, d1, d2, d3):
    width = d0.shape[1]
    z = meta[meta.shape[0] - 1]
    normed_grad = (g0[0].astype(F32) + g1[0].astype(F32)) + (gx[...].astype(F32) + gy[...].astype(F32))
    normed_grad = normed_grad + gd[...].astype(F32)
    unit, inverse = normalize(hidden[...])
    upstream = cot[...].astype(F32)
    hidden_grad = upstream + norm_back(normed_grad, unit, inverse, vecs[3:4])
    hidden_grad_ref[...] = hidden_grad
    grad = hidden_grad.astype(BF16)
    grad_ref[...] = grad
    for k, out in enumerate((d0, d1, d2, d3)):
        start = pl.multiple_of((z ^ k) * width, width)
        out[...] = mm_rt(grad, weights[pl.ds(start, width), :]).astype(BF16)
    sums_ref[0:1, :] = jnp.sum(normed_grad * unit, axis=0, keepdims=True)
    sums_ref[1:2, :] = jnp.sum(normed_grad, axis=0, keepdims=True)
    sums_ref[2:3, :] = jnp.sum(grad.astype(F32), axis=0, keepdims=True)
    sums_ref[3:4, :] = jnp.sum(upstream, axis=0, keepdims=True)


def middle(meta, stacks, moved, hidden, cot, weights, vecs):
    rows, model = hidden.shape
    width = model // ZS
    return pl.pallas_call(
        middle_kernel,
        name="middle",
        grid_spec=pltpu.PrefetchScalarGridSpec(
            num_scalar_prefetch=1,
            grid=(1,),
            in_specs=[block(1, rows, model)] * 2
            + [block(rows, model)] * 5
            + [block(model, model), block(*vecs.shape)],
            out_specs=[block(rows, model)] * 2 + [block(4, model)] + [block(rows, width)] * ZS,
        ),
        out_shape=[shape_of((rows, model), F32), shape_of((rows, model), BF16), shape_of((4, model), F32)]
        + [shape_of((rows, width), BF16)] * ZS,
        compiler_params=params(),
        cost_estimate=cost(2 * rows * model * model, rows * model * 26 + 2 * model * model),
    )(meta, *stacks, *moved, hidden, cot, weights, vecs)


def finish_kernel(x, mine, near, far, hidden_grad, vecs, out):
    unit, inverse = normalize(x[...].astype(F32))
    upstream = mine[...].astype(F32) + near[...].astype(F32) + far[...].astype(F32)
    out[...] = (hidden_grad[...] + norm_back(upstream, unit, inverse, vecs[0:1])).astype(BF16)


def finish(x, mine, near, far, hidden_grad, vecs):
    rows, model = x.shape
    steps = 3 if rows % 48 == 0 else 1
    part = pl.BlockSpec((rows // steps, model), lambda i: (i, 0))
    return pl.pallas_call(
        finish_kernel,
        name="finish",
        grid=(steps,),
        in_specs=[part] * 5 + [block(*vecs.shape)],
        out_specs=part,
        out_shape=shape_of((rows, model), BF16),
        compiler_params=params(),
        cost_estimate=cost(20 * rows * model, rows * model * 12),
    )(x, mine, near, far, hidden_grad, vecs)


def place_up_kernel(seat, mine, other, out):
    width = mine.shape[2]
    side, team = seat[0] & 1, seat[1]
    for j in range(TEAM):
        own, got = mine[j ^ team].astype(F32), other[j ^ team].astype(F32)
        out[:, 2 * j * width : (2 * j + 1) * width] = jnp.where(side == 0, own, got)
        out[:, (2 * j + 1) * width : (2 * j + 2) * width] = jnp.where(side == 0, got, own)


def place_up(seat, mine, other):
    _, rows, width = mine.shape
    return pl.pallas_call(
        place_up_kernel,
        name="place_up",
        grid_spec=pltpu.PrefetchScalarGridSpec(
            num_scalar_prefetch=1,
            grid=(1,),
            in_specs=[block(*mine.shape)] * 2,
            out_specs=block(rows, 2 * TEAM * width),
        ),
        out_shape=shape_of((rows, 2 * TEAM * width), F32),
        compiler_params=params(),
        cost_estimate=cost(1, 12 * rows * TEAM * width),
    )(seat, mine, other)


def per_device(
    inputs,
    lengths,
    cotangent,
    attn_gain,
    attn_shift,
    qkv_weight,
    qv_bias,
    proj_weight,
    proj_bias,
    mlp_gain,
    mlp_shift,
    up_weight,
    up_bias,
    down_weight,
    down_bias,
):
    count, local, model = inputs.shape
    size = lax.axis_size("fsdp")
    outer = size // TEAM
    place = lax.axis_index("fsdp").astype(jnp.uint32)
    seat = lax.axis_index("seq").astype(jnp.uint32)
    z = seat.astype(jnp.int32)
    team = place & (TEAM - 1)
    core = team & 1
    chip = team >> 1
    tokens = count * local
    width = model // ZS
    own_rows = qkv_weight.shape[0]
    hidden_units = up_weight.shape[1]
    feed_width = hidden_units // TEAM
    meta = jnp.concatenate([lengths.astype(jnp.int32), z.reshape(1)])

    rows = lax.all_gather(inputs, "seq", axis=0, tiled=False)

    def over_team(own):
        quad = jnp.stack([own] + [swap(own, 2 * m) for m in (1, 2, 3)])
        return jnp.concatenate([quad, swap(quad, 1)], axis=0)

    columns = [
        lax.dynamic_slice(qkv_weight, (jnp.uint32(0), seat * width + i * model), (own_rows, width)) for i in range(3)
    ]
    vectors = (attn_gain, attn_shift, proj_bias, mlp_gain, mlp_shift, down_bias)
    lanes, spot, packed = 3 * width, 0, []
    for vector in vectors:
        packed.append(jnp.pad(vector, (spot, lanes - spot - vector.shape[0])))
        spot += vector.shape[0]
    row_one = functools.reduce(jnp.add, packed).reshape(1, lanes)
    row_two = jnp.pad(qv_bias, (0, lanes - qv_bias.shape[0])).reshape(1, lanes)
    small_rows = jnp.pad(row_one, ((0, 7), (0, 0))) + jnp.pad(row_two, ((1, 6), (0, 0)))
    piece = jnp.concatenate([jnp.concatenate(columns, axis=1), small_rows], axis=0)
    pieces = over_team(piece)
    weights = jnp.stack([pick(pieces, ((j ^ team) & 1) * 4 + ((j ^ team) >> 1)) for j in range(TEAM)])
    weights = gather_over_outer(weights, size)
    vecs = weights[:, own_rows, : 6 * own_rows].reshape(size, 6, own_rows).transpose(1, 0, 2)
    vecs = vecs.reshape(6, model).astype(F32)
    bias_qv = weights[:, own_rows + 1, : qv_bias.shape[0]].reshape(1, 2 * model).astype(F32)
    bias_quarter = jnp.concatenate(
        [
            lax.dynamic_slice(bias_qv, (jnp.uint32(0), seat * width), (1, width)),
            jnp.zeros((1, width), F32),
            lax.dynamic_slice(bias_qv, (jnp.uint32(0), model + seat * width), (1, width)),
        ],
        axis=1,
    )
    proj = lax.all_gather(proj_weight, "fsdp", axis=0, tiled=True)

    up_blocks = up_weight.reshape(own_rows, outer, TEAM, feed_width // outer).transpose(2, 0, 1, 3)
    up_blocks = up_blocks.reshape(TEAM, own_rows, feed_width)
    groups = [[o * TEAM + t for t in range(TEAM)] for o in range(outer)]
    up = lax.all_to_all(
        up_blocks, "fsdp", split_axis=0, concat_axis=0, axis_index_groups=groups, tiled=True
    ).reshape(TEAM * own_rows, feed_width)
    up = gather_over_outer(up, size)
    down = gather_over_outer(down_weight, size)
    bias_up = gather_over_outer(up_bias, size).astype(F32).reshape(1, feed_width)

    half = model // 2

    def over_chips(own):
        by_x, by_y = swap(own, 2), swap(own, 4)
        diagonal = jnp.concatenate([swap(by_x[:, :half], 4), swap(by_y[:, half:], 2)], axis=1)
        return jnp.stack([own, by_x, by_y, diagonal])

    positions = z * local + jnp.arange(local, dtype=jnp.int32)
    row_valid = (positions[None, :] < lengths[:, None])[:, :, None]
    cot = jnp.where(row_valid, cotangent, jnp.zeros_like(cotangent)).reshape(tokens, model)
    cot_even = over_chips(cot)
    cot_odd = swap(cot_even, 1)

    def down_back(stack):
        out = lax.dot_general(stack, down, (((2,), (1,)), ((), ())), preferred_element_type=F32)
        return out


    qkv, normed_attn, *context = attend(meta, after(rows, cot_odd, up), weights, vecs, bias_quarter)
    context = [context[0]] + [cross(context[k], k) for k in range(1, ZS)]
    above_even, above_odd = (down_back(after(part, qkv)) for part in (cot_even, cot_odd))
    own = inputs.reshape(tokens, model)
    context[0] = after(context[0], above_even, above_odd)
    hidden, normed = project(meta, context, own, proj, vecs)

    normed_even = over_chips(normed)
    normed_odd = swap(normed_even, 1)
    act_even, grad_even, back_even = feed(normed_even, above_even, up, bias_up)
    act_odd, grad_odd, back_odd = feed(normed_odd, above_odd, up, bias_up)
    back_core = swap(back_odd, 1)
    sums = [joined(back_even[m], back_core[m]) for m in (1, 2, 3)]
    moved = [swap(part, 2 * m) for m, part in zip((1, 2, 3), sums)]
    act_even = after(act_even, *sums)
    down_part = down_gradient((act_even, act_odd), (grad_even, grad_odd), (cot_even, cot_odd))
    out_even, out_odd, up_part = feed_grads(
        (act_even, after(act_odd, down_part)), (grad_even, grad_odd), (normed_even, normed_odd), down
    )
    if outer > 1:
        bias_part = rows_over_outer(down_part[feed_width, :feed_width].astype(F32), size)
        bias_part = jnp.pad(bias_part.reshape(1, -1), ((0, 15), (0, model - bias_part.shape[0])))
        down_part = rows_over_outer(down_part[:feed_width], size)
        down_part = jnp.concatenate([down_part, bias_part.astype(BF16)], axis=0)
    down_rows = down_weight.shape[0]
    up_part = rows_over_outer(up_part, size)
    down_total = lax.psum(down_part, "seq")
    side = seat & 1
    half_width = feed_width // 2
    up_keep, up_give = (
        lax.dynamic_slice(up_part, (jnp.uint32(0), part * half_width), (up_part.shape[0], half_width))
        for part in (side, 1 - side)
    )

    hidden_grad, attn_grad, mid_sums, *context_grad = middle(
        meta, (back_even, back_core), moved, after(hidden, out_even), cot, proj, vecs
    )

    def over_core(part, *others):
        keep, give = pick(part, core, 1), pick(part, 1 - core, 1)
        return joined(after(keep, *others), swap(give, 1))

    def over_team_chips(both, at, *others):
        total = after(pick(both, at(0)), *others).astype(F32)
        for m in (1, 2, 3):
            total = total + swap(pick(both, at(m)), 2 * m).astype(F32)
        return total.astype(BF16)

    proj_part = mm_lt(jnp.concatenate(context, axis=1), attn_grad)
    if outer == 1:
        proj_part = proj_part.astype(BF16).reshape(ZS, 2, own_rows, model)
        mid_rows = mid_sums.reshape(4, TEAM, own_rows).transpose(1, 0, 2).reshape(4, 2, 1, 4 * own_rows)
        mid_rows = jnp.pad(mid_rows, ((0, 0), (0, 0), (0, 7), (0, model - 4 * own_rows))).astype(BF16)
        mid_rows = jnp.stack([pick(mid_rows, seat ^ k) for k in range(ZS)])
        proj_part = jnp.concatenate([proj_part, mid_rows], axis=2)
        chip_at = lambda m: chip ^ m ^ seat
    else:
        proj_part = proj_part.reshape(ZS, width, model)
        proj_part = jnp.stack([pick(proj_part, seat ^ j) for j in range(ZS)]).reshape(model, model)
        proj_part = rows_over_outer(proj_part, size).astype(BF16).reshape(4, 2, own_rows, model)
        chip_at = lambda m: chip ^ m

    context_grad = [context_grad[0]] + [cross(context_grad[k], k) for k in range(1, ZS)]
    up_half = joined(after(up_keep, *context_grad), cross(up_give, 1))
    up_across = cross(up_half, 2)
    qkv_grad, attn_sums, *parts = attend_back(meta, rows, context_grad, after(qkv, up_half), weights)

    qkv_part = mm_lt(normed_attn.reshape(-1, model), qkv_grad.reshape(-1, 3 * width)).astype(BF16)

    if outer == 1:
        qkv_part = qkv_part.reshape(4, 2, own_rows, 3 * width)
        gains = attn_sums[:2].reshape(2, TEAM, own_rows).transpose(1, 0, 2).reshape(4, 2, 1, 2 * own_rows)
        biases = jnp.concatenate([attn_sums[2, :width], attn_sums[2, 2 * width : 3 * width]])
        biases = jnp.broadcast_to(biases, (4, 2, 1, 2 * width))
        packed = jnp.concatenate([gains, biases], axis=3)
        packed = jnp.pad(packed, ((0, 0), (0, 0), (0, 7), (0, 3 * width - packed.shape[3]))).astype(BF16)
        qkv_part = jnp.concatenate([qkv_part, packed], axis=2)
    else:
        qkv_part = rows_over_outer(qkv_part, size).reshape(4, 2, own_rows, 3 * width)

    near = [cross(parts[k], 1) for k in (1, 3)]
    qkv_both = over_core(qkv_part)
    down_grad = down_total[:down_rows].astype(F32)
    proj_both = over_core(proj_part, qkv_both, down_grad)
    middle_sum = joined(after(parts[2], proj_both), near[1])
    far = cross(middle_sum, 2)
    up_sum = lax.optimization_barrier(joined(after(up_half, middle_sum), up_across))
    up_sum = up_sum.reshape(4, 2, own_rows, half_width)
    pair = jnp.stack([pick(up_sum, core, 1), swap(pick(up_sum, 1 - core, 1), 1)], axis=1)
    up_moved = [swap(pick(pair, chip ^ m), 2 * m) for m in (1, 2, 3)]
    out_core = swap(after(out_odd, qkv_grad), 1)
    out_sums = [joined(after(out_even[m], up_sum), out_core[m]) for m in (1, 2, 3)]
    out_moved = [swap(part, 2 * m) for m, part in zip((1, 2, 3), out_sums)]
    input_grad = finish(own, parts[0], near[0], far, after(hidden_grad, pair, down_grad, *out_sums), vecs)
    qkv_mine = lax.optimization_barrier(over_team_chips(qkv_both, lambda m: chip ^ m, up_sum))
    proj_mine = over_team_chips(proj_both, chip_at, up_sum)
    lanes = qkv_mine.shape[1]
    packed = jnp.concatenate([after(qkv_mine, far), proj_mine], axis=1)
    packed_two = cross(packed, 2)
    up_rel = jnp.stack([after(pick(pair, chip), packed)] + up_moved)
    up_rel = lax.optimization_barrier(up_rel.reshape(TEAM, own_rows, half_width))
    up_other = cross(up_rel, 1)
    packed_two = after(packed_two, up_rel, input_grad)
    qkv_two = packed_two[:, :lanes]
    proj_two = lax.optimization_barrier(joined(proj_mine, packed_two[:, lanes:]))
    packed_one = cross(jnp.concatenate([qkv_mine, qkv_two, proj_two], axis=1), 1)
    qkv_near = [packed_one[:, :lanes], packed_one[:, lanes : 2 * lanes]]
    proj_total = joined(proj_two, packed_one[:, 2 * lanes :]).astype(F32)
    input_grad = input_grad.reshape(inputs.shape)

    output = after(hidden, qkv_two) + vecs[5:6] + out_even[0].astype(F32) + out_core[0].astype(F32)
    for part in out_moved:
        output = output + part.astype(F32)
    output = jnp.where(row_valid, output.reshape(inputs.shape), 0.0).astype(BF16)

    up_bias_grad = down_total[down_rows, : up_bias.shape[0]].astype(F32)
    seats = jnp.stack([seat, team]).astype(jnp.int32)
    if outer == 1:
        up_grad = place_up(seats, up_rel, up_other)
    else:
        up_first = jnp.where(side == 0, up_rel, up_other)
        up_second = jnp.where(side == 0, up_other, up_rel)
        up_rel = jnp.concatenate([up_first, up_second], axis=2)
        up_grad = jnp.stack([pick(up_rel, j ^ team) for j in range(TEAM)], axis=1).astype(F32)
        up_grad = up_grad.reshape(own_rows, TEAM, outer, feed_width // outer).transpose(0, 2, 1, 3)
        up_grad = up_grad.reshape(own_rows, hidden_units)
    proj_grad = proj_total[:own_rows]
    qkv_parts = jnp.stack([qkv_mine, qkv_near[0], qkv_two, qkv_near[1]])
    ordered = [pick(qkv_parts, seat ^ j).astype(F32) for j in range(ZS)]
    qkv_weight_grad = jnp.concatenate(
        [part[:own_rows, i * width : (i + 1) * width] for i in range(3) for part in ordered], axis=1
    )

    if outer == 1:
        mid = proj_total[own_rows, : 4 * own_rows].reshape(4, own_rows)
        packed = jnp.stack([part[own_rows] for part in ordered])
        gains = packed[:, : 2 * own_rows]
        gains = (gains[0] + gains[1]) + (gains[2] + gains[3])
        attn_gain_grad, attn_shift_grad = gains[:own_rows], gains[own_rows:]
        mine = pick(packed, place & (ZS - 1))
        start = 2 * own_rows + (place >> 2) * width
        qv_bias_grad = lax.dynamic_slice(mine, (start,), (width,))
        mlp_gain_grad, mlp_shift_grad, proj_bias_grad, down_bias_grad = mid
    else:
        biases = jnp.zeros((2, ZS, width), F32)
        biases = lax.dynamic_update_slice(
            biases, jnp.stack([attn_sums[2, :width], attn_sums[2, 2 * width : 3 * width]])[:, None], (0, z, 0)
        )
        packed = jnp.concatenate([attn_sums[0], attn_sums[1], mid_sums.reshape(-1)]).reshape(6, size, own_rows)
        packed = jnp.concatenate([packed.transpose(1, 0, 2).reshape(size, -1), biases.reshape(size, -1)], axis=1)
        packed = lax.psum_scatter(packed, "fsdp", scatter_dimension=0, tiled=False)
        packed = lax.psum(packed, "seq")
        vectors = packed[: 6 * own_rows].reshape(6, own_rows)
        attn_gain_grad, attn_shift_grad, mlp_gain_grad, mlp_shift_grad, proj_bias_grad, down_bias_grad = vectors
        qv_bias_grad = packed[6 * own_rows :]

    return (
        output,
        input_grad,
        attn_gain_grad,
        attn_shift_grad,
        qkv_weight_grad,
        qv_bias_grad,
        proj_grad,
        proj_bias_grad,
        mlp_gain_grad,
        mlp_shift_grad,
        up_grad,
        up_bias_grad,
        down_grad,
        down_bias_grad,
    )


def solution(mesh):
    split = P("fsdp")
    tokens = P("fsdp", "seq", None)
    matrix = P("fsdp", None)
    in_specs = (tokens, split, tokens, split, split, matrix, split, matrix) + (split,) * 3 + (matrix, split, matrix, split)
    out_specs = (tokens, tokens, split, split, matrix, split, matrix) + (split,) * 3 + (matrix, split, matrix, split)
    return jax.shard_map(per_device, mesh=mesh, in_specs=in_specs, out_specs=out_specs, check_vma=False)
```
